256 devices in a mesh: vid: 128 (over z, y, x_lo, core), aud: 2 (over x_hi).
Axes of the slice: x: 4 (x_hi: 2, x_lo: 2; x = x_hi * 2 + x_lo), y: 4, z: 8, core: 2. Of those that a mesh axis runs over, the one named last changes fastest.
Arguments:
- q_video: bfloat16 [32768, 1536], P('vid', 'aud'), may hold values from -240 to 240
- video_key_rows: bfloat16 [32768, 1536], P('vid', 'aud'), may hold values from -6 to 6
- video_value_rows: bfloat16 [32768, 1536], P('vid', 'aud'), may hold values from -6 to 6
- g_video: bfloat16 [32768, 1536], P('vid', 'aud'), may hold values from -6 to 6
- q_audio: bfloat16 [8192, 1536], P(('vid', 'aud')), may hold values from -240 to 240
- k_audio: bfloat16 [8192, 1536], P(('vid', 'aud')), may hold values from -6 to 6
- v_audio: bfloat16 [8192, 1536], P(('vid', 'aud')), may hold values from -6 to 6
- g_audio: bfloat16 [8192, 1536], P(('vid', 'aud')), may hold values from -6 to 6
- window: int32 [512, 2], replicated, may hold values from 0 to 127, as said below
- audio_len: int32 [128], replicated, may hold values from 1 to 64
Outputs:
- out_video: bfloat16 [32768, 1536], P('vid', 'aud')
- out_audio: bfloat16 [8192, 1536], P(('vid', 'aud'))
- dq_video: bfloat16 [32768, 1536], P('vid', 'aud')
- dk_video: bfloat16 [32768, 1536], P('vid', 'aud')
- dv_video: bfloat16 [32768, 1536], P('vid', 'aud')
- dq_audio: bfloat16 [8192, 1536], P(('vid', 'aud'))
- dk_audio: bfloat16 [8192, 1536], P(('vid', 'aud'))
- dv_audio: bfloat16 [8192, 1536], P(('vid', 'aud'))
The draws below stay inside these ranges and needn't reach their ends.
Inputs may be any that keep to these rules, and one draw needn't show every extreme that they name: window[i] = (start, count) with 1 <= count <= 3 (3 is reached in every draw), start <= i // 4 < start + count, and start + count <= 128.
All inputs are finite; a program needn't handle non-finite values.
Results may differ from the reference program's by a relative error of at most 0.0095.
Values may be sent and summed in bfloat16 or wider, within the bound.
No kernel may reach another device: no remote copies, remote signals or barrier semaphores. Data moves between devices by JAX's collectives and lax.ppermute only.
A program may use at most 64 MiB of HBM per device.

```python
import jax
import jax.numpy as jnp
from jax import lax

HD = 64
D = 1536
BLK = 64
WMAX = 3
ABLK = 128
VBLK = 512
ATOK = 8192
VTOK = 32768


def normal_block(key, tag, height, width):
    drawn = jax.random.normal(jax.random.fold_in(key, tag), (height, width), jnp.float32)
    return jnp.clip(drawn, -6.0, 6.0)


def draw_video_key_rows(key, part):
    return normal_block(key, 11, VTOK, D).astype(jnp.bfloat16)


def draw_k_audio(key, part):
    return normal_block(key, 12, ATOK, D).astype(jnp.bfloat16)


def draw_q_video(key, part):
    drawn = normal_block(key, 13, VTOK, D)
    return drawn.astype(jnp.bfloat16)


def draw_q_audio(key, part):
    drawn = normal_block(key, 15, ATOK, D)
    return drawn.astype(jnp.bfloat16)


def draw_window(key, part):
    block_ids = jnp.arange(VBLK)
    number = jax.random.randint(jax.random.fold_in(key, 21), (VBLK,), 1, WMAX + 1)
    number = jnp.where(block_ids % 16 == 3, WMAX, number)
    window_shift = jax.random.randint(jax.random.fold_in(key, 22), (VBLK,), 0, WMAX) % number
    first = jnp.clip(block_ids // 4 - window_shift, 0, ABLK - number)
    return jnp.stack([first, number], axis=1).astype(jnp.int32)


def draw_audio_len(key, part):
    lengths = jax.random.randint(jax.random.fold_in(key, 23), (ABLK,), 1, BLK + 1)
    lengths = jnp.where(jnp.arange(ABLK) % 8 == 0, BLK, lengths)
    return lengths.astype(jnp.int32)


def level_of(own_key, shape, cuts, smallest, largest):
    def one(position, shards_of):
        heights = jax.random.uniform(jax.random.fold_in(jax.random.fold_in(own_key, 6), position), (shards_of,), jnp.float32, smallest / len(cuts), largest / len(cuts))
        return jnp.repeat(jnp.exp(heights), shape[position] // shards_of).reshape((-1,) + (1,) * (len(shape) - position - 1))

    loudness = one(*cuts[0])
    for cut in cuts[1:]:
        loudness = loudness * one(*cut)
    return loudness


def normal_values(key, dims, scale, reach, split=(), held_as=jnp.bfloat16):
    values = scale * jax.random.normal(key, dims, jnp.float32)
    if split:
        values = values * level_of(key, dims, split, -0.22, 0.18)
    return jnp.clip(values, -reach, reach).astype(held_as)


def setup_inputs(seed: int = 0) -> dict:
    splits = jax.random.split(jax.random.key(seed), 11)
    return {
        "q_video": draw_q_video(jax.random.fold_in(splits[10], 71), 0),
        "video_key_rows": draw_video_key_rows(jax.random.fold_in(splits[10], 71), 0),
        "video_value_rows": normal_values(splits[2], (VTOK, D), 1.0, 6.0, ((0, 128), (1, 2))),
        "g_video": normal_values(splits[3], (VTOK, D), 1.0, 6.0, ((0, 128), (1, 2))),
        "q_audio": draw_q_audio(jax.random.fold_in(splits[10], 71), 0),
        "k_audio": draw_k_audio(jax.random.fold_in(splits[10], 71), 0),
        "v_audio": normal_values(splits[6], (ATOK, D), 1.0, 6.0, ((0, 256),)),
        "g_audio": normal_values(splits[7], (ATOK, D), 1.0, 6.0, ((0, 256),)),
        "window": draw_window(jax.random.fold_in(splits[10], 71), 0),
        "audio_len": draw_audio_len(jax.random.fold_in(splits[10], 71), 0),
    }


NEG_FILL = -1.0e30


def split_heads(matrix):
    return matrix.astype(jnp.float32).reshape(matrix.shape[0], matrix.shape[1] // HD, HD)


def flatten_heads(tensor):
    return tensor.reshape(tensor.shape[0], -1)


def pair_block(queries, key_rows, value_rows, cotangent, allowed, query_valid):
    scale = HD ** -0.5
    q_heads = split_heads(queries)
    k_heads = split_heads(key_rows)
    v_heads = split_heads(value_rows)
    g_heads = split_heads(cotangent) * query_valid[:, None, None]
    scores = jnp.einsum("rhd,khd->hrk", q_heads, k_heads) * scale
    scores = jnp.where(allowed[None], scores, NEG_FILL)
    row_max = jnp.max(scores, axis=2, keepdims=True)
    row_sum = jnp.sum(jnp.where(allowed[None], jnp.exp(scores - row_max), 0.0), axis=2, keepdims=True)
    attention_probs = jnp.where(allowed[None], jnp.exp(scores - (row_max + jnp.log(row_sum))), 0.0)
    weights_b = lax.optimization_barrier(attention_probs.astype(jnp.bfloat16)).astype(jnp.float32)
    mixed = jnp.einsum("hrk,khd->rhd", weights_b, v_heads) * query_valid[:, None, None]
    out_rows = flatten_heads(mixed).astype(jnp.bfloat16)
    deltas = jnp.sum(g_heads * split_heads(out_rows), axis=2)
    grad_p = jnp.einsum("rhd,khd->hrk", g_heads, v_heads)
    grad_s = (attention_probs * (grad_p - deltas.T[:, :, None])).astype(jnp.bfloat16)
    grad_s = lax.optimization_barrier(grad_s).astype(jnp.float32)
    grad_q = jnp.einsum("hrk,khd->rhd", grad_s, k_heads) * scale
    grad_k = jnp.einsum("hrk,rhd->khd", grad_s, q_heads) * scale
    grad_v = jnp.einsum("hrk,rhd->khd", weights_b, g_heads)
    return out_rows, flatten_heads(grad_q), flatten_heads(grad_k), flatten_heads(grad_v)


def add_rows(accum, piece, start):
    current = lax.dynamic_slice_in_dim(accum, start, piece.shape[0], 0)
    return lax.dynamic_update_slice_in_dim(accum, current + piece, start, 0)


def reference(q_video, video_key_rows, video_value_rows, g_video, q_audio, k_audio, v_audio, g_audio, window, audio_len):
    audio_count = audio_len.shape[0]
    video_count = window.shape[0]
    width = q_video.shape[1]
    span = 2 * WMAX - 1
    group = 4 * BLK
    pad_audio = (WMAX - 1) * BLK
    pad_video = (WMAX - 1) * group
    starts = window[:, 0]
    counts = window[:, 1]
    k_audio_pad = jnp.pad(k_audio, ((pad_audio, pad_audio), (0, 0)))
    v_audio_pad = jnp.pad(v_audio, ((pad_audio, pad_audio), (0, 0)))
    k_video_pad = jnp.pad(video_key_rows, ((pad_video, pad_video), (0, 0)))
    v_video_pad = jnp.pad(video_value_rows, ((pad_video, pad_video), (0, 0)))
    token_pos = jnp.arange(span * BLK) % BLK

    def video_step(carry, index):
        grad_k_acc, grad_v_acc = carry
        queries = lax.dynamic_slice_in_dim(q_video, index * group, group, 0)
        cotangent = lax.dynamic_slice_in_dim(g_video, index * group, group, 0)
        key_rows = lax.dynamic_slice_in_dim(k_audio_pad, index * BLK, span * BLK, 0)
        value_rows = lax.dynamic_slice_in_dim(v_audio_pad, index * BLK, span * BLK, 0)
        first = lax.dynamic_slice_in_dim(starts, index * 4, 4, 0)
        number = lax.dynamic_slice_in_dim(counts, index * 4, 4, 0)
        audio_ids = index - (WMAX - 1) + jnp.arange(span)
        block_ok = (audio_ids[None] >= first[:, None]) & (audio_ids[None] < first[:, None] + number[:, None])
        lengths = jnp.take(audio_len, jnp.clip(audio_ids, 0, audio_count - 1))
        key_ok = token_pos < jnp.repeat(lengths, BLK)
        allowed = jnp.repeat(jnp.repeat(block_ok, BLK, 0), BLK, 1) & key_ok[None]
        out_rows, grad_q, grad_k, grad_v = pair_block(queries, key_rows, value_rows, cotangent, allowed, jnp.ones((group,), jnp.float32))
        grad_k_acc = add_rows(grad_k_acc, grad_k, index * BLK)
        grad_v_acc = add_rows(grad_v_acc, grad_v, index * BLK)
        return (grad_k_acc, grad_v_acc), (out_rows, grad_q.astype(jnp.bfloat16))

    def audio_step(carry, index):
        grad_k_acc, grad_v_acc = carry
        queries = lax.dynamic_slice_in_dim(q_audio, index * BLK, BLK, 0)
        cotangent = lax.dynamic_slice_in_dim(g_audio, index * BLK, BLK, 0)
        key_rows = lax.dynamic_slice_in_dim(k_video_pad, index * group, span * group, 0)
        value_rows = lax.dynamic_slice_in_dim(v_video_pad, index * group, span * group, 0)
        video_ids = 4 * (index - (WMAX - 1)) + jnp.arange(4 * span)
        inside = (video_ids >= 0) & (video_ids < video_count)
        clipped = jnp.clip(video_ids, 0, video_count - 1)
        first = jnp.take(starts, clipped)
        number = jnp.take(counts, clipped)
        block_ok = inside & (index >= first) & (index < first + number)
        allowed = jnp.broadcast_to(jnp.repeat(block_ok, BLK)[None], (BLK, span * group))
        query_valid = (jnp.arange(BLK) < audio_len[index]).astype(jnp.float32)
        out_rows, grad_q, grad_k, grad_v = pair_block(queries, key_rows, value_rows, cotangent, allowed, query_valid)
        grad_k_acc = add_rows(grad_k_acc, grad_k, index * group)
        grad_v_acc = add_rows(grad_v_acc, grad_v, index * group)
        return (grad_k_acc, grad_v_acc), (out_rows, grad_q.astype(jnp.bfloat16))

    audio_zero = jnp.zeros((audio_count * BLK + 2 * pad_audio, width), jnp.float32)
    (dk_a, dv_a), (out_v, dq_v) = lax.scan(video_step, (audio_zero, audio_zero), jnp.arange(audio_count, dtype=jnp.int32))
    video_zero = jnp.zeros((video_count * BLK + 2 * pad_video, width), jnp.float32)
    (dk_v, dv_v), (out_a, dq_a) = lax.scan(audio_step, (video_zero, video_zero), jnp.arange(audio_count, dtype=jnp.int32))
    audio_tokens = audio_count * BLK
    video_tokens = video_count * BLK
    out_video = out_v.reshape(video_tokens, width)
    dq_video = dq_v.reshape(video_tokens, width)
    out_audio = out_a.reshape(audio_tokens, width)
    dq_audio = dq_a.reshape(audio_tokens, width)
    dk_audio = dk_a[pad_audio:pad_audio + audio_tokens].astype(jnp.bfloat16)
    dv_audio = dv_a[pad_audio:pad_audio + audio_tokens].astype(jnp.bfloat16)
    dk_video = dk_v[pad_video:pad_video + video_tokens].astype(jnp.bfloat16)
    dv_video = dv_v[pad_video:pad_video + video_tokens].astype(jnp.bfloat16)
    return (out_video, out_audio, dq_video, dk_video, dv_video, dq_audio, dk_audio, dv_audio)
```

```python
import jax
import jax.numpy as jnp
from jax import lax
from jax.experimental import pallas as pl
from jax.experimental.pallas import tpu as pltpu
from jax.sharding import PartitionSpec as P

HD = 64
BLK = 64
WMAX = 3
PAIR = 2 * HD
NEG = -1e30
BF = jnp.bfloat16
F32 = jnp.float32

NPOS = 6
KEYS = NPOS * BLK


def nt(x, y):
    return lax.dot_general(x, y, (((1,), (1,)), ((), ())), preferred_element_type=F32)


def nn(x, y):
    return lax.dot_general(x, y, (((1,), (0,)), ((), ())), preferred_element_type=F32)


def coords(idx_ref):
    idx = idx_ref[0]
    return idx >> 2, (idx >> 1) & 1, idx & 1


def head_part(x, e):
    lane = lax.broadcasted_iota(jnp.int32, x.shape, 1)
    return jnp.where((lane < HD) if e == 0 else (lane >= HD), x, jnp.zeros_like(x))


def pack_kernel(idx_ref, len_ref, *refs):
    mine, other, keep, send = refs[:4], refs[4:8], refs[8], refs[9]
    c, r, a = coords(idx_ref)
    half, quarter = keep.shape[2], keep.shape[3]
    row = lax.broadcasted_iota(jnp.int32, (half, quarter), 0) + a * half
    for slot, arrays in ((r, mine), (1 - r, other)):
        valid = row < len_ref[2 * c + slot]
        for n, ref in enumerate(arrays):
            for part, out in ((a, keep), (1 - a, send)):
                col = pl.multiple_of((2 * part + r) * quarter, 128)
                x = ref[:, pl.ds(col, quarter)]
                if n == 0:
                    x = x * jnp.asarray(HD**-0.5, BF)
                if n == 1:
                    x = jnp.where(valid, x, jnp.zeros_like(x))
                out[n, slot] = x


def piece_rows(idx_ref):
    c, _, a = coords(idx_ref)
    half = BLK // 2
    side = 2 - 2 * (c & 1)
    starts = []
    for place, part in ((1, a), (1, 1 - a), (side, a), (side, 1 - a), (2 - side, a), (2 - side, 1 - a)):
        first = place * 2 * BLK + part * half
        starts.append([pl.multiple_of(first + core * BLK, half) for core in range(2)])
    return starts


def gather_audio(idx_ref, pieces, dst):
    half = BLK // 2
    for ref, firsts in zip(pieces, piece_rows(idx_ref)):
        for core, first in enumerate(firsts):
            for n in range(2):
                dst[n, pl.ds(first, half), :] = ref[n, core]


def scatter_audio(idx_ref, src, pieces):
    half = BLK // 2
    for ref, firsts in zip(pieces, piece_rows(idx_ref)):
        for core, first in enumerate(firsts):
            for n in range(2):
                ref[n, core] = src[n, pl.ds(first, half), :].astype(ref.dtype)


def window_bounds(win_ref, c, stretch, shape, axis):
    block = lax.broadcasted_iota(jnp.int32, shape, axis) // BLK
    lo = jnp.zeros(shape, jnp.int32)
    hi = jnp.zeros(shape, jnp.int32)
    for b in range(4):
        start = win_ref[4 * stretch + b, 0] - (2 * c - 2)
        count = win_ref[4 * stretch + b, 1]
        lo = jnp.where(block == b, start, lo)
        hi = jnp.where(block == b, start + count, hi)
    return lo, hi


def av_bias(idx_ref, win_ref, bias):
    c, r, _ = coords(idx_ref)
    for i, stretch in enumerate((r, 1 - r)):
        shape = bias.shape[1:]
        lo, hi = window_bounds(win_ref, c, stretch, shape, 0)
        place = lax.broadcasted_iota(jnp.int32, shape, 1) // BLK
        bias[i] = jnp.where((place >= lo) & (place < hi), 0.0, NEG)


def va_bias(idx_ref, win_ref, len_ref, bias):
    c, r, _ = coords(idx_ref)
    shape = bias.shape[1:]
    row = lax.broadcasted_iota(jnp.int32, shape, 0)
    place = row // BLK
    length = jnp.zeros(shape, jnp.int32)
    for j in range(NPOS):
        block = jnp.clip(2 * c - 2 + j, 0, len_ref.shape[0] - 1)
        length = jnp.where(place == j, len_ref[block], length)
    valid = (row % BLK) < length
    for i, stretch in enumerate((r, 1 - r)):
        lo, hi = window_bounds(win_ref, c, stretch, shape, 1)
        bias[i] = jnp.where((place >= lo) & (place < hi) & valid, 0.0, NEG)


def stats_kernel(idx_ref, win_ref, *refs):
    pieces = refs[:6]
    video = ((refs[6], refs[7]), (refs[8], refs[9]))
    stat_ref, audio, bias = refs[10:]

    @pl.when(pl.program_id(0) == 0)
    def _():
        av_bias(idx_ref, win_ref, bias)

    gather_audio(idx_ref, pieces, audio)
    queries, cot = audio[0], audio[1]
    lses, deltas = [], []
    for e in range(2):
        parts = []
        for i, (k_ref, v_ref) in enumerate(video):
            s = nt(head_part(k_ref[...], e), queries) + bias[i]
            m = jnp.max(s, axis=0, keepdims=True)
            ex = jnp.exp(s - m)
            dp = nt(head_part(v_ref[...], e), cot)
            parts.append((m, jnp.sum(ex, axis=0, keepdims=True), jnp.sum(ex * dp, axis=0, keepdims=True)))
        m = jnp.maximum(parts[0][0], parts[1][0])
        w0, w1 = jnp.exp(parts[0][0] - m), jnp.exp(parts[1][0] - m)
        total = parts[0][1] * w0 + parts[1][1] * w1
        lses.append(m + jnp.log(total))
        deltas.append((parts[0][2] * w0 + parts[1][2] * w1) / total)
    stat_ref[0] = jnp.concatenate(lses + deltas + lses + deltas, axis=0)


def merge_stats(idx_ref, chips, own, by_a, by_b, before2, after2):
    c, _, _ = coords(idx_ref)
    even = (c & 1) == 0
    before = jnp.where(even, by_b, by_a)
    after = jnp.where(even, by_a, by_b)
    w = 2 * BLK

    def part(x, k, there):
        x = x[:, k * w : (k + 1) * w]
        return jnp.where(there, x[0:2], NEG), x[2:4]

    one, two = c >= 1, c >= 2
    nxt, nxt2 = c + 1 < chips, c + 2 < chips
    always = c >= 0
    groups = (
        (part(own, 0, always), part(before, 1, one), part(before2, 2, two)),
        (part(own, 1, always), part(before, 2, one), part(after, 0, nxt)),
        (part(own, 2, always), part(after, 1, nxt), part(after2, 0, nxt2)),
    )
    lses, deltas = [], []
    for group in groups:
        m = jnp.maximum(jnp.maximum(group[0][0], group[1][0]), group[2][0])
        ws = [jnp.exp(lse - m) for lse, _ in group]
        total = ws[0] + ws[1] + ws[2]
        lses.append(m + jnp.log(total))
        deltas.append(sum(wt * d for wt, (_, d) in zip(ws, group)) / total)
    return jnp.concatenate(lses, axis=1), jnp.concatenate(deltas, axis=1)


def va_kernel(idx_ref, win_ref, len_ref, *refs):
    pieces = refs[:6]
    video = ((refs[6], refs[7]), (refs[8], refs[9]))
    outs = ((refs[10], refs[11]), (refs[12], refs[13]))
    back = refs[14:20]
    audio, bias, grads = refs[20:]

    @pl.when(pl.program_id(0) == 0)
    def _():
        va_bias(idx_ref, win_ref, len_ref, bias)

    gather_audio(idx_ref, pieces, audio)
    keys, values = audio[0], audio[1]
    keys_t, values_t = keys.T, values.T
    k_heads = [head_part(keys, e) for e in range(2)]
    v_heads = [head_part(values, e) for e in range(2)]
    dk, dv = None, None
    for i, ((q_ref, g_ref), (out_ref, dq_ref)) in enumerate(zip(video, outs)):
        q = q_ref[...] * jnp.asarray(HD**-0.5, BF)
        g = g_ref[...]
        out_t, dq_t = [], []
        for e in range(2):
            s = nt(k_heads[e], q) + bias[i]
            m = jnp.max(s, axis=0, keepdims=True)
            ex = jnp.exp(s - m)
            p = ex * (1.0 / jnp.sum(ex, axis=0, keepdims=True))
            pb = p.astype(BF)
            dp = nt(v_heads[e], g)
            delta = jnp.sum(p * dp, axis=0, keepdims=True)
            ds = (p * (dp - delta)).astype(BF)
            dk_e, dv_e = nn(ds, head_part(q, e)), nn(pb, head_part(g, e))
            dk = dk_e if dk is None else dk + dk_e
            dv = dv_e if dv is None else dv + dv_e
            out_t.append(nn(values_t[e * HD : (e + 1) * HD], pb))
            dq_t.append(nn(keys_t[e * HD : (e + 1) * HD], ds))
        out_ref[...] = jnp.concatenate(out_t, axis=0).T.astype(BF)
        dq_ref[...] = (jnp.concatenate(dq_t, axis=0).T * HD**-0.5).astype(BF)
    grads[0] = dk
    grads[1] = dv
    scatter_audio(idx_ref, grads, back)


def av_kernel(chips, idx_ref, win_ref, *refs):
    pieces = refs[:6]
    video = ((refs[6], refs[7]), (refs[8], refs[9]))
    stats = [ref[0] for ref in refs[10:15]]
    outs = ((refs[21], refs[22]), (refs[23], refs[24]))
    back = refs[25:31]
    audio, bias, grads = refs[31:]

    @pl.when(pl.program_id(0) == 0)
    def _():
        av_bias(idx_ref, win_ref, bias)

    gather_audio(idx_ref, pieces, audio)
    queries, cot = audio[0], audio[1]
    q_heads = [head_part(queries, e) for e in range(2)]
    g_heads = [head_part(cot, e) for e in range(2)]
    lse, delta = merge_stats(idx_ref, chips, *stats)
    dq_t, out_t = [None, None], [None, None]
    for i, ((k_ref, v_ref), (dk_ref, dv_ref)) in enumerate(zip(video, outs)):
        keys, values = k_ref[...], v_ref[...]
        keys_t, values_t = keys.T, values.T
        dk, dv = None, None
        for e in range(2):
            s = nt(head_part(keys, e), queries) + bias[i]
            p = jnp.exp(s - lse[e : e + 1])
            pb = p.astype(BF)
            dp = nt(head_part(values, e), cot)
            ds = (p * (dp - delta[e : e + 1])).astype(BF)
            dk_e, dv_e = nn(ds, q_heads[e]), nn(pb, g_heads[e])
            dk = dk_e if dk is None else dk + dk_e
            dv = dv_e if dv is None else dv + dv_e
            dq_e = nn(keys_t[e * HD : (e + 1) * HD], ds)
            out_e = nn(values_t[e * HD : (e + 1) * HD], pb)
            dq_t[e] = dq_e if i == 0 else dq_t[e] + dq_e
            out_t[e] = out_e if i == 0 else out_t[e] + out_e
        dk_ref[...] = dk.astype(BF)
        dv_ref[...] = dv.astype(BF)
    grads[0] = jnp.concatenate(dq_t, axis=0).T * HD**-0.5
    grads[1] = jnp.concatenate(out_t, axis=0).T
    scatter_audio(idx_ref, grads, back)


def sum_kernel(idx_ref, len_ref, keep, by_aud, by_a, by_ax, by_b, by_bx, mine, other):
    c, r, a = coords(idx_ref)
    half, quarter = keep.shape[2], keep.shape[3]
    row = lax.broadcasted_iota(jnp.int32, (half, quarter), 0) + a * half
    for slot, out in ((r, mine), (1 - r, other)):
        valid = row < len_ref[2 * c + slot]
        for part, parts in ((a, (keep, by_a, by_b)), (1 - a, (by_aud, by_ax, by_bx))):
            for n in range(4):
                x = sum(ref[n, slot].astype(F32) for ref in parts)
                if n == 3:
                    x = jnp.where(valid, x, 0.0)
                out[n, part] = x.astype(BF)


def join_audio_kernel(idx_ref, mine, other, *outs):
    _, r, _ = coords(idx_ref)
    quarter = mine.shape[3]
    for n, out in enumerate(outs):
        for part in range(2):
            for core, ref in ((r, mine), (1 - r, other)):
                col = pl.multiple_of((2 * part + core) * quarter, 128)
                out[:, pl.ds(col, quarter)] = ref[n, part]


def join_video_kernel(idx_ref, *refs):
    for src, out in zip(refs[4:8], refs[8:12]):
        out[...] = src[...]


def cost(flops, transcendentals, nbytes):
    return pl.CostEstimate(flops=flops, transcendentals=transcendentals, bytes_accessed=nbytes)


def make_body(mesh):
    nv = mesh.shape["vid"]
    chips = nv // 2
    everyone = [(v, a) for v in range(nv) for a in range(2)]

    def perm(move):
        pairs = []
        for v, a in everyone:
            w, b = move(v, a)
            if 0 <= w < nv:
                pairs.append((2 * v + a, 2 * w + b))
        return pairs

    def diagonal(v):
        return 2 * ((((v >> 1) + 1) ^ 1) - 1) + (v & 1)

    moves = {
        "core": perm(lambda v, a: (v ^ 1, a)),
        "aud": perm(lambda v, a: (v, 1 - a)),
        "A": perm(lambda v, a: (v ^ 2, a)),
        "Ax": perm(lambda v, a: (v ^ 2, 1 - a)),
        "B": perm(lambda v, a: (diagonal(v), a)),
        "Bx": perm(lambda v, a: (diagonal(v), 1 - a)),
        "p2": perm(lambda v, a: (v + 4, a)),
        "m2": perm(lambda v, a: (v - 4, a)),
    }

    def move(x, name):
        return lax.ppermute(x, ("vid", "aud"), moves[name])

    def body(q_v, k_v, v_v, g_v, q_a, k_a, v_a, g_a, window, audio_len):
        rows, width = q_v.shape
        quarter = width // 2
        half = q_a.shape[0]
        steps = quarter // PAIR
        idx = jnp.reshape(2 * lax.axis_index("vid") + lax.axis_index("aud"), (1,)).astype(jnp.int32)
        shape = jax.ShapeDtypeStruct

        smem = pl.BlockSpec(memory_space=pltpu.SMEM)
        win_spec = pl.BlockSpec((8, 2), lambda h, i: (i[0] >> 2, 0), memory_space=pltpu.SMEM)
        len_spec = pl.BlockSpec(memory_space=pltpu.SMEM)

        def piece_spec(n):
            return pl.BlockSpec((2, 2, half, PAIR), lambda h, i: (n, 0, 0, h))

        own_spec = pl.BlockSpec((rows, PAIR), lambda h, i: (0, ((i[0] >> 1) & 1) * steps + h))
        far_spec = pl.BlockSpec((rows, PAIR), lambda h, i: (0, h))
        join_spec = pl.BlockSpec((rows, PAIR), lambda h, i: (0, (1 - ((i[0] >> 1) & 1)) * steps + h))
        stat_spec = pl.BlockSpec((1, 8, KEYS), lambda h, i: (h, 0, 0))
        any_spec = pl.BlockSpec(memory_space=pl.ANY)

        def call(kernel, name, ins, outs, args, grid=(steps,), scratch=(), aliases=None, est=None):
            return pl.pallas_call(
                kernel,
                name=name,
                grid_spec=pltpu.PrefetchScalarGridSpec(
                    num_scalar_prefetch=1,
                    grid=grid,
                    in_specs=ins,
                    out_specs=[s for s, _ in outs],
                    scratch_shapes=list(scratch),
                ),
                out_shape=[o for _, o in outs],
                input_output_aliases=aliases or {},
                cost_estimate=est,
            )(idx, *args)

        audio = (q_a, g_a, k_a, v_a)
        audio_other = [move(x, "core") for x in audio]
        piece = shape((4, 2, half, quarter), BF)
        whole = pl.BlockSpec(memory_space=pltpu.VMEM)
        keep, send = call(
            pack_kernel, "pack", [smem] + [whole] * 8, [(whole, piece)] * 2, (audio_len, *audio, *audio_other), grid=(),
            est=cost(0, 0, 1200000),
        )
        pieces = [
            keep,
            move(send, "aud"),
            move(keep, "A"),
            move(send, "Ax"),
            move(keep, "B"),
            move(send, "Bx"),
        ]
        q_f, k_f, v_f, g_f = [move(x, "core") for x in (q_v, k_v, v_v, g_v)]

        audio_scratch = pltpu.VMEM((2, KEYS, PAIR), BF)
        grad_scratch = pltpu.VMEM((2, KEYS, PAIR), F32)
        pairs = 2 * steps * 2 * rows * KEYS

        stat = shape((steps, 8, KEYS), F32)
        (stats,) = call(
            stats_kernel,
            "stats",
            [win_spec] + [piece_spec(0)] * 6 + [own_spec] * 4,
            [(stat_spec, stat)],
            (window, *pieces, k_v, v_v, k_f, v_f),
            scratch=(audio_scratch, pltpu.VMEM((2, rows, KEYS), F32)),
            est=cost(4 * HD * pairs, pairs, 3000000),
        )
        others = [move(stats, name) for name in ("A", "B", "p2", "m2")]

        full, far = shape((rows, width), BF), shape((rows, quarter), BF)
        va = call(
            va_kernel,
            "va",
            [win_spec, len_spec] + [piece_spec(1)] * 6 + [own_spec] * 4,
            [(own_spec, full)] * 2 + [(far_spec, far)] * 2 + [(piece_spec(0), piece)] * 6,
            (window, audio_len, *pieces, q_v, g_v, q_f, g_f),
            scratch=(audio_scratch, pltpu.VMEM((2, KEYS, rows), F32), grad_scratch),
            est=cost(10 * HD * pairs, pairs, 5000000),
        )
        out_video, dq_video, out_far, dq_far = va[:4]
        av = call(
            lambda *refs: av_kernel(chips, *refs),
            "av",
            [win_spec] + [piece_spec(0)] * 6 + [own_spec] * 4 + [stat_spec] * 5 + [any_spec] * 6,
            [(own_spec, full)] * 2 + [(far_spec, far)] * 2 + [(piece_spec(1), piece)] * 6,
            (window, *pieces, k_v, v_v, k_f, v_f, stats, *others, *va[4:]),
            scratch=(audio_scratch, pltpu.VMEM((2, rows, KEYS), F32), grad_scratch),
            aliases={17 + i: 4 + i for i in range(6)},
            est=cost(12 * HD * pairs, pairs, 5000000),
        )
        dk_video, dv_video, dk_far, dv_far = av[:4]
        back = av[4:]
        parts = [back[0]] + [move(x, name) for x, name in zip(back[1:], ("aud", "A", "Ax", "B", "Bx"))]

        fars = [move(x, "core") for x in (out_far, dq_far, dk_far, dv_far)]
        out_video, dq_video, dk_video, dv_video = call(
            join_video_kernel,
            "join_video",
            [any_spec] * 4 + [far_spec] * 4,
            [(join_spec, full)] * 4,
            (out_video, dq_video, dk_video, dv_video, *fars),
            aliases={1 + i: i for i in range(4)},
            est=cost(0, 0, 1600000),
        )
        mine, other = call(
            sum_kernel, "sum_audio", [smem] + [whole] * 6, [(whole, piece_q(piece))] * 2, (audio_len, *parts), grid=(),
            est=cost(1000000, 0, 1600000),
        )
        other = move(other, "core")
        dk_audio, dv_audio, dq_audio, out_audio = call(
            join_audio_kernel,
            "join_audio",
            [whole] * 2,
            [(whole, shape((half, 2 * width), BF))] * 4,
            (mine, other),
            grid=(),
            est=cost(0, 0, 800000),
        )
        return (out_video, out_audio, dq_video, dk_video, dv_video, dq_audio, dk_audio, dv_audio)

    return body


def piece_q(piece):
    return jax.ShapeDtypeStruct((4, 2) + piece.shape[2:], piece.dtype)


def solution(mesh):
    video, audio = P("vid", "aud"), P(("vid", "aud"), None)
    return jax.shard_map(
        make_body(mesh),
        mesh=mesh,
        in_specs=(video,) * 4 + (audio,) * 4 + (P(), P()),
        out_specs=(video, audio, video, video, video, audio, audio, audio),
        check_vma=False,
    )
```

```python
import jax
import jax.numpy as jnp
from jax import lax
from jax.experimental import pallas as pl
from jax.experimental.pallas import tpu as pltpu
from jax.sharding import PartitionSpec as P


HD = 64
BLK = 64
PAIR = 2 * HD
NEG = -1e30
BF = jnp.bfloat16
F32 = jnp.float32


NPOS = 6
KEYS = NPOS * BLK


def nt(x, y):
    return lax.dot_general(x, y, (((1,), (1,)), ((), ())), preferred_element_type=F32)


def nn(x, y):
    return lax.dot_general(x, y, (((1,), (0,)), ((), ())), preferred_element_type=F32)


def coords(idx_ref):
    idx = idx_ref[0]
    return idx >> 2, (idx >> 1) & 1, idx & 1


def head_part(x, e):
    lane = lax.broadcasted_iota(jnp.int32, x.shape, 1)
    return jnp.where((lane < HD) if e == 0 else (lane >= HD), x, jnp.zeros_like(x))


def pack_kernel(idx_ref, len_ref, *refs):
    mine, other, keep, send, local, sems = refs[:4], refs[4:8], refs[8], refs[9], refs[10], refs[11]
    c, r, a = coords(idx_ref)
    copies = [pltpu.make_async_copy(src, local.at[n], sems.at[n]) for n, src in enumerate(mine)]
    for copy in copies:
        copy.start()
    for copy in copies:
        copy.wait()
    mine = [local.at[n] for n in range(4)]
    half, quarter = keep.shape[2], keep.shape[3]
    row = lax.broadcasted_iota(jnp.int32, (half, quarter), 0) + a * half
    for slot, arrays in ((r, mine), (1 - r, other)):
        valid = row < len_ref[2 * c + slot]
        for n, ref in enumerate(arrays):
            for part, out in ((a, keep), (1 - a, send)):
                col = pl.multiple_of((2 * part + r) * quarter, 128)
                x = ref[:, pl.ds(col, quarter)]
                if n == 0:
                    x = x * jnp.asarray(HD**-0.5, BF)
                if n == 1:
                    x = jnp.where(valid, x, jnp.zeros_like(x))
                out[n, slot] = x


def piece_rows(idx_ref):
    c, _, a = coords(idx_ref)
    half = BLK // 2
    side = 2 - 2 * (c & 1)
    starts = []
    for place, part in ((1, a), (1, 1 - a), (side, a), (side, 1 - a), (2 - side, a), (2 - side, 1 - a)):
        first = place * 2 * BLK + part * half
        starts.append([pl.multiple_of(first + core * BLK, half) for core in range(2)])
    return starts


def gather_audio(idx_ref, pieces, dst):
    half = BLK // 2
    for ref, firsts in zip(pieces, piece_rows(idx_ref)):
        for core, first in enumerate(firsts):
            for n in range(2):
                dst[n, pl.ds(first, half), :] = ref[n, core]


def scatter_audio(idx_ref, src, pieces):
    half = BLK // 2
    for ref, firsts in zip(pieces, piece_rows(idx_ref)):
        for core, first in enumerate(firsts):
            for n in range(2):
                ref[n, core] = src[n, pl.ds(first, half), :].astype(ref.dtype)


def window_bounds(win_ref, c, stretch, shape, axis):
    block = lax.broadcasted_iota(jnp.int32, shape, axis) // BLK
    lo = jnp.zeros(shape, jnp.int32)
    hi = jnp.zeros(shape, jnp.int32)
    for b in range(4):
        start = win_ref[4 * stretch + b, 0] - (2 * c - 2)
        count = win_ref[4 * stretch + b, 1]
        lo = jnp.where(block == b, start, lo)
        hi = jnp.where(block == b, start + count, hi)
    return lo, hi


def av_bias(idx_ref, win_ref, bias):
    c, r, _ = coords(idx_ref)
    for i, stretch in enumerate((r, 1 - r)):
        shape = bias.shape[1:]
        lo, hi = window_bounds(win_ref, c, stretch, shape, 0)
        place = lax.broadcasted_iota(jnp.int32, shape, 1) // BLK
        bias[i] = jnp.where((place >= lo) & (place < hi), 0.0, NEG)


def va_bias(idx_ref, win_ref, len_ref, bias):
    c, r, _ = coords(idx_ref)
    shape = bias.shape[1:]
    row = lax.broadcasted_iota(jnp.int32, shape, 0)
    place = row // BLK
    length = jnp.zeros(shape, jnp.int32)
    for j in range(NPOS):
        block = jnp.clip(2 * c - 2 + j, 0, len_ref.shape[0] - 1)
        length = jnp.where(place == j, len_ref[block], length)
    valid = (row % BLK) < length
    for i, stretch in enumerate((r, 1 - r)):
        lo, hi = window_bounds(win_ref, c, stretch, shape, 1)
        bias[i] = jnp.where((place >= lo) & (place < hi) & valid, 0.0, NEG)


def stats_kernel(idx_ref, win_ref, *refs):
    pieces = refs[:6]
    video = ((refs[6], refs[7]), (refs[8], refs[9]))
    stat_ref, audio, bias = refs[10:]

    @pl.when(pl.program_id(0) == 0)
    def _():
        av_bias(idx_ref, win_ref, bias)

    gather_audio(idx_ref, pieces, audio)
    queries, cot = audio[0], audio[1]
    lses, deltas = [], []
    for e in range(2):
        parts = []
        for i, (k_ref, v_ref) in enumerate(video):
            s = nt(head_part(k_ref[...], e), queries) + bias[i]
            m = jnp.max(s, axis=0, keepdims=True)
            ex = jnp.exp(s - m)
            dp = nt(head_part(v_ref[...], e), cot)
            parts.append((m, jnp.sum(ex, axis=0, keepdims=True), jnp.sum(ex * dp, axis=0, keepdims=True)))
        m = jnp.maximum(parts[0][0], parts[1][0])
        w0, w1 = jnp.exp(parts[0][0] - m), jnp.exp(parts[1][0] - m)
        total = parts[0][1] * w0 + parts[1][1] * w1
        lses.append(m + jnp.log(total))
        deltas.append((parts[0][2] * w0 + parts[1][2] * w1) / total)
    stat_ref[0] = jnp.concatenate(lses + deltas + lses + deltas, axis=0)


def merge_stats(idx_ref, chips, own, by_a, by_b, before2, after2):
    c, _, _ = coords(idx_ref)
    even = (c & 1) == 0
    before = jnp.where(even, by_b, by_a)
    after = jnp.where(even, by_a, by_b)
    w = 2 * BLK

    def part(x, k, there):
        x = x[:, k * w : (k + 1) * w]
        return jnp.where(there, x[0:2], NEG), x[2:4]

    one, two = c >= 1, c >= 2
    nxt, nxt2 = c + 1 < chips, c + 2 < chips
    always = c >= 0
    groups = (
        (part(own, 0, always), part(before, 1, one), part(before2, 2, two)),
        (part(own, 1, always), part(before, 2, one), part(after, 0, nxt)),
        (part(own, 2, always), part(after, 1, nxt), part(after2, 0, nxt2)),
    )
    lses, deltas = [], []
    for group in groups:
        m = jnp.maximum(jnp.maximum(group[0][0], group[1][0]), group[2][0])
        ws = [jnp.exp(lse - m) for lse, _ in group]
        total = ws[0] + ws[1] + ws[2]
        lses.append(m + jnp.log(total))
        deltas.append(sum(wt * d for wt, (_, d) in zip(ws, group)) / total)
    return jnp.concatenate(lses, axis=1), jnp.concatenate(deltas, axis=1)


def va_kernel(idx_ref, win_ref, len_ref, *refs):
    pieces = refs[:6]
    video = ((refs[6], refs[7]), (refs[8], refs[9]))
    outs = ((refs[10], refs[11]), (refs[12], refs[13]))
    back = refs[14:20]
    audio, bias, grads = refs[20:]

    @pl.when(pl.program_id(0) == 0)
    def _():
        va_bias(idx_ref, win_ref, len_ref, bias)

    gather_audio(idx_ref, pieces, audio)
    keys, values = audio[0], audio[1]
    keys_t, values_t = keys.T, values.T
    k_heads = [head_part(keys, e) for e in range(2)]
    v_heads = [head_part(values, e) for e in range(2)]
    dk, dv = None, None
    for i, ((q_ref, g_ref), (out_ref, dq_ref)) in enumerate(zip(video, outs)):
        q = q_ref[...] * jnp.asarray(HD**-0.5, BF)
        g = g_ref[...]
        out_t, dq_t = [], []
        for e in range(2):
            s = nt(k_heads[e], q) + bias[i]
            m = jnp.max(s, axis=0, keepdims=True)
            ex = jnp.exp(s - m)
            p = ex * (1.0 / jnp.sum(ex, axis=0, keepdims=True))
            pb = p.astype(BF)
            dp = nt(v_heads[e], g)
            delta = jnp.sum(p * dp, axis=0, keepdims=True)
            ds = (p * (dp - delta)).astype(BF)
            dk_e, dv_e = nn(ds, head_part(q, e)), nn(pb, head_part(g, e))
            dk = dk_e if dk is None else dk + dk_e
            dv = dv_e if dv is None else dv + dv_e
            out_t.append(nn(values_t[e * HD : (e + 1) * HD], pb))
            dq_t.append(nn(keys_t[e * HD : (e + 1) * HD], ds))
        out_ref[...] = jnp.concatenate(out_t, axis=0).T.astype(BF)
        dq_ref[...] = (jnp.concatenate(dq_t, axis=0).T * HD**-0.5).astype(BF)
    grads[0] = dk
    grads[1] = dv
    scatter_audio(idx_ref, grads, back)


def av_kernel(chips, idx_ref, win_ref, *refs):
    pieces = refs[:6]
    video = ((refs[6], refs[7]), (refs[8], refs[9]))
    stats = [ref[0] for ref in refs[10:15]]
    outs = ((refs[21], refs[22]), (refs[23], refs[24]))
    back = refs[25:31]
    audio, bias, grads = refs[31:]

    @pl.when(pl.program_id(0) == 0)
    def _():
        av_bias(idx_ref, win_ref, bias)

    gather_audio(idx_ref, pieces, audio)
    queries, cot = audio[0], audio[1]
    q_heads = [head_part(queries, e) for e in range(2)]
    g_heads = [head_part(cot, e) for e in range(2)]
    lse, delta = merge_stats(idx_ref, chips, *stats)
    dq_t, out_t = [None, None], [None, None]
    for i, ((k_ref, v_ref), (dk_ref, dv_ref)) in enumerate(zip(video, outs)):
        keys, values = k_ref[...], v_ref[...]
        keys_t, values_t = keys.T, values.T
        dk, dv = None, None
        for e in range(2):
            s = nt(head_part(keys, e), queries) + bias[i]
            p = jnp.exp(s - lse[e : e + 1])
            pb = p.astype(BF)
            dp = nt(head_part(values, e), cot)
            ds = (p * (dp - delta[e : e + 1])).astype(BF)
            dk_e, dv_e = nn(ds, q_heads[e]), nn(pb, g_heads[e])
            dk = dk_e if dk is None else dk + dk_e
            dv = dv_e if dv is None else dv + dv_e
            dq_e = nn(keys_t[e * HD : (e + 1) * HD], ds)
            out_e = nn(values_t[e * HD : (e + 1) * HD], pb)
            dq_t[e] = dq_e if i == 0 else dq_t[e] + dq_e
            out_t[e] = out_e if i == 0 else out_t[e] + out_e
        dk_ref[...] = dk.astype(BF)
        dv_ref[...] = dv.astype(BF)
    grads[0] = jnp.concatenate(dq_t, axis=0).T * HD**-0.5
    grads[1] = jnp.concatenate(out_t, axis=0).T
    scatter_audio(idx_ref, grads, back)


def sum_kernel(idx_ref, len_ref, keep, by_aud, by_a, by_ax, by_b, by_bx, after, mine, other):
    c, r, a = coords(idx_ref)
    half, quarter = keep.shape[2], keep.shape[3]
    row = lax.broadcasted_iota(jnp.int32, (half, quarter), 0) + a * half
    for slot, out in ((r, mine), (1 - r, other)):
        valid = row < len_ref[2 * c + slot]
        for part, parts in ((a, (keep, by_a, by_b)), (1 - a, (by_aud, by_ax, by_bx))):
            for n in range(4):
                x = sum(ref[n, slot].astype(F32) for ref in parts)
                if n == 3:
                    x = jnp.where(valid, x, 0.0)
                out[n, part] = x.astype(BF)


def join_audio_kernel(idx_ref, mine, other, *outs):
    _, r, _ = coords(idx_ref)
    quarter = mine.shape[3]
    for n, out in enumerate(outs):
        for part in range(2):
            for core, ref in ((r, mine), (1 - r, other)):
                col = pl.multiple_of((2 * part + core) * quarter, 128)
                out[:, pl.ds(col, quarter)] = ref[n, part]


def join_video_kernel(idx_ref, *refs):
    for src, out in zip(refs[4:8], refs[8:12]):
        out[...] = src[...]
    refs[12][0] = 0


def cost(flops, transcendentals, nbytes):
    return pl.CostEstimate(flops=flops, transcendentals=transcendentals, bytes_accessed=nbytes)


def make_body(mesh):
    nv = mesh.shape["vid"]
    chips = nv // 2
    everyone = [(v, a) for v in range(nv) for a in range(2)]

    def perm(move):
        pairs = []
        for v, a in everyone:
            w, b = move(v, a)
            if 0 <= w < nv:
                pairs.append((2 * v + a, 2 * w + b))
        return pairs

    def diagonal(v):
        return 2 * ((((v >> 1) + 1) ^ 1) - 1) + (v & 1)

    moves = {
        "core": perm(lambda v, a: (v ^ 1, a)),
        "aud": perm(lambda v, a: (v, 1 - a)),
        "A": perm(lambda v, a: (v ^ 2, a)),
        "Ax": perm(lambda v, a: (v ^ 2, 1 - a)),
        "B": perm(lambda v, a: (diagonal(v), a)),
        "Bx": perm(lambda v, a: (diagonal(v), 1 - a)),
        "p2": perm(lambda v, a: (v + 4, a)),
        "m2": perm(lambda v, a: (v - 4, a)),
    }

    def move(x, name):
        return lax.ppermute(x, ("vid", "aud"), moves[name])

    def step(q_v, k_v, v_v, g_v, q_a, k_a, v_a, g_a, window, audio_len):
        rows, width = q_v.shape
        quarter = width // 2
        half = q_a.shape[0]
        steps = quarter // PAIR
        idx = jnp.reshape(2 * lax.axis_index("vid") + lax.axis_index("aud"), (1,)).astype(jnp.int32)
        shape = jax.ShapeDtypeStruct

        smem = pl.BlockSpec(memory_space=pltpu.SMEM)
        win_spec = pl.BlockSpec((8, 2), lambda h, i: (i[0] >> 2, 0), memory_space=pltpu.SMEM)
        len_spec = pl.BlockSpec(memory_space=pltpu.SMEM)

        def piece_spec(n):
            return pl.BlockSpec((2, 2, half, PAIR), lambda h, i: (n, 0, 0, h))

        own_spec = pl.BlockSpec((rows, PAIR), lambda h, i: (0, ((i[0] >> 1) & 1) * steps + h))
        far_spec = pl.BlockSpec((rows, PAIR), lambda h, i: (0, h))
        join_spec = pl.BlockSpec((rows, PAIR), lambda h, i: (0, (1 - ((i[0] >> 1) & 1)) * steps + h))
        stat_spec = pl.BlockSpec((1, 8, KEYS), lambda h, i: (h, 0, 0))
        any_spec = pl.BlockSpec(memory_space=pl.ANY)
        hbm = pl.BlockSpec(memory_space=pltpu.HBM)

        def call(kernel, ins, outs, args, grid=(steps,), scratch=(), aliases=None, est=None):
            return pl.pallas_call(
                kernel,
                grid_spec=pltpu.PrefetchScalarGridSpec(
                    num_scalar_prefetch=1,
                    grid=grid,
                    in_specs=ins,
                    out_specs=[s for s, _ in outs],
                    scratch_shapes=list(scratch),
                ),
                out_shape=[o for _, o in outs],
                input_output_aliases=aliases or {},
                cost_estimate=est,
                compiler_params=pltpu.CompilerParams(vmem_limit_bytes=24 << 20),
            )(idx, *args)

        audio = (q_a, g_a, k_a, v_a)
        audio_other = [move(x, "core") for x in audio]
        piece = shape((4, 2, half, quarter), BF)
        whole = pl.BlockSpec(memory_space=pltpu.VMEM)
        keep, send = call(
            pack_kernel, [smem] + [hbm] * 4 + [whole] * 4, [(whole, piece)] * 2, (audio_len, *[pltpu.with_memory_space_constraint(x, pltpu.HBM) for x in audio], *audio_other), grid=(),
            scratch=(pltpu.VMEM((4, half, 2 * width), BF), pltpu.SemaphoreType.DMA((4,))),
            est=cost(0, 0, 1200000),
        )
        pieces = [keep, move(send, "aud"), move(keep, "A"), move(send, "Ax"), move(keep, "B"), move(send, "Bx")]
        k_f, v_f, q_f, g_f = [move(x, "core") for x in (k_v, v_v, q_v, g_v)]

        audio_scratch = pltpu.VMEM((2, KEYS, PAIR), BF)
        grad_scratch = pltpu.VMEM((2, KEYS, PAIR), F32)
        pairs = 2 * steps * 2 * rows * KEYS

        stat = shape((steps, 8, KEYS), F32)
        (stats,) = call(
            stats_kernel,
            [win_spec] + [piece_spec(0)] * 6 + [own_spec] * 4,
            [(stat_spec, stat)],
            (window, *pieces, k_v, v_v, k_f, v_f),
            scratch=(audio_scratch, pltpu.VMEM((2, rows, KEYS), F32)),
            est=cost(4 * HD * pairs, pairs, 3000000),
        )
        others = [move(stats, name) for name in ("A", "B", "p2", "m2")]

        full, far = shape((rows, width), BF), shape((rows, quarter), BF)
        va = call(
            va_kernel,
            [win_spec, len_spec] + [piece_spec(1)] * 6 + [own_spec] * 4,
            [(own_spec, full)] * 2 + [(far_spec, far)] * 2 + [(piece_spec(0), piece)] * 6,
            (window, audio_len, *pieces, q_v, g_v, q_f, g_f),
            scratch=(audio_scratch, pltpu.VMEM((2, KEYS, rows), F32), grad_scratch),
            est=cost(10 * HD * pairs, pairs, 5000000),
        )
        out_video, dq_video, out_far, dq_far = va[:4]
        av = call(
            lambda *refs: av_kernel(chips, *refs),
            [win_spec] + [piece_spec(0)] * 6 + [own_spec] * 4 + [stat_spec] * 5 + [any_spec] * 6,
            [(own_spec, full)] * 2 + [(far_spec, far)] * 2 + [(piece_spec(1), piece)] * 6,
            (window, *pieces, k_v, v_v, k_f, v_f, stats, *others, *va[4:]),
            scratch=(audio_scratch, pltpu.VMEM((2, rows, KEYS), F32), grad_scratch),
            aliases={17 + i: 4 + i for i in range(6)},
            est=cost(12 * HD * pairs, pairs, 5000000),
        )
        dk_video, dv_video, dk_far, dv_far = av[:4]
        back = av[4:]
        parts = [back[0]] + [move(x, name) for x, name in zip(back[1:], ("aud", "A", "Ax", "B", "Bx"))]

        fars = [move(x, "core") for x in (out_far, dq_far, dk_far, dv_far)]
        out_video, dq_video, dk_video, dv_video, joined = call(
            join_video_kernel,
            [any_spec] * 4 + [far_spec] * 4,
            [(join_spec, full)] * 4 + [(smem, shape((1,), jnp.int32))],
            (out_video, dq_video, dk_video, dv_video, *fars),
            aliases={1 + i: i for i in range(4)},
            est=cost(0, 0, 1600000),
        )
        mine, other = call(
            sum_kernel, [smem] + [whole] * 6 + [smem], [(whole, piece)] * 2, (audio_len, *parts, joined), grid=(),
            est=cost(1000000, 0, 1600000),
        )
        other = move(other, "core")
        dk_audio, dv_audio, dq_audio, out_audio = call(
            join_audio_kernel,
            [whole] * 2,
            [(whole, shape((half, 2 * width), BF))] * 4,
            (mine, other),
            grid=(),
            est=cost(0, 0, 800000),
        )
        return (out_video, out_audio, dq_video, dk_video, dv_video, dq_audio, dk_audio, dv_audio)

    return step


def solution(mesh):
    video, audio = P("vid", "aud"), P(("vid", "aud"), None)
    return jax.shard_map(
        make_body(mesh),
        mesh=mesh,
        in_specs=(video,) * 4 + (audio,) * 4 + (P(), P()),
        out_specs=(video, audio, video, video, video, audio, audio, audio),
        check_vma=False,
    )
```

```python
import jax
import jax.numpy as jnp
from jax import lax
from jax.experimental import pallas as pl
from jax.experimental.pallas import tpu as pltpu
from jax.sharding import PartitionSpec as P


HD = 64
BLK = 64
WMAX = 3
PAIR = 2 * HD
NEG = -1e30
BF = jnp.bfloat16
F32 = jnp.float32


NPOS = 6
KEYS = NPOS * BLK
GROUP = 8


def nt(x, y):
    return lax.dot_general(x, y, (((1,), (1,)), ((), ())), preferred_element_type=F32)


def nn(x, y):
    return lax.dot_general(x, y, (((1,), (0,)), ((), ())), preferred_element_type=F32)


def coords(idx_ref):
    idx = idx_ref[0]
    return idx >> 2, (idx >> 1) & 1, idx & 1


def head_part(x, e):
    lane = lax.broadcasted_iota(jnp.int32, x.shape, 1)
    return jnp.where((lane < HD) if e == 0 else (lane >= HD), x, jnp.zeros_like(x))


def pack_kernel(idx_ref, len_ref, *refs):
    mine, other, keep, send, local, sems = refs[:4], refs[4:8], refs[8], refs[9], refs[10], refs[11]
    c, r, a = coords(idx_ref)
    copies = [pltpu.make_async_copy(src, local.at[n], sems.at[n]) for n, src in enumerate(mine)]
    for copy in copies:
        copy.start()
    for copy in copies:
        copy.wait()
    mine = [local.at[n] for n in range(4)]
    half, quarter = keep.shape[2], keep.shape[3]
    row = lax.broadcasted_iota(jnp.int32, (half, quarter), 0) + a * half
    for slot, arrays in ((r, mine), (1 - r, other)):
        valid = row < len_ref[2 * c + slot]
        for n, ref in enumerate(arrays):
            for part, out in ((a, keep), (1 - a, send)):
                col = pl.multiple_of((2 * part + r) * quarter, 128)
                x = ref[:, pl.ds(col, quarter)]
                if n == 0:
                    x = x * jnp.asarray(HD**-0.5, BF)
                if n == 1:
                    x = jnp.where(valid, x, jnp.zeros_like(x))
                out[n, slot] = x


def piece_rows(idx_ref):
    c, _, a = coords(idx_ref)
    half = BLK // 2
    side = 2 - 2 * (c & 1)
    starts = []
    for place, part in ((1, a), (1, 1 - a), (side, a), (side, 1 - a), (2 - side, a), (2 - side, 1 - a)):
        first = place * 2 * BLK + part * half
        starts.append([pl.multiple_of(first + core * BLK, half) for core in range(2)])
    return starts


def gather_audio(idx_ref, pieces, dst):
    half = BLK // 2
    for ref, firsts in zip(pieces, piece_rows(idx_ref)):
        for core, first in enumerate(firsts):
            for n in range(2):
                dst[n, pl.ds(first, half), :] = ref[n, core]


def scatter_audio(idx_ref, src, pieces):
    half = BLK // 2
    for ref, firsts in zip(pieces, piece_rows(idx_ref)):
        for core, first in enumerate(firsts):
            for n in range(2):
                ref[n, core] = src[n, pl.ds(first, half), :].astype(ref.dtype)


def window_bounds(win_ref, c, stretch, shape, axis):
    block = lax.broadcasted_iota(jnp.int32, shape, axis) // BLK
    lo = jnp.zeros(shape, jnp.int32)
    hi = jnp.zeros(shape, jnp.int32)
    for b in range(4):
        start = win_ref[4 * stretch + b, 0] - (2 * c - 2)
        count = win_ref[4 * stretch + b, 1]
        lo = jnp.where(block == b, start, lo)
        hi = jnp.where(block == b, start + count, hi)
    return lo, hi


def av_bias(idx_ref, win_ref, bias):
    c, r, _ = coords(idx_ref)
    for i, stretch in enumerate((r, 1 - r)):
        shape = bias.shape[1:]
        lo, hi = window_bounds(win_ref, c, stretch, shape, 0)
        place = lax.broadcasted_iota(jnp.int32, shape, 1) // BLK
        bias[i] = jnp.where((place >= lo) & (place < hi), 0.0, NEG)


def window_of(idx_ref, win_ref, stretch, b):
    c, _, _ = coords(idx_ref)
    return win_ref[4 * stretch + b, 0] - (2 * c - 2), win_ref[4 * stretch + b, 1]


def block_bias(idx_ref, win_ref, len_ref, bias):
    c, r, _ = coords(idx_ref)
    row = lax.broadcasted_iota(jnp.int32, bias.shape[1:], 0)
    for i, stretch in enumerate((r, 1 - r)):
        for b in range(4):
            start, count = window_of(idx_ref, win_ref, stretch, b)
            keep = row < count * BLK
            if len_ref is not None:
                length = jnp.zeros(row.shape, jnp.int32)
                for j in range(WMAX):
                    block = jnp.clip(2 * c - 2 + start + j, 0, len_ref.shape[0] - 1)
                    length = jnp.where(row // BLK == j, len_ref[block], length)
                keep = keep & (row % BLK < length)
            bias[4 * i + b] = jnp.where(keep, 0.0, NEG)


def both_heads(x):
    return jnp.concatenate([head_part(x, 0), head_part(x, 1)], axis=0)


def own_heads(x):
    lane = lax.broadcasted_iota(jnp.int32, (BLK, PAIR), 1)
    return jnp.where(lane < HD, x[:BLK], x[BLK:])


def block_groups(r):
    blocks = [(i, stretch, b) for b in range(4) for i, stretch in enumerate((r, 1 - r))]
    return [blocks[n : n + GROUP] for n in range(0, 8, GROUP)]


def tn(x, y):
    return lax.dot_general(x, y, (((0,), (0,)), ((), ())), preferred_element_type=F32)


def stats_kernel(idx_ref, win_ref, *refs):
    pieces = refs[:6]
    video = ((refs[6], refs[7]), (refs[8], refs[9]))
    stat_ref, audio, bias = refs[10:]

    @pl.when(pl.program_id(0) == 0)
    def _():
        av_bias(idx_ref, win_ref, bias)

    gather_audio(idx_ref, pieces, audio)
    queries, cot = audio[0], audio[1]
    lses, deltas = [], []
    for e in range(2):
        parts = []
        for i, (k_ref, v_ref) in enumerate(video):
            s = nt(head_part(k_ref[...], e), queries) + bias[i]
            m = jnp.max(s, axis=0, keepdims=True)
            ex = jnp.exp(s - m)
            dp = nt(head_part(v_ref[...], e), cot)
            parts.append((m, jnp.sum(ex, axis=0, keepdims=True), jnp.sum(ex * dp, axis=0, keepdims=True)))
        m = jnp.maximum(parts[0][0], parts[1][0])
        w0, w1 = jnp.exp(parts[0][0] - m), jnp.exp(parts[1][0] - m)
        total = parts[0][1] * w0 + parts[1][1] * w1
        lses.append(m + jnp.log(total))
        deltas.append((parts[0][2] * w0 + parts[1][2] * w1) / total)
    stat_ref[0] = jnp.concatenate(lses + deltas + lses + deltas, axis=0)


def merge_stats(idx_ref, chips, own, by_a, by_b, before2, after2):
    c, _, _ = coords(idx_ref)
    even = (c & 1) == 0
    before = jnp.where(even, by_b, by_a)
    after = jnp.where(even, by_a, by_b)
    w = 2 * BLK

    def part(x, k, there):
        x = x[:, k * w : (k + 1) * w]
        return jnp.where(there, x[0:2], NEG), x[2:4]

    one, two = c >= 1, c >= 2
    nxt, nxt2 = c + 1 < chips, c + 2 < chips
    always = c >= 0
    groups = (
        (part(own, 0, always), part(before, 1, one), part(before2, 2, two)),
        (part(own, 1, always), part(before, 2, one), part(after, 0, nxt)),
        (part(own, 2, always), part(after, 1, nxt), part(after2, 0, nxt2)),
    )
    lses, deltas = [], []
    for group in groups:
        m = jnp.maximum(jnp.maximum(group[0][0], group[1][0]), group[2][0])
        ws = [jnp.exp(lse - m) for lse, _ in group]
        total = ws[0] + ws[1] + ws[2]
        lses.append(m + jnp.log(total))
        deltas.append(sum(wt * d for wt, (_, d) in zip(ws, group)) / total)
    return jnp.concatenate(lses, axis=1), jnp.concatenate(deltas, axis=1)


def va_kernel(idx_ref, win_ref, len_ref, *refs):
    pieces = refs[:6]
    video = ((refs[6], refs[7]), (refs[8], refs[9]))
    outs = ((refs[10], refs[11]), (refs[12], refs[13]))
    back = refs[14:20]
    audio, bias, grads = refs[20:]
    _, r, _ = coords(idx_ref)

    @pl.when(pl.program_id(0) == 0)
    def _():
        block_bias(idx_ref, win_ref, len_ref, bias)

    gather_audio(idx_ref, pieces, audio)
    grads[...] = jnp.zeros(grads.shape, F32)
    scale = jnp.asarray(HD**-0.5, BF)
    for group in block_groups(r):
        work = []
        for i, stretch, b in group:
            start, _ = window_of(idx_ref, win_ref, stretch, b)
            span = pl.ds(pl.multiple_of(start * BLK, BLK), WMAX * BLK)
            rows = slice(b * BLK, (b + 1) * BLK)
            q = both_heads(video[i][0][rows, :] * scale)
            g = both_heads(video[i][1][rows, :])
            keys, values = audio[0, span, :], audio[1, span, :]
            s = nt(keys, q) + bias[4 * i + b]
            dp = nt(values, g)
            work.append((i, rows, span, q, g, keys, values, s, dp))
        done = []
        for i, rows, span, q, g, keys, values, s, dp in work:
            ex = jnp.exp(s - jnp.max(s, axis=0, keepdims=True))
            inv = 1.0 / jnp.sum(ex, axis=0, keepdims=True)
            delta = jnp.sum(ex * dp, axis=0, keepdims=True) * inv
            p = ex * inv
            pb = p.astype(BF)
            ds = (p * (dp - delta)).astype(BF)
            done.append((i, rows, span, nn(ds, q), nn(pb, g), tn(pb, values), tn(ds, keys)))
        for i, rows, span, dk, dv, out, dq in done:
            grads[0, span, :] += dk
            grads[1, span, :] += dv
            outs[i][0][rows, :] = own_heads(out).astype(BF)
            outs[i][1][rows, :] = (own_heads(dq) * HD**-0.5).astype(BF)
    scatter_audio(idx_ref, grads, back)


def av_kernel(chips, idx_ref, win_ref, *refs):
    pieces = refs[:6]
    video = ((refs[6], refs[7]), (refs[8], refs[9]))
    stats = [ref[0] for ref in refs[10:15]]
    outs = ((refs[21], refs[22]), (refs[23], refs[24]))
    back = refs[25:31]
    audio, bias, grads, rowstat = refs[31:]
    _, r, _ = coords(idx_ref)

    @pl.when(pl.program_id(0) == 0)
    def _():
        block_bias(idx_ref, win_ref, None, bias)

    gather_audio(idx_ref, pieces, audio)
    for n, x in enumerate(merge_stats(idx_ref, chips, *stats)):
        wide = [jnp.broadcast_to(x[e : e + 1], (HD, KEYS)) for e in range(2)]
        rowstat[n] = jnp.concatenate(wide, axis=0).T
    grads[...] = jnp.zeros(grads.shape, F32)
    for group in block_groups(r):
        work = []
        for i, stretch, b in group:
            start, _ = window_of(idx_ref, win_ref, stretch, b)
            span = pl.ds(pl.multiple_of(start * BLK, BLK), WMAX * BLK)
            rows = slice(b * BLK, (b + 1) * BLK)
            keys = both_heads(video[i][0][rows, :])
            values = both_heads(video[i][1][rows, :])
            q, g = audio[0, span, :], audio[1, span, :]
            s = nt(q, keys) + bias[4 * i + b]
            dp = nt(g, values)
            work.append((i, rows, span, keys, values, q, g, s, dp))
        done = []
        for i, rows, span, keys, values, q, g, s, dp in work:
            p = jnp.exp(s - rowstat[0, span, :])
            pb = p.astype(BF)
            ds = (p * (dp - rowstat[1, span, :])).astype(BF)
            done.append((i, rows, span, nn(ds, keys), nn(pb, values), tn(ds, q), tn(pb, g)))
        for i, rows, span, dq, out, dk, dv in done:
            grads[0, span, :] += dq
            grads[1, span, :] += out
            outs[i][0][rows, :] = own_heads(dk).astype(BF)
            outs[i][1][rows, :] = own_heads(dv).astype(BF)
    grads[0] = grads[0] * HD**-0.5
    scatter_audio(idx_ref, grads, back)


def sum_kernel(idx_ref, len_ref, keep, by_aud, by_a, by_ax, by_b, by_bx, after, mine, other):
    c, r, a = coords(idx_ref)
    half, quarter = keep.shape[2], keep.shape[3]
    row = lax.broadcasted_iota(jnp.int32, (half, quarter), 0) + a * half
    for slot, out in ((r, mine), (1 - r, other)):
        valid = row < len_ref[2 * c + slot]
        for part, parts in ((a, (keep, by_a, by_b)), (1 - a, (by_aud, by_ax, by_bx))):
            for n in range(4):
                x = sum(ref[n, slot].astype(F32) for ref in parts)
                if n == 3:
                    x = jnp.where(valid, x, 0.0)
                out[n, part] = x.astype(BF)


def join_audio_kernel(idx_ref, mine, other, *outs):
    _, r, _ = coords(idx_ref)
    quarter = mine.shape[3]
    for n, out in enumerate(outs):
        for part in range(2):
            for core, ref in ((r, mine), (1 - r, other)):
                col = pl.multiple_of((2 * part + core) * quarter, 128)
                out[:, pl.ds(col, quarter)] = ref[n, part]


def join_video_kernel(idx_ref, *refs):
    for src, out in zip(refs[4:8], refs[8:12]):
        out[...] = src[...]
    refs[12][0] = 0


def cost(flops, transcendentals, nbytes):
    return pl.CostEstimate(flops=flops, transcendentals=transcendentals, bytes_accessed=nbytes)


def make_body(mesh):
    nv = mesh.shape["vid"]
    chips = nv // 2
    everyone = [(v, a) for v in range(nv) for a in range(2)]

    def perm(move):
        pairs = []
        for v, a in everyone:
            w, b = move(v, a)
            if 0 <= w < nv:
                pairs.append((2 * v + a, 2 * w + b))
        return pairs

    def diagonal(v):
        return 2 * ((((v >> 1) + 1) ^ 1) - 1) + (v & 1)

    moves = {
        "core": perm(lambda v, a: (v ^ 1, a)),
        "aud": perm(lambda v, a: (v, 1 - a)),
        "A": perm(lambda v, a: (v ^ 2, a)),
        "Ax": perm(lambda v, a: (v ^ 2, 1 - a)),
        "B": perm(lambda v, a: (diagonal(v), a)),
        "Bx": perm(lambda v, a: (diagonal(v), 1 - a)),
        "p2": perm(lambda v, a: (v + 4, a)),
        "m2": perm(lambda v, a: (v - 4, a)),
    }

    def move(x, name):
        return lax.ppermute(x, ("vid", "aud"), moves[name])

    def step(q_v, k_v, v_v, g_v, q_a, k_a, v_a, g_a, window, audio_len):
        rows, width = q_v.shape
        quarter = width // 2
        half = q_a.shape[0]
        steps = quarter // PAIR
        idx = jnp.reshape(2 * lax.axis_index("vid") + lax.axis_index("aud"), (1,)).astype(jnp.int32)
        shape = jax.ShapeDtypeStruct

        smem = pl.BlockSpec(memory_space=pltpu.SMEM)
        win_spec = pl.BlockSpec((8, 2), lambda h, i: (i[0] >> 2, 0), memory_space=pltpu.SMEM)
        len_spec = pl.BlockSpec(memory_space=pltpu.SMEM)

        def piece_spec(n):
            return pl.BlockSpec((2, 2, half, PAIR), lambda h, i: (n, 0, 0, h))

        own_spec = pl.BlockSpec((rows, PAIR), lambda h, i: (0, ((i[0] >> 1) & 1) * steps + h))
        far_spec = pl.BlockSpec((rows, PAIR), lambda h, i: (0, h))
        join_spec = pl.BlockSpec((rows, PAIR), lambda h, i: (0, (1 - ((i[0] >> 1) & 1)) * steps + h))
        stat_spec = pl.BlockSpec((1, 8, KEYS), lambda h, i: (h, 0, 0))
        any_spec = pl.BlockSpec(memory_space=pl.ANY)
        hbm = pl.BlockSpec(memory_space=pltpu.HBM)

        def call(kernel, ins, outs, args, grid=(steps,), scratch=(), aliases=None, est=None):
            return pl.pallas_call(
                kernel,
                grid_spec=pltpu.PrefetchScalarGridSpec(
                    num_scalar_prefetch=1,
                    grid=grid,
                    in_specs=ins,
                    out_specs=[s for s, _ in outs],
                    scratch_shapes=list(scratch),
                ),
                out_shape=[o for _, o in outs],
                input_output_aliases=aliases or {},
                cost_estimate=est,
                compiler_params=pltpu.CompilerParams(vmem_limit_bytes=24 << 20),
            )(idx, *args)

        audio = (q_a, g_a, k_a, v_a)
        audio_other = [move(x, "core") for x in audio]
        piece = shape((4, 2, half, quarter), BF)
        whole = pl.BlockSpec(memory_space=pltpu.VMEM)
        keep, send = call(
            pack_kernel, [smem] + [hbm] * 4 + [whole] * 4, [(whole, piece)] * 2, (audio_len, *[pltpu.with_memory_space_constraint(x, pltpu.HBM) for x in audio], *audio_other), grid=(),
            scratch=(pltpu.VMEM((4, half, 2 * width), BF), pltpu.SemaphoreType.DMA((4,))),
            est=cost(0, 0, 1200000),
        )
        pieces = [keep, move(send, "aud"), move(keep, "A"), move(send, "Ax"), move(keep, "B"), move(send, "Bx")]
        k_f, v_f, q_f, g_f = [move(x, "core") for x in (k_v, v_v, q_v, g_v)]

        audio_scratch = pltpu.VMEM((2, KEYS, PAIR), BF)
        grad_scratch = pltpu.VMEM((2, KEYS, PAIR), F32)
        bias_scratch = pltpu.VMEM((8, WMAX * BLK, PAIR), F32)
        pairs = 2 * steps * 2 * rows * KEYS

        stat = shape((steps, 8, KEYS), F32)
        (stats,) = call(
            stats_kernel,
            [win_spec] + [piece_spec(0)] * 6 + [own_spec] * 4,
            [(stat_spec, stat)],
            (window, *pieces, k_v, v_v, k_f, v_f),
            scratch=(audio_scratch, pltpu.VMEM((2, rows, KEYS), F32)),
            est=cost(4 * HD * pairs, pairs, 3000000),
        )
        others = [move(stats, name) for name in ("A", "B", "p2", "m2")]

        full, far = shape((rows, width), BF), shape((rows, quarter), BF)
        va = call(
            va_kernel,
            [win_spec, len_spec] + [piece_spec(1)] * 6 + [own_spec] * 4,
            [(own_spec, full)] * 2 + [(far_spec, far)] * 2 + [(piece_spec(0), piece)] * 6,
            (window, audio_len, *pieces, q_v, g_v, q_f, g_f),
            scratch=(audio_scratch, bias_scratch, grad_scratch),
            est=cost(10 * HD * pairs, pairs, 5000000),
        )
        out_video, dq_video, out_far, dq_far = va[:4]
        av = call(
            lambda *refs: av_kernel(chips, *refs),
            [win_spec] + [piece_spec(0)] * 6 + [own_spec] * 4 + [stat_spec] * 5 + [any_spec] * 6,
            [(own_spec, full)] * 2 + [(far_spec, far)] * 2 + [(piece_spec(1), piece)] * 6,
            (window, *pieces, k_v, v_v, k_f, v_f, stats, *others, *va[4:]),
            scratch=(audio_scratch, bias_scratch, grad_scratch, grad_scratch),
            aliases={17 + i: 4 + i for i in range(6)},
            est=cost(12 * HD * pairs, pairs, 5000000),
        )
        dk_video, dv_video, dk_far, dv_far = av[:4]
        back = av[4:]
        parts = [back[0]] + [move(x, name) for x, name in zip(back[1:], ("aud", "A", "Ax", "B", "Bx"))]

        fars = [move(x, "core") for x in (out_far, dq_far, dk_far, dv_far)]
        out_video, dq_video, dk_video, dv_video, joined = call(
            join_video_kernel,
            [any_spec] * 4 + [far_spec] * 4,
            [(join_spec, full)] * 4 + [(smem, shape((1,), jnp.int32))],
            (out_video, dq_video, dk_video, dv_video, *fars),
            aliases={1 + i: i for i in range(4)},
            est=cost(0, 0, 1600000),
        )
        mine, other = call(
            sum_kernel, [smem] + [whole] * 6 + [smem], [(whole, piece)] * 2, (audio_len, *parts, joined), grid=(),
            est=cost(1000000, 0, 1600000),
        )
        other = move(other, "core")
        dk_audio, dv_audio, dq_audio, out_audio = call(
            join_audio_kernel,
            [whole] * 2,
            [(whole, shape((half, 2 * width), BF))] * 4,
            (mine, other),
            grid=(),
            est=cost(0, 0, 800000),
        )
        return (out_video, out_audio, dq_video, dk_video, dv_video, dq_audio, dk_audio, dv_audio)

    return step


def solution(mesh):
    video, audio = P("vid", "aud"), P(("vid", "aud"), None)
    return jax.shard_map(
        make_body(mesh),
        mesh=mesh,
        in_specs=(video,) * 4 + (audio,) * 4 + (P(), P()),
        out_specs=(video, audio, video, video, video, audio, audio, audio),
        check_vma=False,
    )
```

```python
import jax
import jax.numpy as jnp
from jax import lax
from jax.experimental import pallas as pl
from jax.experimental.pallas import tpu as pltpu
from jax.sharding import PartitionSpec as P


HD = 64
BLK = 64
WMAX = 3
PAIR = 2 * HD
NEG = -1e30
BF = jnp.bfloat16
F32 = jnp.float32


NPOS = 6
KEYS = NPOS * BLK
GROUP = 8


def nt(x, y):
    return lax.dot_general(x, y, (((1,), (1,)), ((), ())), preferred_element_type=F32)


def nn(x, y):
    return lax.dot_general(x, y, (((1,), (0,)), ((), ())), preferred_element_type=F32)


def coords(idx_ref):
    idx = idx_ref[0]
    return idx >> 2, (idx >> 1) & 1, idx & 1


def head_part(x, e):
    lane = lax.broadcasted_iota(jnp.int32, x.shape, 1)
    return jnp.where((lane < HD) if e == 0 else (lane >= HD), x, jnp.zeros_like(x))


def pack_kernel(idx_ref, len_ref, *refs):
    mine, other, keep, send, local, sems = refs[:4], refs[4:8], refs[8], refs[9], refs[10], refs[11]
    c, r, a = coords(idx_ref)
    copies = [pltpu.make_async_copy(src, local.at[n], sems.at[n]) for n, src in enumerate(mine)]
    for copy in copies:
        copy.start()
    for copy in copies:
        copy.wait()
    mine = [local.at[n] for n in range(4)]
    half, quarter = keep.shape[2], keep.shape[3]
    row = lax.broadcasted_iota(jnp.int32, (half, quarter), 0) + a * half
    for slot, arrays in ((r, mine), (1 - r, other)):
        valid = row < len_ref[2 * c + slot]
        for n, ref in enumerate(arrays):
            for part, out in ((a, keep), (1 - a, send)):
                col = pl.multiple_of((2 * part + r) * quarter, 128)
                x = ref[:, pl.ds(col, quarter)]
                if n == 0:
                    x = x * jnp.asarray(HD**-0.5, BF)
                if n == 1:
                    x = jnp.where(valid, x, jnp.zeros_like(x))
                out[n, slot] = x


def piece_rows(idx_ref):
    c, _, a = coords(idx_ref)
    half = BLK // 2
    side = 2 - 2 * (c & 1)
    starts = []
    for place, part in ((1, a), (1, 1 - a), (side, a), (side, 1 - a), (2 - side, a), (2 - side, 1 - a)):
        first = place * 2 * BLK + part * half
        starts.append([pl.multiple_of(first + core * BLK, half) for core in range(2)])
    return starts


def gather_audio(idx_ref, pieces, dst):
    half = BLK // 2
    for ref, firsts in zip(pieces, piece_rows(idx_ref)):
        for core, first in enumerate(firsts):
            for n in range(2):
                dst[n, pl.ds(first, half), :] = ref[n, core]


def scatter_audio(idx_ref, src, pieces):
    half = BLK // 2
    for ref, firsts in zip(pieces, piece_rows(idx_ref)):
        for core, first in enumerate(firsts):
            for n in range(2):
                ref[n, core] = src[n, pl.ds(first, half), :].astype(ref.dtype)


def window_bounds(win_ref, c, stretch, shape, axis):
    block = lax.broadcasted_iota(jnp.int32, shape, axis) // BLK
    lo = jnp.zeros(shape, jnp.int32)
    hi = jnp.zeros(shape, jnp.int32)
    for b in range(4):
        start = win_ref[4 * stretch + b, 0] - (2 * c - 2)
        count = win_ref[4 * stretch + b, 1]
        lo = jnp.where(block == b, start, lo)
        hi = jnp.where(block == b, start + count, hi)
    return lo, hi


def window_of(idx_ref, win_ref, stretch, b):
    c, _, _ = coords(idx_ref)
    return win_ref[4 * stretch + b, 0] - (2 * c - 2), win_ref[4 * stretch + b, 1]


def block_bias(idx_ref, win_ref, len_ref, bias):
    c, r, _ = coords(idx_ref)
    row = lax.broadcasted_iota(jnp.int32, bias.shape[1:], 0)
    for i, stretch in enumerate((r, 1 - r)):
        for b in range(4):
            start, count = window_of(idx_ref, win_ref, stretch, b)
            keep = row < count * BLK
            if len_ref is not None:
                length = jnp.zeros(row.shape, jnp.int32)
                for j in range(WMAX):
                    block = jnp.clip(2 * c - 2 + start + j, 0, len_ref.shape[0] - 1)
                    length = jnp.where(row // BLK == j, len_ref[block], length)
                keep = keep & (row % BLK < length)
            bias[4 * i + b] = jnp.where(keep, 0.0, NEG)


def both_heads(x):
    return jnp.concatenate([head_part(x, 0), head_part(x, 1)], axis=0)


def own_heads(x):
    lane = lax.broadcasted_iota(jnp.int32, (BLK, PAIR), 1)
    return jnp.where(lane < HD, x[:BLK], x[BLK:])


def block_groups(r):
    blocks = [(i, stretch, b) for b in range(4) for i, stretch in enumerate((r, 1 - r))]
    return [blocks[n : n + GROUP] for n in range(0, 8, GROUP)]


def tn(x, y):
    return lax.dot_general(x, y, (((0,), (0,)), ((), ())), preferred_element_type=F32)


def group_places(c):
    side = 2 - 2 * (c & 1)
    return 1, side, 2 - side


def group_bias(idx_ref, win_ref, groups, bias):
    c, r, _ = coords(idx_ref)
    places = group_places(c)
    shape = bias.shape[1:]
    lane = lax.broadcasted_iota(jnp.int32, shape, 1)
    place = jnp.zeros(shape, jnp.int32)
    for n, group in enumerate(groups):
        place = jnp.where(lane // PAIR == n, 2 * places[group], place)
    place = place + (lane % PAIR) // BLK
    for i, stretch in enumerate((r, 1 - r)):
        lo, hi = window_bounds(win_ref, c, stretch, shape, 0)
        bias[i] = jnp.where((place >= lo) & (place < hi), 0.0, NEG)


def stats_kernel(groups, idx_ref, win_ref, *refs):
    count = len(groups)
    pieces, refs = refs[: 2 * count], refs[2 * count :]
    video, refs = ((refs[0], refs[1]), (refs[2], refs[3])), refs[4:]
    stat_ref, audio, bias = refs[-3:]
    _, _, a = coords(idx_ref)
    half = BLK // 2

    @pl.when(pl.program_id(0) == 0)
    def _():
        group_bias(idx_ref, win_ref, groups, bias)

    for n in range(count):
        for ref, part in ((pieces[2 * n], a), (pieces[2 * n + 1], 1 - a)):
            for core in range(2):
                first = pl.multiple_of(n * PAIR + core * BLK + part * half, half)
                for k in range(2):
                    audio[k, pl.ds(first, half), :] = ref[k, core]
    queries, cot = audio[0], audio[1]
    lses, deltas = [], []
    for e in range(2):
        parts = []
        for i, (k_ref, v_ref) in enumerate(video):
            s = nt(head_part(k_ref[...], e), queries) + bias[i]
            m = jnp.max(s, axis=0, keepdims=True)
            ex = jnp.exp(s - m)
            dp = nt(head_part(v_ref[...], e), cot)
            parts.append((m, jnp.sum(ex, axis=0, keepdims=True), jnp.sum(ex * dp, axis=0, keepdims=True)))
        m = jnp.maximum(parts[0][0], parts[1][0])
        w0, w1 = jnp.exp(parts[0][0] - m), jnp.exp(parts[1][0] - m)
        total = parts[0][1] * w0 + parts[1][1] * w1
        lses.append(m + jnp.log(total))
        deltas.append((parts[0][2] * w0 + parts[1][2] * w1) / total)
    rows = jnp.concatenate(lses + deltas + lses + deltas, axis=0)
    if count == 1:
        rows = jnp.concatenate([refs[0][0, :, :PAIR], rows], axis=1)
    stat_ref[0] = rows


def merge_stats(idx_ref, chips, own_a, own_b, by_a, by_b, by_q, by_q2):
    c, _, _ = coords(idx_ref)
    even = (c & 1) == 0
    has_b = jnp.where(even, c >= 2, c + 2 < chips)
    has_q2 = jnp.where(even, c + 2 < chips, c >= 2)

    def part(x, k, there=None):
        x = x[:, k * PAIR : (k + 1) * PAIR]
        return (x[0:2] if there is None else jnp.where(there, x[0:2], NEG)), x[2:4]

    merged = []
    for group in (
        (part(own_a, 0), part(by_a, 1), part(by_b, 1, has_b)),
        (part(own_a, 1), part(by_a, 0), part(by_q2, 1, has_q2)),
        (part(own_b, 1), part(by_b, 0, has_b), part(by_q, 1, has_b)),
    ):
        m = jnp.maximum(jnp.maximum(group[0][0], group[1][0]), group[2][0])
        ws = [jnp.exp(lse - m) for lse, _ in group]
        total = ws[0] + ws[1] + ws[2]
        merged.append((m + jnp.log(total), sum(wt * d for wt, (_, d) in zip(ws, group)) / total))
    return merged


def va_kernel(idx_ref, win_ref, len_ref, *refs):
    pieces = refs[:6]
    video = ((refs[6], refs[7]), (refs[8], refs[9]))
    outs = ((refs[10], refs[11]), (refs[12], refs[13]))
    back = refs[14:20]
    audio, bias, grads = refs[20:]
    _, r, _ = coords(idx_ref)

    @pl.when(pl.program_id(0) == 0)
    def _():
        block_bias(idx_ref, win_ref, len_ref, bias)

    gather_audio(idx_ref, pieces, audio)
    grads[...] = jnp.zeros(grads.shape, F32)
    scale = jnp.asarray(HD**-0.5, BF)
    for group in block_groups(r):
        work = []
        for i, stretch, b in group:
            start, _ = window_of(idx_ref, win_ref, stretch, b)
            span = pl.ds(pl.multiple_of(start * BLK, BLK), WMAX * BLK)
            rows = slice(b * BLK, (b + 1) * BLK)
            q = both_heads(video[i][0][rows, :] * scale)
            g = both_heads(video[i][1][rows, :])
            keys, values = audio[0, span, :], audio[1, span, :]
            s = nt(keys, q) + bias[4 * i + b]
            dp = nt(values, g)
            work.append((i, rows, span, q, g, keys, values, s, dp))
        done = []
        for i, rows, span, q, g, keys, values, s, dp in work:
            ex = jnp.exp(s - jnp.max(s, axis=0, keepdims=True))
            inv = 1.0 / jnp.sum(ex, axis=0, keepdims=True)
            delta = jnp.sum(ex * dp, axis=0, keepdims=True) * inv
            p = ex * inv
            pb = p.astype(BF)
            ds = (p * (dp - delta)).astype(BF)
            done.append((i, rows, span, nn(ds, q), nn(pb, g), tn(pb, values), tn(ds, keys)))
        for i, rows, span, dk, dv, out, dq in done:
            grads[0, span, :] += dk
            grads[1, span, :] += dv
            outs[i][0][rows, :] = own_heads(out).astype(BF)
            outs[i][1][rows, :] = (own_heads(dq) * HD**-0.5).astype(BF)
    scatter_audio(idx_ref, grads, back)


def av_kernel(chips, idx_ref, win_ref, *refs):
    pieces = refs[:6]
    video = ((refs[6], refs[7]), (refs[8], refs[9]))
    stats = [ref[0] for ref in refs[10:16]]
    outs = ((refs[22], refs[23]), (refs[24], refs[25]))
    back = refs[26:32]
    audio, bias, grads, rowstat = refs[32:]
    c, r, _ = coords(idx_ref)

    @pl.when(pl.program_id(0) == 0)
    def _():
        block_bias(idx_ref, win_ref, None, bias)

    gather_audio(idx_ref, pieces, audio)
    for place, merged in zip(group_places(c), merge_stats(idx_ref, chips, *stats)):
        for n, x in enumerate(merged):
            wide = [jnp.broadcast_to(x[e : e + 1], (HD, PAIR)) for e in range(2)]
            rowstat[n, pl.ds(place * PAIR, PAIR), :] = jnp.concatenate(wide, axis=0).T
    grads[...] = jnp.zeros(grads.shape, F32)
    for group in block_groups(r):
        work = []
        for i, stretch, b in group:
            start, _ = window_of(idx_ref, win_ref, stretch, b)
            span = pl.ds(pl.multiple_of(start * BLK, BLK), WMAX * BLK)
            rows = slice(b * BLK, (b + 1) * BLK)
            keys = both_heads(video[i][0][rows, :])
            values = both_heads(video[i][1][rows, :])
            q, g = audio[0, span, :], audio[1, span, :]
            s = nt(q, keys) + bias[4 * i + b]
            dp = nt(g, values)
            work.append((i, rows, span, keys, values, q, g, s, dp))
        done = []
        for i, rows, span, keys, values, q, g, s, dp in work:
            p = jnp.exp(s - rowstat[0, span, :])
            pb = p.astype(BF)
            ds = (p * (dp - rowstat[1, span, :])).astype(BF)
            done.append((i, rows, span, nn(ds, keys), nn(pb, values), tn(ds, q), tn(pb, g)))
        for i, rows, span, dq, out, dk, dv in done:
            grads[0, span, :] += dq
            grads[1, span, :] += out
            outs[i][0][rows, :] = own_heads(dk).astype(BF)
            outs[i][1][rows, :] = own_heads(dv).astype(BF)
    grads[0] = grads[0] * HD**-0.5
    scatter_audio(idx_ref, grads, back)


def sum_kernel(idx_ref, len_ref, keep, by_aud, by_a, by_ax, by_b, by_bx, after, mine, other):
    c, r, a = coords(idx_ref)
    half, quarter = keep.shape[2], keep.shape[3]
    row = lax.broadcasted_iota(jnp.int32, (half, quarter), 0) + a * half
    for slot, out in ((r, mine), (1 - r, other)):
        valid = row < len_ref[2 * c + slot]
        for part, parts in ((a, (keep, by_a, by_b)), (1 - a, (by_aud, by_ax, by_bx))):
            for n in range(4):
                x = sum(ref[n, slot].astype(F32) for ref in parts)
                if n == 3:
                    x = jnp.where(valid, x, 0.0)
                out[n, part] = x.astype(BF)


def join_audio_kernel(idx_ref, mine, other, *outs):
    _, r, _ = coords(idx_ref)
    quarter = mine.shape[3]
    for n, out in enumerate(outs):
        for part in range(2):
            for core, ref in ((r, mine), (1 - r, other)):
                col = pl.multiple_of((2 * part + core) * quarter, 128)
                out[:, pl.ds(col, quarter)] = ref[n, part]


def join_video_kernel(idx_ref, *refs):
    for src, out in zip(refs[4:8], refs[8:12]):
        out[...] = src[...]
    refs[12][0] = 0


def cost(flops, transcendentals, nbytes):
    return pl.CostEstimate(flops=flops, transcendentals=transcendentals, bytes_accessed=nbytes)


def make_body(mesh):
    nv = mesh.shape["vid"]
    chips = nv // 2
    everyone = [(v, a) for v in range(nv) for a in range(2)]

    def perm(move):
        pairs = []
        for v, a in everyone:
            w, b = move(v, a)
            if 0 <= w < nv:
                pairs.append((2 * v + a, 2 * w + b))
        return pairs

    def diagonal(v):
        return 2 * ((((v >> 1) + 1) ^ 1) - 1) + (v & 1)

    moves = {
        "core": perm(lambda v, a: (v ^ 1, a)),
        "aud": perm(lambda v, a: (v, 1 - a)),
        "A": perm(lambda v, a: (v ^ 2, a)),
        "Ax": perm(lambda v, a: (v ^ 2, 1 - a)),
        "B": perm(lambda v, a: (diagonal(v), a)),
        "Bx": perm(lambda v, a: (diagonal(v), 1 - a)),
        "Q": perm(lambda v, a: (v - 4 if v & 2 else v + 4, a)),
        "Q2": perm(lambda v, a: (v + 4 if v & 2 else v - 4, a)),
    }

    def move(x, name):
        return lax.ppermute(x, ("vid", "aud"), moves[name])

    def step(q_v, k_v, v_v, g_v, q_a, k_a, v_a, g_a, window, audio_len):
        rows, width = q_v.shape
        quarter = width // 2
        half = q_a.shape[0]
        steps = quarter // PAIR
        idx = jnp.reshape(2 * lax.axis_index("vid") + lax.axis_index("aud"), (1,)).astype(jnp.int32)
        shape = jax.ShapeDtypeStruct

        smem = pl.BlockSpec(memory_space=pltpu.SMEM)
        win_spec = pl.BlockSpec((8, 2), lambda h, i: (i[0] >> 2, 0), memory_space=pltpu.SMEM)
        len_spec = pl.BlockSpec(memory_space=pltpu.SMEM)

        def piece_spec(n):
            return pl.BlockSpec((2, 2, half, PAIR), lambda h, i: (n, 0, 0, h))

        own_spec = pl.BlockSpec((rows, PAIR), lambda h, i: (0, ((i[0] >> 1) & 1) * steps + h))
        far_spec = pl.BlockSpec((rows, PAIR), lambda h, i: (0, h))
        join_spec = pl.BlockSpec((rows, PAIR), lambda h, i: (0, (1 - ((i[0] >> 1) & 1)) * steps + h))
        stat_spec = pl.BlockSpec((1, 8, 2 * PAIR), lambda h, i: (h, 0, 0))
        any_spec = pl.BlockSpec(memory_space=pl.ANY)
        hbm = pl.BlockSpec(memory_space=pltpu.HBM)

        def call(kernel, ins, outs, args, grid=(steps,), scratch=(), aliases=None, est=None):
            return pl.pallas_call(
                kernel,
                grid_spec=pltpu.PrefetchScalarGridSpec(
                    num_scalar_prefetch=1,
                    grid=grid,
                    in_specs=ins,
                    out_specs=[s for s, _ in outs],
                    scratch_shapes=list(scratch),
                ),
                out_shape=[o for _, o in outs],
                input_output_aliases=aliases or {},
                cost_estimate=est,
                compiler_params=pltpu.CompilerParams(vmem_limit_bytes=24 << 20),
            )(idx, *args)

        audio = (q_a, g_a, k_a, v_a)
        audio_other = [move(x, "core") for x in audio]
        piece = shape((4, 2, half, quarter), BF)
        whole = pl.BlockSpec(memory_space=pltpu.VMEM)
        keep, send = call(
            pack_kernel, [smem] + [hbm] * 4 + [whole] * 4, [(whole, piece)] * 2, (audio_len, *[pltpu.with_memory_space_constraint(x, pltpu.HBM) for x in audio], *audio_other), grid=(),
            scratch=(pltpu.VMEM((4, half, 2 * width), BF), pltpu.SemaphoreType.DMA((4,))),
            est=cost(0, 0, 1200000),
        )
        pieces = [keep, move(send, "aud"), move(keep, "A"), move(send, "Ax"), move(keep, "B"), move(send, "Bx")]
        k_f, v_f, q_f, g_f = [move(x, "core") for x in (k_v, v_v, q_v, g_v)]

        audio_scratch = pltpu.VMEM((2, KEYS, PAIR), BF)
        grad_scratch = pltpu.VMEM((2, KEYS, PAIR), F32)
        bias_scratch = pltpu.VMEM((8, WMAX * BLK, PAIR), F32)
        pairs = 2 * steps * 2 * rows * KEYS

        stat = shape((steps, 8, 2 * PAIR), F32)

        def find_stats(groups, before):
            lanes = len(groups) * PAIR
            (found,) = call(
                lambda *refs: stats_kernel(groups, *refs),
                [win_spec] + [piece_spec(0)] * (2 * len(groups)) + [own_spec] * 4 + [stat_spec] * len(before),
                [(stat_spec, stat)],
                (window, *[pieces[2 * g + n] for g in groups for n in range(2)], k_v, v_v, k_f, v_f, *before),
                scratch=(pltpu.VMEM((2, lanes, PAIR), BF), pltpu.VMEM((2, rows, lanes), F32)),
                est=cost(4 * HD * pairs * lanes // KEYS, pairs * lanes // KEYS, 2000000),
            )
            return found

        stats_a = find_stats((0, 1), ())
        by_a, by_q = move(stats_a, "A"), move(stats_a, "Q")
        stats_b = find_stats((2,), (stats_a,))
        by_b, by_q2 = move(stats_b, "B"), move(stats_b, "Q2")

        full, far = shape((rows, width), BF), shape((rows, quarter), BF)
        va = call(
            va_kernel,
            [win_spec, len_spec] + [piece_spec(1)] * 6 + [own_spec] * 4,
            [(own_spec, full)] * 2 + [(far_spec, far)] * 2 + [(piece_spec(0), piece)] * 6,
            (window, audio_len, *pieces, q_v, g_v, q_f, g_f),
            scratch=(audio_scratch, bias_scratch, grad_scratch),
            est=cost(10 * HD * pairs, pairs, 5000000),
        )
        out_video, dq_video, out_far, dq_far = va[:4]
        av = call(
            lambda *refs: av_kernel(chips, *refs),
            [win_spec] + [piece_spec(0)] * 6 + [own_spec] * 4 + [stat_spec] * 6 + [any_spec] * 6,
            [(own_spec, full)] * 2 + [(far_spec, far)] * 2 + [(piece_spec(1), piece)] * 6,
            (window, *pieces, k_v, v_v, k_f, v_f, stats_a, stats_b, by_a, by_b, by_q, by_q2, *va[4:]),
            scratch=(audio_scratch, bias_scratch, grad_scratch, grad_scratch),
            aliases={18 + i: 4 + i for i in range(6)},
            est=cost(12 * HD * pairs, pairs, 5000000),
        )
        dk_video, dv_video, dk_far, dv_far = av[:4]
        back = av[4:]
        parts = [back[0]] + [move(x, name) for x, name in zip(back[1:], ("aud", "A", "Ax", "B", "Bx"))]

        fars = [move(x, "core") for x in (out_far, dq_far, dk_far, dv_far)]
        out_video, dq_video, dk_video, dv_video, joined = call(
            join_video_kernel,
            [any_spec] * 4 + [far_spec] * 4,
            [(join_spec, full)] * 4 + [(smem, shape((1,), jnp.int32))],
            (out_video, dq_video, dk_video, dv_video, *fars),
            aliases={1 + i: i for i in range(4)},
            est=cost(0, 0, 1600000),
        )
        mine, other = call(
            sum_kernel, [smem] + [whole] * 6 + [smem], [(whole, piece)] * 2, (audio_len, *parts, joined), grid=(),
            est=cost(1000000, 0, 1600000),
        )
        other = move(other, "core")
        dk_audio, dv_audio, dq_audio, out_audio = call(
            join_audio_kernel,
            [whole] * 2,
            [(whole, shape((half, 2 * width), BF))] * 4,
            (mine, other),
            grid=(),
            est=cost(0, 0, 800000),
        )
        return (out_video, out_audio, dq_video, dk_video, dv_video, dq_audio, dk_audio, dv_audio)

    return step


def solution(mesh):
    video, audio = P("vid", "aud"), P(("vid", "aud"), None)
    return jax.shard_map(
        make_body(mesh),
        mesh=mesh,
        in_specs=(video,) * 4 + (audio,) * 4 + (P(), P()),
        out_specs=(video, audio, video, video, video, audio, audio, audio),
        check_vma=False,
    )
```

```python
import jax
import jax.numpy as jnp
from jax import lax
from jax.experimental import pallas as pl
from jax.experimental.pallas import tpu as pltpu
from jax.sharding import PartitionSpec as P


HD = 64
BLK = 64
WMAX = 3
PAIR = 2 * HD
NEG = -1e30
BF = jnp.bfloat16
F32 = jnp.float32


NPOS = 6
KEYS = NPOS * BLK
GROUP = 8


def nt(x, y):
    return lax.dot_general(x, y, (((1,), (1,)), ((), ())), preferred_element_type=F32)


def nn(x, y):
    return lax.dot_general(x, y, (((1,), (0,)), ((), ())), preferred_element_type=F32)


def coords(idx_ref):
    idx = idx_ref[0]
    return idx >> 2, (idx >> 1) & 1, idx & 1


def head_part(x, e):
    lane = lax.broadcasted_iota(jnp.int32, x.shape, 1)
    return jnp.where((lane < HD) if e == 0 else (lane >= HD), x, jnp.zeros_like(x))


def pack_kernel(idx_ref, len_ref, *refs):
    mine, other, keep, send, local, sems = refs[:4], refs[4:8], refs[8], refs[9], refs[10], refs[11]
    c, r, a = coords(idx_ref)
    copies = [pltpu.make_async_copy(src, local.at[n], sems.at[n]) for n, src in enumerate(mine)]
    for copy in copies:
        copy.start()
    for copy in copies:
        copy.wait()
    mine = [local.at[n] for n in range(4)]
    half, quarter = keep.shape[2], keep.shape[3]
    row = lax.broadcasted_iota(jnp.int32, (half, quarter), 0) + a * half
    for slot, arrays in ((r, mine), (1 - r, other)):
        valid = row < len_ref[2 * c + slot]
        for n, ref in enumerate(arrays):
            for part, out in ((a, keep), (1 - a, send)):
                col = pl.multiple_of((2 * part + r) * quarter, 128)
                x = ref[:, pl.ds(col, quarter)]
                if n == 0:
                    x = x * jnp.asarray(HD**-0.5, BF)
                if n == 1:
                    x = jnp.where(valid, x, jnp.zeros_like(x))
                out[n, slot] = x


def piece_rows(idx_ref):
    c, _, a = coords(idx_ref)
    half = BLK // 2
    side = 2 - 2 * (c & 1)
    starts = []
    for place, part in ((1, a), (1, 1 - a), (side, a), (side, 1 - a), (2 - side, a), (2 - side, 1 - a)):
        first = place * 2 * BLK + part * half
        starts.append([pl.multiple_of(first + core * BLK, half) for core in range(2)])
    return starts


def gather_audio(idx_ref, pieces, arrays, dst):
    half = BLK // 2
    for ref, firsts in zip(pieces, piece_rows(idx_ref)):
        for core, first in enumerate(firsts):
            for n, k in enumerate(arrays):
                dst[n, pl.ds(first, half), :] = ref[k, core]


def scatter_audio(idx_ref, sources, pieces):
    half = BLK // 2
    for ref, firsts in zip(pieces, piece_rows(idx_ref)):
        for core, first in enumerate(firsts):
            for n, src in enumerate(sources):
                ref[n, core] = src[n % 2, pl.ds(first, half), :]


def pair_cols(idx_ref, h, quarter):
    _, r, _ = coords(idx_ref)
    col = pl.multiple_of(h * PAIR, PAIR)
    return pl.ds(col, PAIR), pl.ds(pl.multiple_of(r * quarter + col, PAIR), PAIR)


def window_bounds(win_ref, c, stretch, shape, axis):
    block = lax.broadcasted_iota(jnp.int32, shape, axis) // BLK
    lo = jnp.zeros(shape, jnp.int32)
    hi = jnp.zeros(shape, jnp.int32)
    for b in range(4):
        start = win_ref[4 * stretch + b, 0] - (2 * c - 2)
        count = win_ref[4 * stretch + b, 1]
        lo = jnp.where(block == b, start, lo)
        hi = jnp.where(block == b, start + count, hi)
    return lo, hi


def window_of(idx_ref, win_ref, stretch, b):
    c, _, _ = coords(idx_ref)
    return win_ref[4 * stretch + b, 0] - (2 * c - 2), win_ref[4 * stretch + b, 1]


def block_bias(idx_ref, win_ref, len_ref, bias):
    c, r, _ = coords(idx_ref)
    row = lax.broadcasted_iota(jnp.int32, bias.shape[1:], 0)
    for i, stretch in enumerate((r, 1 - r)):
        for b in range(4):
            start, count = window_of(idx_ref, win_ref, stretch, b)
            keep = row < count * BLK
            if len_ref is not None:
                length = jnp.zeros(row.shape, jnp.int32)
                for j in range(WMAX):
                    block = jnp.clip(2 * c - 2 + start + j, 0, len_ref.shape[0] - 1)
                    length = jnp.where(row // BLK == j, len_ref[block], length)
                keep = keep & (row % BLK < length)
            bias[4 * i + b] = jnp.where(keep, 0.0, NEG)


def both_heads(x):
    return jnp.concatenate([head_part(x, 0), head_part(x, 1)], axis=0)


def own_heads(x):
    lane = lax.broadcasted_iota(jnp.int32, (BLK, PAIR), 1)
    return jnp.where(lane < HD, x[:BLK], x[BLK:])


def block_groups(r):
    blocks = [(i, stretch, b) for b in range(4) for i, stretch in enumerate((r, 1 - r))]
    return [blocks[n : n + GROUP] for n in range(0, 8, GROUP)]


def tn(x, y):
    return lax.dot_general(x, y, (((0,), (0,)), ((), ())), preferred_element_type=F32)


def group_places(c):
    side = 2 - 2 * (c & 1)
    return 1, side, 2 - side


def group_bias(idx_ref, win_ref, groups, bias):
    c, r, _ = coords(idx_ref)
    places = group_places(c)
    shape = bias.shape[1:]
    lane = lax.broadcasted_iota(jnp.int32, shape, 1)
    place = jnp.zeros(shape, jnp.int32)
    for n, group in enumerate(groups):
        place = jnp.where(lane // PAIR == n, 2 * places[group], place)
    place = place + (lane % PAIR) // BLK
    for i, stretch in enumerate((r, 1 - r)):
        lo, hi = window_bounds(win_ref, c, stretch, shape, 0)
        bias[i] = jnp.where((place >= lo) & (place < hi), 0.0, NEG)


def stats_kernel(groups, idx_ref, win_ref, *refs):
    count = len(groups)
    pieces, refs = refs[: 2 * count], refs[2 * count :]
    video, refs = ((refs[0], refs[1]), (refs[2], refs[3])), refs[4:]
    stat_ref, audio, bias = refs[-3:]
    _, _, a = coords(idx_ref)
    half, quarter = BLK // 2, audio.shape[2]
    group_bias(idx_ref, win_ref, groups, bias)
    for n in range(count):
        for ref, part in ((pieces[2 * n], a), (pieces[2 * n + 1], 1 - a)):
            for core in range(2):
                first = pl.multiple_of(n * PAIR + core * BLK + part * half, half)
                for k in range(2):
                    audio[k, pl.ds(first, half), :] = ref[k, core]

    @pl.loop(0, quarter // PAIR)
    def _(h):
        cols, wide_cols = pair_cols(idx_ref, h, quarter)
        queries, cot = audio[0, :, cols], audio[1, :, cols]
        lses, deltas = [], []
        for e in range(2):
            parts = []
            for i, (k_ref, v_ref) in enumerate(video):
                s = nt(head_part(k_ref[:, wide_cols], e), queries) + bias[i]
                m = jnp.max(s, axis=0, keepdims=True)
                ex = jnp.exp(s - m)
                dp = nt(head_part(v_ref[:, wide_cols], e), cot)
                parts.append((m, jnp.sum(ex, axis=0, keepdims=True), jnp.sum(ex * dp, axis=0, keepdims=True)))
            m = jnp.maximum(parts[0][0], parts[1][0])
            w0, w1 = jnp.exp(parts[0][0] - m), jnp.exp(parts[1][0] - m)
            total = parts[0][1] * w0 + parts[1][1] * w1
            lses.append(m + jnp.log(total))
            deltas.append((parts[0][2] * w0 + parts[1][2] * w1) / total)
        rows = jnp.concatenate(lses + deltas + lses + deltas, axis=0)
        if count == 1:
            rows = jnp.concatenate([refs[0][h][:, :PAIR], rows], axis=1)
        stat_ref[h] = rows


def merge_stats(idx_ref, chips, own_a, own_b, by_a, by_b, by_q, by_q2):
    c, _, _ = coords(idx_ref)
    even = (c & 1) == 0
    has_b = jnp.where(even, c >= 2, c + 2 < chips)
    has_q2 = jnp.where(even, c + 2 < chips, c >= 2)

    def part(x, k, there=None):
        x = x[:, k * PAIR : (k + 1) * PAIR]
        return (x[0:2] if there is None else jnp.where(there, x[0:2], NEG)), x[2:4]

    merged = []
    for group in (
        (part(own_a, 0), part(by_a, 1), part(by_b, 1, has_b)),
        (part(own_a, 1), part(by_a, 0), part(by_q2, 1, has_q2)),
        (part(own_b, 1), part(by_b, 0, has_b), part(by_q, 1, has_b)),
    ):
        m = jnp.maximum(jnp.maximum(group[0][0], group[1][0]), group[2][0])
        ws = [jnp.exp(lse - m) for lse, _ in group]
        total = ws[0] + ws[1] + ws[2]
        merged.append((m + jnp.log(total), sum(wt * d for wt, (_, d) in zip(ws, group)) / total))
    return merged


def va_kernel(idx_ref, win_ref, len_ref, *refs):
    pieces = refs[:6]
    video = ((refs[6], refs[7]), (refs[8], refs[9]))
    outs = ((refs[10], refs[11]), (refs[12], refs[13]))
    kv_grads, audio, bias, grads = refs[14:]
    _, r, _ = coords(idx_ref)
    quarter = audio.shape[2]
    block_bias(idx_ref, win_ref, len_ref, bias)
    gather_audio(idx_ref, pieces, (2, 3), audio)
    scale = jnp.asarray(HD**-0.5, BF)

    @pl.loop(0, quarter // PAIR)
    def _(h):
        cols, wide_cols = pair_cols(idx_ref, h, quarter)
        grads[...] = jnp.zeros(grads.shape, F32)
        for group in block_groups(r):
            work = []
            for i, stretch, b in group:
                start, _ = window_of(idx_ref, win_ref, stretch, b)
                span = pl.ds(pl.multiple_of(start * BLK, BLK), WMAX * BLK)
                rows = slice(b * BLK, (b + 1) * BLK)
                q = both_heads(video[i][0][rows, wide_cols] * scale)
                g = both_heads(video[i][1][rows, wide_cols])
                keys, values = audio[0, span, cols], audio[1, span, cols]
                s = nt(keys, q) + bias[4 * i + b]
                dp = nt(values, g)
                work.append((i, rows, span, q, g, keys, values, s, dp))
            done = []
            for i, rows, span, q, g, keys, values, s, dp in work:
                ex = jnp.exp(s - jnp.max(s, axis=0, keepdims=True))
                inv = 1.0 / jnp.sum(ex, axis=0, keepdims=True)
                delta = jnp.sum(ex * dp, axis=0, keepdims=True) * inv
                p = ex * inv
                pb = p.astype(BF)
                ds = (p * (dp - delta)).astype(BF)
                done.append((i, rows, span, nn(ds, q), nn(pb, g), tn(pb, values), tn(ds, keys)))
            for i, rows, span, dk, dv, out, dq in done:
                grads[0, span, :] += dk
                grads[1, span, :] += dv
                outs[i][0][rows, cols] = own_heads(out).astype(BF)
                outs[i][1][rows, cols] = (own_heads(dq) * HD**-0.5).astype(BF)
        for n in range(2):
            kv_grads[n, :, cols] = grads[n].astype(BF)


def av_kernel(chips, idx_ref, win_ref, *refs):
    pieces = refs[:6]
    video = ((refs[6], refs[7]), (refs[8], refs[9]))
    stats, kv_grads = refs[10:16], refs[16]
    outs = ((refs[17], refs[18]), (refs[19], refs[20]))
    back = refs[21:27]
    audio, bias, grads, rowstat, qo_grads = refs[27:]
    c, r, _ = coords(idx_ref)
    quarter = audio.shape[2]
    block_bias(idx_ref, win_ref, None, bias)
    gather_audio(idx_ref, pieces, (0, 1), audio)

    @pl.loop(0, quarter // PAIR)
    def _(h):
        cols, wide_cols = pair_cols(idx_ref, h, quarter)
        for place, merged in zip(group_places(c), merge_stats(idx_ref, chips, *[ref[h] for ref in stats])):
            for n, x in enumerate(merged):
                wide = [jnp.broadcast_to(x[e : e + 1], (HD, PAIR)) for e in range(2)]
                rowstat[n, pl.ds(place * PAIR, PAIR), :] = jnp.concatenate(wide, axis=0).T
        grads[...] = jnp.zeros(grads.shape, F32)
        for group in block_groups(r):
            work = []
            for i, stretch, b in group:
                start, _ = window_of(idx_ref, win_ref, stretch, b)
                span = pl.ds(pl.multiple_of(start * BLK, BLK), WMAX * BLK)
                rows = slice(b * BLK, (b + 1) * BLK)
                keys = both_heads(video[i][0][rows, wide_cols])
                values = both_heads(video[i][1][rows, wide_cols])
                q, g = audio[0, span, cols], audio[1, span, cols]
                s = nt(q, keys) + bias[4 * i + b]
                dp = nt(g, values)
                work.append((i, rows, span, keys, values, q, g, s, dp))
            done = []
            for i, rows, span, keys, values, q, g, s, dp in work:
                p = jnp.exp(s - rowstat[0, span, :])
                pb = p.astype(BF)
                ds = (p * (dp - rowstat[1, span, :])).astype(BF)
                done.append((i, rows, span, nn(ds, keys), nn(pb, values), tn(ds, q), tn(pb, g)))
            for i, rows, span, dq, out, dk, dv in done:
                grads[0, span, :] += dq
                grads[1, span, :] += out
                outs[i][0][rows, cols] = own_heads(dk).astype(BF)
                outs[i][1][rows, cols] = own_heads(dv).astype(BF)
        qo_grads[0, :, cols] = (grads[0] * HD**-0.5).astype(BF)
        qo_grads[1, :, cols] = grads[1].astype(BF)

    scatter_audio(idx_ref, (kv_grads, kv_grads, qo_grads, qo_grads), back)


def sum_kernel(idx_ref, len_ref, keep, by_aud, by_a, by_ax, by_b, by_bx, after, mine, other):
    c, r, a = coords(idx_ref)
    half, quarter = keep.shape[2], keep.shape[3]
    row = lax.broadcasted_iota(jnp.int32, (half, quarter), 0) + a * half
    for slot, out in ((r, mine), (1 - r, other)):
        valid = row < len_ref[2 * c + slot]
        for part, parts in ((a, (keep, by_a, by_b)), (1 - a, (by_aud, by_ax, by_bx))):
            for n in range(4):
                x = sum(ref[n, slot].astype(F32) for ref in parts)
                if n == 3:
                    x = jnp.where(valid, x, 0.0)
                out[n, part] = x.astype(BF)


def join_audio_kernel(idx_ref, mine, other, *outs):
    _, r, _ = coords(idx_ref)
    quarter = mine.shape[3]
    for n, out in enumerate(outs):
        for part in range(2):
            for core, ref in ((r, mine), (1 - r, other)):
                col = pl.multiple_of((2 * part + core) * quarter, 128)
                out[:, pl.ds(col, quarter)] = ref[n, part]


def join_video_kernel(idx_ref, *refs):
    _, r, _ = coords(idx_ref)
    quarter = refs[0].shape[1]
    for own, far, out in zip(refs[:4], refs[4:8], refs[8:12]):
        for core, src in ((r, own), (1 - r, far)):
            out[:, pl.ds(pl.multiple_of(core * quarter, PAIR), quarter)] = src[...]
    refs[12][0] = 0


def cost(flops, transcendentals, nbytes):
    return pl.CostEstimate(flops=flops, transcendentals=transcendentals, bytes_accessed=nbytes)


def make_body(mesh):
    nv = mesh.shape["vid"]
    chips = nv // 2
    everyone = [(v, a) for v in range(nv) for a in range(2)]

    def perm(move):
        pairs = []
        for v, a in everyone:
            w, b = move(v, a)
            if 0 <= w < nv:
                pairs.append((2 * v + a, 2 * w + b))
        return pairs

    def diagonal(v):
        return 2 * ((((v >> 1) + 1) ^ 1) - 1) + (v & 1)

    moves = {
        "core": perm(lambda v, a: (v ^ 1, a)),
        "aud": perm(lambda v, a: (v, 1 - a)),
        "A": perm(lambda v, a: (v ^ 2, a)),
        "Ax": perm(lambda v, a: (v ^ 2, 1 - a)),
        "B": perm(lambda v, a: (diagonal(v), a)),
        "Bx": perm(lambda v, a: (diagonal(v), 1 - a)),
        "Q": perm(lambda v, a: (v - 4 if v & 2 else v + 4, a)),
        "Q2": perm(lambda v, a: (v + 4 if v & 2 else v - 4, a)),
    }

    def move(x, name):
        return lax.ppermute(x, ("vid", "aud"), moves[name])

    def step(q_v, k_v, v_v, g_v, q_a, k_a, v_a, g_a, window, audio_len):
        rows, width = q_v.shape
        quarter = width // 2
        half = q_a.shape[0]
        steps = quarter // PAIR
        idx = jnp.reshape(2 * lax.axis_index("vid") + lax.axis_index("aud"), (1,)).astype(jnp.int32)
        shape = jax.ShapeDtypeStruct

        smem = pl.BlockSpec(memory_space=pltpu.SMEM)
        win_spec = pl.BlockSpec((8, 2), lambda g, i: (i[0] >> 2, 0), memory_space=pltpu.SMEM)
        len_spec = smem
        whole = pl.BlockSpec(memory_space=pltpu.VMEM)
        hbm = pl.BlockSpec(memory_space=pltpu.HBM)

        def call(kernel, ins, outs, args, grid=(1,), scratch=(), est=None):
            return pl.pallas_call(
                kernel,
                grid_spec=pltpu.PrefetchScalarGridSpec(
                    num_scalar_prefetch=1,
                    grid=grid,
                    in_specs=ins,
                    out_specs=[s for s, _ in outs],
                    scratch_shapes=list(scratch),
                ),
                out_shape=[o for _, o in outs],
                cost_estimate=est,
                compiler_params=pltpu.CompilerParams(vmem_limit_bytes=24 << 20),
            )(idx, *args)

        audio = (q_a, g_a, k_a, v_a)
        audio_other = [move(x, "core") for x in audio]
        piece = shape((4, 2, half, quarter), BF)
        keep, send = call(
            pack_kernel, [smem] + [hbm] * 4 + [whole] * 4, [(whole, piece)] * 2, (audio_len, *[pltpu.with_memory_space_constraint(x, pltpu.HBM) for x in audio], *audio_other), grid=(),
            scratch=(pltpu.VMEM((4, half, 2 * width), BF), pltpu.SemaphoreType.DMA((4,))),
            est=cost(0, 0, 1200000),
        )
        pieces = [keep, move(send, "aud"), move(keep, "A"), move(send, "Ax"), move(keep, "B"), move(send, "Bx")]
        k_f, v_f, q_f, g_f = [move(x, "core") for x in (k_v, v_v, q_v, g_v)]

        audio_scratch = pltpu.VMEM((2, KEYS, quarter), BF)
        grad_scratch = pltpu.VMEM((2, KEYS, PAIR), F32)
        bias_scratch = pltpu.VMEM((8, WMAX * BLK, PAIR), F32)
        pairs = 2 * steps * 2 * rows * KEYS

        stat = shape((steps, 8, 2 * PAIR), F32)

        def find_stats(groups, before):
            lanes = len(groups) * PAIR
            (found,) = call(
                lambda *refs: stats_kernel(groups, *refs),
                [win_spec] + [whole] * (2 * len(groups) + 4 + len(before)),
                [(whole, stat)],
                (window, *[pieces[2 * g + n] for g in groups for n in range(2)], k_v, v_v, k_f, v_f, *before),
                scratch=(pltpu.VMEM((2, lanes, quarter), BF), pltpu.VMEM((2, rows, lanes), F32)),
                est=cost(4 * HD * pairs * lanes // KEYS, pairs * lanes // KEYS, 2000000),
            )
            return found

        stats_a = find_stats((0, 1), ())
        by_a, by_q = move(stats_a, "A"), move(stats_a, "Q")
        stats_b = find_stats((2,), (stats_a,))
        by_b, by_q2 = move(stats_b, "B"), move(stats_b, "Q2")

        full, part = shape((rows, width), BF), shape((rows, quarter), BF)
        out_own, dq_own, out_far, dq_far, kv_grads = call(
            va_kernel,
            [win_spec, len_spec] + [whole] * 10,
            [(whole, part)] * 4 + [(whole, shape((2, KEYS, quarter), BF))],
            (window, audio_len, *pieces, q_v, g_v, q_f, g_f),
            scratch=(audio_scratch, bias_scratch, grad_scratch),
            est=cost(10 * HD * pairs, pairs, 5000000),
        )
        dk_own, dv_own, dk_far, dv_far, *back = call(
            lambda *refs: av_kernel(chips, *refs),
            [win_spec] + [whole] * 17,
            [(whole, part)] * 4 + [(whole, piece)] * 6,
            (window, *pieces, k_v, v_v, k_f, v_f, stats_a, stats_b, by_a, by_b, by_q, by_q2, kv_grads),
            scratch=(audio_scratch, bias_scratch, grad_scratch, grad_scratch, audio_scratch),
            est=cost(12 * HD * pairs, pairs, 5000000),
        )
        parts = [back[0]] + [move(x, name) for x, name in zip(back[1:], ("aud", "A", "Ax", "B", "Bx"))]

        fars = [move(x, "core") for x in (out_far, dq_far, dk_far, dv_far)]
        out_video, dq_video, dk_video, dv_video, joined = call(
            join_video_kernel,
            [whole] * 8,
            [(whole, full)] * 4 + [(smem, shape((1,), jnp.int32))],
            (out_own, dq_own, dk_own, dv_own, *fars),
            est=cost(0, 0, 1600000),
        )
        mine, other = call(
            sum_kernel, [smem] + [whole] * 6 + [smem], [(whole, piece)] * 2, (audio_len, *parts, joined), grid=(),
            est=cost(1000000, 0, 1600000),
        )
        other = move(other, "core")
        dk_audio, dv_audio, dq_audio, out_audio = call(
            join_audio_kernel,
            [whole] * 2,
            [(whole, shape((half, 2 * width), BF))] * 4,
            (mine, other),
            grid=(),
            est=cost(0, 0, 800000),
        )
        return (out_video, out_audio, dq_video, dk_video, dv_video, dq_audio, dk_audio, dv_audio)

    return step


def solution(mesh):
    video, audio = P("vid", "aud"), P(("vid", "aud"), None)
    return jax.shard_map(
        make_body(mesh),
        mesh=mesh,
        in_specs=(video,) * 4 + (audio,) * 4 + (P(), P()),
        out_specs=(video, audio, video, video, video, audio, audio, audio),
        check_vma=False,
    )
```

```python
import jax
import jax.numpy as jnp
from jax import lax
from jax.experimental import pallas as pl
from jax.experimental.pallas import tpu as pltpu
from jax.sharding import PartitionSpec as P


HD = 64
BLK = 64
WMAX = 3
PAIR = 2 * HD
NEG = -1e30
BF = jnp.bfloat16
F32 = jnp.float32


NPOS = 6
KEYS = NPOS * BLK
GROUP = 8


def nt(x, y):
    return lax.dot_general(x, y, (((1,), (1,)), ((), ())), preferred_element_type=F32)


def nn(x, y):
    return lax.dot_general(x, y, (((1,), (0,)), ((), ())), preferred_element_type=F32)


def coords(idx_ref):
    idx = idx_ref[0]
    return idx >> 2, (idx >> 1) & 1, idx & 1


def head_part(x, e):
    lane = lax.broadcasted_iota(jnp.int32, x.shape, 1)
    return jnp.where((lane < HD) if e == 0 else (lane >= HD), x, jnp.zeros_like(x))


def load_kernel(idx_ref, *refs):
    srcs, dst, sems = refs[:4], refs[4], refs[5]
    copies = [pltpu.make_async_copy(src, dst.at[n], sems.at[n]) for n, src in enumerate(srcs)]
    for copy in copies:
        copy.start()
    for copy in copies:
        copy.wait()


def pack_kernel(idx_ref, len_ref, mine, *refs):
    other, (keep, send, carry) = refs[:4], refs[4:]
    c, r, a = coords(idx_ref)
    half, quarter = keep.shape[2], keep.shape[3]
    row = lax.broadcasted_iota(jnp.int32, (half, quarter), 0) + a * half
    carried = a ^ r
    for slot, arrays in ((r, [mine.at[n] for n in range(4)]), (1 - r, other)):
        valid = row < len_ref[2 * c + slot]
        for n, ref in enumerate(arrays):

            def part(which, core):
                col = pl.multiple_of((2 * which + core) * quarter, 128)
                x = ref[:, pl.ds(col, quarter)]
                if n == 0:
                    x = x * jnp.asarray(HD**-0.5, BF)
                if n == 1:
                    x = jnp.where(valid, x, jnp.zeros_like(x))
                return x

            keep[n, slot] = part(a, r)
            send[n, slot] = part(1 - a, r)
            carry[0, n, slot] = part(carried, r)
            carry[1, n, slot] = part(carried, 1 - r)


def piece_rows(idx_ref, swapped):
    c, r, a = coords(idx_ref)
    last = (a ^ r) if swapped else a
    half = BLK // 2
    side = 2 - 2 * (c & 1)
    starts = []
    for place, part in ((1, a), (1, 1 - a), (side, a), (side, 1 - a), (2 - side, last), (2 - side, 1 - last)):
        first = place * 2 * BLK + part * half
        starts.append([pl.multiple_of(first + core * BLK, half) for core in range(2)])
    return starts


def piece_views(pieces):
    return [*pieces[:-2], pieces[-2].at[0], pieces[-1].at[1]]


def gather_audio(idx_ref, pieces, arrays, dst):
    half = BLK // 2
    for ref, firsts in zip(piece_views(pieces), piece_rows(idx_ref, True)):
        for core, first in enumerate(firsts):
            for n, k in enumerate(arrays):
                dst[n, pl.ds(first, half), :] = ref[k, core]


def scatter_audio(idx_ref, sources, pieces):
    half = BLK // 2
    for ref, firsts in zip(pieces, piece_rows(idx_ref, False)):
        for core, first in enumerate(firsts):
            for n, src in enumerate(sources):
                ref[n, core] = src[n % 2, pl.ds(first, half), :]


def pair_cols(idx_ref, h, quarter):
    _, r, _ = coords(idx_ref)
    col = pl.multiple_of(h * PAIR, PAIR)
    return pl.ds(col, PAIR), pl.ds(pl.multiple_of(r * quarter + col, PAIR), PAIR)


def window_bounds(win_ref, c, stretch, shape, axis):
    block = lax.broadcasted_iota(jnp.int32, shape, axis) // BLK
    lo = jnp.zeros(shape, jnp.int32)
    hi = jnp.zeros(shape, jnp.int32)
    for b in range(4):
        start = win_ref[4 * stretch + b, 0] - (2 * c - 2)
        count = win_ref[4 * stretch + b, 1]
        lo = jnp.where(block == b, start, lo)
        hi = jnp.where(block == b, start + count, hi)
    return lo, hi


def window_of(idx_ref, win_ref, stretch, b):
    c, _, _ = coords(idx_ref)
    return win_ref[4 * stretch + b, 0] - (2 * c - 2), win_ref[4 * stretch + b, 1]


def block_bias(idx_ref, win_ref, len_ref, bias):
    c, r, _ = coords(idx_ref)
    row = lax.broadcasted_iota(jnp.int32, bias.shape[1:], 0)
    for i, stretch in enumerate((r, 1 - r)):
        for b in range(4):
            start, count = window_of(idx_ref, win_ref, stretch, b)
            keep = row < count * BLK
            if len_ref is not None:
                length = jnp.zeros(row.shape, jnp.int32)
                for j in range(WMAX):
                    block = jnp.clip(2 * c - 2 + start + j, 0, len_ref.shape[0] - 1)
                    length = jnp.where(row // BLK == j, len_ref[block], length)
                keep = keep & (row % BLK < length)
            bias[4 * i + b] = jnp.where(keep, 0.0, NEG)


def both_heads(x):
    return jnp.concatenate([head_part(x, 0), head_part(x, 1)], axis=0)


def own_heads(x):
    lane = lax.broadcasted_iota(jnp.int32, (BLK, PAIR), 1)
    return jnp.where(lane < HD, x[:BLK], x[BLK:])


def block_groups(r):
    blocks = [(i, stretch, b) for b in range(4) for i, stretch in enumerate((r, 1 - r))]
    return [blocks[n : n + GROUP] for n in range(0, 8, GROUP)]


def tn(x, y):
    return lax.dot_general(x, y, (((0,), (0,)), ((), ())), preferred_element_type=F32)


def group_places(c):
    side = 2 - 2 * (c & 1)
    return 1, side, 2 - side


def group_bias(idx_ref, win_ref, groups, bias):
    c, r, _ = coords(idx_ref)
    places = group_places(c)
    shape = bias.shape[1:]
    lane = lax.broadcasted_iota(jnp.int32, shape, 1)
    place = jnp.zeros(shape, jnp.int32)
    for n, group in enumerate(groups):
        place = jnp.where(lane // PAIR == n, 2 * places[group], place)
    place = place + (lane % PAIR) // BLK
    for i, stretch in enumerate((r, 1 - r)):
        lo, hi = window_bounds(win_ref, c, stretch, shape, 0)
        bias[i] = jnp.where((place >= lo) & (place < hi), 0.0, NEG)


def stats_kernel(groups, idx_ref, win_ref, *refs):
    count = len(groups)
    pieces, refs = refs[: 2 * count], refs[2 * count :]
    video, refs = ((refs[0], refs[1]), (refs[2], refs[3])), refs[4:]
    stat_ref, audio, bias = refs[-3:]
    _, r, a = coords(idx_ref)
    half, quarter = BLK // 2, audio.shape[2]
    if 2 in groups:
        pieces = piece_views(pieces)
    group_bias(idx_ref, win_ref, groups, bias)
    for n in range(count):
        first_part = (a ^ r) if groups[n] == 2 else a
        for ref, part in ((pieces[2 * n], first_part), (pieces[2 * n + 1], 1 - first_part)):
            for core in range(2):
                first = pl.multiple_of(n * PAIR + core * BLK + part * half, half)
                for k in range(2):
                    audio[k, pl.ds(first, half), :] = ref[k, core]

    @pl.loop(0, quarter // PAIR)
    def _(h):
        cols, wide_cols = pair_cols(idx_ref, h, quarter)
        queries, cot = audio[0, :, cols], audio[1, :, cols]
        lses, deltas = [], []
        for e in range(2):
            parts = []
            for i, (k_ref, v_ref) in enumerate(video):
                s = nt(head_part(k_ref[:, wide_cols], e), queries) + bias[i]
                m = jnp.max(s, axis=0, keepdims=True)
                ex = jnp.exp(s - m)
                dp = nt(head_part(v_ref[:, wide_cols], e), cot)
                parts.append((m, jnp.sum(ex, axis=0, keepdims=True), jnp.sum(ex * dp, axis=0, keepdims=True)))
            m = jnp.maximum(parts[0][0], parts[1][0])
            w0, w1 = jnp.exp(parts[0][0] - m), jnp.exp(parts[1][0] - m)
            total = parts[0][1] * w0 + parts[1][1] * w1
            lses.append(m + jnp.log(total))
            deltas.append((parts[0][2] * w0 + parts[1][2] * w1) / total)
        rows = jnp.concatenate(lses + deltas + lses + deltas, axis=0)
        if count == 1:
            rows = jnp.concatenate([refs[0][h][:, :PAIR], rows], axis=1)
        stat_ref[h] = rows


def merge_stats(idx_ref, chips, own_a, own_b, by_a, by_b, by_q, by_q2):
    c, _, _ = coords(idx_ref)
    even = (c & 1) == 0
    has_b = jnp.where(even, c >= 2, c + 2 < chips)
    has_q2 = jnp.where(even, c + 2 < chips, c >= 2)

    def part(x, k, there=None):
        x = x[:, k * PAIR : (k + 1) * PAIR]
        return (x[0:2] if there is None else jnp.where(there, x[0:2], NEG)), x[2:4]

    merged = []
    for group in (
        (part(own_a, 0), part(by_a, 1), part(by_b, 1, has_b)),
        (part(own_a, 1), part(by_a, 0), part(by_q2, 1, has_q2)),
        (part(own_b, 1), part(by_b, 0, has_b), part(by_q, 1, has_b)),
    ):
        m = jnp.maximum(jnp.maximum(group[0][0], group[1][0]), group[2][0])
        ws = [jnp.exp(lse - m) for lse, _ in group]
        total = ws[0] + ws[1] + ws[2]
        merged.append((m + jnp.log(total), sum(wt * d for wt, (_, d) in zip(ws, group)) / total))
    return merged


def va_kernel(idx_ref, win_ref, len_ref, *refs):
    pieces = refs[:6]
    video = ((refs[6], refs[7]), (refs[8], refs[9]))
    outs = ((refs[10], refs[11]), (refs[12], refs[13]))
    kv_grads, audio, bias, grads = refs[14:]
    _, r, _ = coords(idx_ref)
    quarter = audio.shape[2]
    block_bias(idx_ref, win_ref, len_ref, bias)
    gather_audio(idx_ref, pieces, (2, 3), audio)
    scale = jnp.asarray(HD**-0.5, BF)

    @pl.loop(0, quarter // PAIR)
    def _(h):
        cols, wide_cols = pair_cols(idx_ref, h, quarter)
        grads[...] = jnp.zeros(grads.shape, F32)
        for group in block_groups(r):
            work = []
            for i, stretch, b in group:
                start, _ = window_of(idx_ref, win_ref, stretch, b)
                span = pl.ds(pl.multiple_of(start * BLK, BLK), WMAX * BLK)
                rows = slice(b * BLK, (b + 1) * BLK)
                q = both_heads(video[i][0][rows, wide_cols] * scale)
                g = both_heads(video[i][1][rows, wide_cols])
                keys, values = audio[0, span, cols], audio[1, span, cols]
                s = nt(keys, q) + bias[4 * i + b]
                dp = nt(values, g)
                work.append((i, rows, span, q, g, keys, values, s, dp))
            done = []
            for i, rows, span, q, g, keys, values, s, dp in work:
                ex = jnp.exp(s - jnp.max(s, axis=0, keepdims=True))
                inv = 1.0 / jnp.sum(ex, axis=0, keepdims=True)
                delta = jnp.sum(ex * dp, axis=0, keepdims=True) * inv
                p = ex * inv
                pb = p.astype(BF)
                ds = (p * (dp - delta)).astype(BF)
                done.append((i, rows, span, nn(ds, q), nn(pb, g), tn(pb, values), tn(ds, keys)))
            for i, rows, span, dk, dv, out, dq in done:
                grads[0, span, :] += dk
                grads[1, span, :] += dv
                outs[i][0][rows, cols] = own_heads(out).astype(BF)
                outs[i][1][rows, cols] = (own_heads(dq) * HD**-0.5).astype(BF)
        for n in range(2):
            kv_grads[n, :, cols] = grads[n].astype(BF)


def av_kernel(chips, idx_ref, win_ref, *refs):
    pieces = refs[:6]
    video = ((refs[6], refs[7]), (refs[8], refs[9]))
    stats, kv_grads = refs[10:16], refs[16]
    outs = ((refs[17], refs[18]), (refs[19], refs[20]))
    back = refs[21:27]
    audio, bias, grads, rowstat, qo_grads = refs[27:]
    c, r, _ = coords(idx_ref)
    quarter = audio.shape[2]
    block_bias(idx_ref, win_ref, None, bias)
    gather_audio(idx_ref, pieces, (0, 1), audio)

    @pl.loop(0, quarter // PAIR)
    def _(h):
        cols, wide_cols = pair_cols(idx_ref, h, quarter)
        for place, merged in zip(group_places(c), merge_stats(idx_ref, chips, *[ref[h] for ref in stats])):
            for n, x in enumerate(merged):
                wide = [jnp.broadcast_to(x[e : e + 1], (HD, PAIR)) for e in range(2)]
                rowstat[n, pl.ds(place * PAIR, PAIR), :] = jnp.concatenate(wide, axis=0).T
        grads[...] = jnp.zeros(grads.shape, F32)
        for group in block_groups(r):
            work = []
            for i, stretch, b in group:
                start, _ = window_of(idx_ref, win_ref, stretch, b)
                span = pl.ds(pl.multiple_of(start * BLK, BLK), WMAX * BLK)
                rows = slice(b * BLK, (b + 1) * BLK)
                keys = both_heads(video[i][0][rows, wide_cols])
                values = both_heads(video[i][1][rows, wide_cols])
                q, g = audio[0, span, cols], audio[1, span, cols]
                s = nt(q, keys) + bias[4 * i + b]
                dp = nt(g, values)
                work.append((i, rows, span, keys, values, q, g, s, dp))
            done = []
            for i, rows, span, keys, values, q, g, s, dp in work:
                p = jnp.exp(s - rowstat[0, span, :])
                pb = p.astype(BF)
                ds = (p * (dp - rowstat[1, span, :])).astype(BF)
                done.append((i, rows, span, nn(ds, keys), nn(pb, values), tn(ds, q), tn(pb, g)))
            for i, rows, span, dq, out, dk, dv in done:
                grads[0, span, :] += dq
                grads[1, span, :] += out
                outs[i][0][rows, cols] = own_heads(dk).astype(BF)
                outs[i][1][rows, cols] = own_heads(dv).astype(BF)
        qo_grads[0, :, cols] = (grads[0] * HD**-0.5).astype(BF)
        qo_grads[1, :, cols] = grads[1].astype(BF)

    scatter_audio(idx_ref, (kv_grads, kv_grads, qo_grads, qo_grads), back)


def sum_kernel(idx_ref, len_ref, keep, by_aud, by_a, by_ax, by_b, by_bx, after, mine, other):
    c, r, a = coords(idx_ref)
    half, quarter = keep.shape[2], keep.shape[3]
    row = lax.broadcasted_iota(jnp.int32, (half, quarter), 0) + a * half
    for slot, out in ((r, mine), (1 - r, other)):
        valid = row < len_ref[2 * c + slot]
        for part, parts in ((a, (keep, by_a, by_b)), (1 - a, (by_aud, by_ax, by_bx))):
            for n in range(4):
                x = sum(ref[n, slot].astype(F32) for ref in parts)
                if n == 3:
                    x = jnp.where(valid, x, 0.0)
                out[n, part] = x.astype(BF)


def join_audio_kernel(idx_ref, mine, other, *outs):
    _, r, _ = coords(idx_ref)
    quarter = mine.shape[3]
    for n, out in enumerate(outs):
        for part in range(2):
            for core, ref in ((r, mine), (1 - r, other)):
                col = pl.multiple_of((2 * part + core) * quarter, 128)
                out[:, pl.ds(col, quarter)] = ref[n, part]


def join_video_kernel(idx_ref, *refs):
    _, r, _ = coords(idx_ref)
    quarter = refs[0].shape[1]
    for own, far, out in zip(refs[:4], refs[4:8], refs[8:12]):
        for core, src in ((r, own), (1 - r, far)):
            out[:, pl.ds(pl.multiple_of(core * quarter, PAIR), quarter)] = src[...]
    refs[12][0] = 0


def cost(flops, transcendentals, nbytes):
    return pl.CostEstimate(flops=flops, transcendentals=transcendentals, bytes_accessed=nbytes)


def make_body(mesh):
    nv = mesh.shape["vid"]
    chips = nv // 2
    everyone = [(v, a) for v in range(nv) for a in range(2)]

    def perm(move):
        pairs = []
        for v, a in everyone:
            w, b = move(v, a)
            if 0 <= w < nv:
                pairs.append((2 * v + a, 2 * w + b))
        return pairs

    def diagonal(v):
        return 2 * ((((v >> 1) + 1) ^ 1) - 1) + (v & 1)

    moves = {
        "core": perm(lambda v, a: (v ^ 1, a)),
        "aud": perm(lambda v, a: (v, 1 - a)),
        "A": perm(lambda v, a: (v ^ 2, a)),
        "Ax": perm(lambda v, a: (v ^ 2, 1 - a)),
        "B": perm(lambda v, a: (diagonal(v), a)),
        "Bx": perm(lambda v, a: (diagonal(v), 1 - a)),
        "Bs": perm(lambda v, a: (diagonal(v), a ^ (v & 1))),
        "Q": perm(lambda v, a: (v - 4 if v & 2 else v + 4, a)),
        "Q2": perm(lambda v, a: (v + 4 if v & 2 else v - 4, a)),
    }

    def move(x, name):
        return lax.ppermute(x, ("vid", "aud"), moves[name])

    def step(q_v, k_v, v_v, g_v, q_a, k_a, v_a, g_a, window, audio_len):
        rows, width = q_v.shape
        quarter = width // 2
        half = q_a.shape[0]
        steps = quarter // PAIR
        idx = jnp.reshape(2 * lax.axis_index("vid") + lax.axis_index("aud"), (1,)).astype(jnp.int32)
        shape = jax.ShapeDtypeStruct

        smem = pl.BlockSpec(memory_space=pltpu.SMEM)
        win_spec = pl.BlockSpec((8, 2), lambda g, i: (i[0] >> 2, 0), memory_space=pltpu.SMEM)
        len_spec = smem
        whole = pl.BlockSpec(memory_space=pltpu.VMEM)
        hbm = pl.BlockSpec(memory_space=pltpu.HBM)

        def call(kernel, ins, outs, args, grid=(1,), scratch=(), est=None):
            return pl.pallas_call(
                kernel,
                grid_spec=pltpu.PrefetchScalarGridSpec(
                    num_scalar_prefetch=1,
                    grid=grid,
                    in_specs=ins,
                    out_specs=[s for s, _ in outs],
                    scratch_shapes=list(scratch),
                ),
                out_shape=[o for _, o in outs],
                cost_estimate=est,
                compiler_params=pltpu.CompilerParams(vmem_limit_bytes=24 << 20),
            )(idx, *args)

        audio = (q_a, g_a, k_a, v_a)
        audio_other = [move(x, "core") for x in audio]
        piece = shape((4, 2, half, quarter), BF)
        stack, both = shape((4, half, 2 * width), BF), shape((2, 4, 2, half, quarter), BF)
        (mine,) = call(
            load_kernel,
            [hbm] * 4,
            [(whole, stack)],
            [pltpu.with_memory_space_constraint(x, pltpu.HBM) for x in audio],
            scratch=(pltpu.SemaphoreType.DMA((4,)),),
            grid=(),
            est=cost(0, 0, 800000),
        )
        keep, send, carry = call(
            pack_kernel,
            [smem] + [whole] * 5,
            [(whole, piece)] * 2 + [(whole, both)],
            (audio_len, mine, *audio_other),
            grid=(),
            est=cost(0, 0, 1600000),
        )
        pieces = [keep, move(send, "aud"), move(keep, "A"), move(send, "Ax")]
        by_carry = move(carry, "Bs")
        pieces += [by_carry, move(by_carry, "core")]
        k_f, v_f, q_f, g_f = [move(x, "core") for x in (k_v, v_v, q_v, g_v)]

        audio_scratch = pltpu.VMEM((2, KEYS, quarter), BF)
        grad_scratch = pltpu.VMEM((2, KEYS, PAIR), F32)
        bias_scratch = pltpu.VMEM((8, WMAX * BLK, PAIR), F32)
        pairs = 2 * steps * 2 * rows * KEYS

        stat = shape((steps, 8, 2 * PAIR), F32)

        def find_stats(groups, before):
            lanes = len(groups) * PAIR
            (found,) = call(
                lambda *refs: stats_kernel(groups, *refs),
                [win_spec] + [whole] * (2 * len(groups) + 4 + len(before)),
                [(whole, stat)],
                (window, *[pieces[2 * g + n] for g in groups for n in range(2)], k_v, v_v, k_f, v_f, *before),
                scratch=(pltpu.VMEM((2, lanes, quarter), BF), pltpu.VMEM((2, rows, lanes), F32)),
                est=cost(4 * HD * pairs * lanes // KEYS, pairs * lanes // KEYS, 2000000),
            )
            return found

        stats_a = find_stats((0, 1), ())
        by_a, by_q = move(stats_a, "A"), move(stats_a, "Q")
        stats_b = find_stats((2,), (stats_a,))
        by_b, by_q2 = move(stats_b, "B"), move(stats_b, "Q2")

        full, part = shape((rows, width), BF), shape((rows, quarter), BF)
        out_own, dq_own, out_far, dq_far, kv_grads = call(
            va_kernel,
            [win_spec, len_spec] + [whole] * 10,
            [(whole, part)] * 4 + [(whole, shape((2, KEYS, quarter), BF))],
            (window, audio_len, *pieces, q_v, g_v, q_f, g_f),
            scratch=(audio_scratch, bias_scratch, grad_scratch),
            est=cost(10 * HD * pairs, pairs, 5000000),
        )
        dk_own, dv_own, dk_far, dv_far, *back = call(
            lambda *refs: av_kernel(chips, *refs),
            [win_spec] + [whole] * 17,
            [(whole, part)] * 4 + [(whole, piece)] * 6,
            (window, *pieces, k_v, v_v, k_f, v_f, stats_a, stats_b, by_a, by_b, by_q, by_q2, kv_grads),
            scratch=(audio_scratch, bias_scratch, grad_scratch, grad_scratch, audio_scratch),
            est=cost(12 * HD * pairs, pairs, 5000000),
        )
        parts = [back[0]] + [move(x, name) for x, name in zip(back[1:], ("aud", "A", "Ax", "B", "Bx"))]

        fars = [move(x, "core") for x in (out_far, dq_far, dk_far, dv_far)]
        out_video, dq_video, dk_video, dv_video, joined = call(
            join_video_kernel,
            [whole] * 8,
            [(whole, full)] * 4 + [(smem, shape((1,), jnp.int32))],
            (out_own, dq_own, dk_own, dv_own, *fars),
            est=cost(0, 0, 1600000),
        )
        mine, other = call(
            sum_kernel, [smem] + [whole] * 6 + [smem], [(whole, piece)] * 2, (audio_len, *parts, joined), grid=(),
            est=cost(1000000, 0, 1600000),
        )
        other = move(other, "core")
        dk_audio, dv_audio, dq_audio, out_audio = call(
            join_audio_kernel,
            [whole] * 2,
            [(whole, shape((half, 2 * width), BF))] * 4,
            (mine, other),
            grid=(),
            est=cost(0, 0, 800000),
        )
        return (out_video, out_audio, dq_video, dk_video, dv_video, dq_audio, dk_audio, dv_audio)

    return step


def solution(mesh):
    video, audio = P("vid", "aud"), P(("vid", "aud"), None)
    return jax.shard_map(
        make_body(mesh),
        mesh=mesh,
        in_specs=(video,) * 4 + (audio,) * 4 + (P(), P()),
        out_specs=(video, audio, video, video, video, audio, audio, audio),
        check_vma=False,
    )
```

```python
import functools

import jax
import jax.numpy as jnp
from jax import lax
from jax.experimental import pallas as pl
from jax.experimental.pallas import tpu as pltpu
from jax.sharding import PartitionSpec as P


HD = 64
BLK = 64
WMAX = 3
PAIR = 2 * HD
NEG = -1e30
BF = jnp.bfloat16
F32 = jnp.float32


NPOS = 6
KEYS = NPOS * BLK
GROUP = 8


def nt(x, y):
    return lax.dot_general(x, y, (((1,), (1,)), ((), ())), preferred_element_type=F32)


def nn(x, y):
    return lax.dot_general(x, y, (((1,), (0,)), ((), ())), preferred_element_type=F32)


def coords(idx_ref):
    idx = idx_ref[0]
    return idx >> 2, (idx >> 1) & 1, idx & 1


def head_part(x, e):
    lane = lax.broadcasted_iota(jnp.int32, x.shape, 1)
    return jnp.where((lane < HD) if e == 0 else (lane >= HD), x, jnp.zeros_like(x))


def load_kernel(idx_ref, *refs):
    srcs, dst, sems = refs[:4], refs[4], refs[5]
    copies = [pltpu.make_async_copy(src, dst.at[n], sems.at[n]) for n, src in enumerate(srcs)]
    for copy in copies:
        copy.start()
    for copy in copies:
        copy.wait()


def pack_kernel(idx_ref, len_ref, mine, *refs):
    other, (keep, send) = refs[:4], refs[4:]
    c, r, a = coords(idx_ref)
    half, quarter = keep.shape[2], keep.shape[3]
    row = lax.broadcasted_iota(jnp.int32, (half, quarter), 0) + a * half
    for slot, arrays in ((r, [mine.at[n] for n in range(4)]), (1 - r, other)):
        valid = row < len_ref[2 * c + slot]
        for n, ref in enumerate(arrays):

            def part(which, core):
                col = pl.multiple_of((2 * which + core) * quarter, 128)
                x = ref[:, pl.ds(col, quarter)]
                if n == 0:
                    x = x * jnp.asarray(HD**-0.5, BF)
                if n == 1:
                    x = jnp.where(valid, x, jnp.zeros_like(x))
                return x

            keep[n, slot] = part(a, r)
            send[n, slot] = part(1 - a, r)


def piece_rows(idx_ref):
    c, _, a = coords(idx_ref)
    half = BLK // 2
    side = 2 - 2 * (c & 1)
    starts = []
    for place, part in ((1, a), (1, 1 - a), (side, a), (side, 1 - a), (2 - side, a), (2 - side, 1 - a)):
        first = place * 2 * BLK + part * half
        starts.append([pl.multiple_of(first + core * BLK, half) for core in range(2)])
    return starts


def gather_audio(idx_ref, pieces, arrays, dst):
    half = BLK // 2
    for ref, firsts in zip(pieces, piece_rows(idx_ref)):
        for core, first in enumerate(firsts):
            for n, k in enumerate(arrays):
                dst[n, pl.ds(first, half), :] = ref[k, core]


def scatter_audio(idx_ref, sources, pieces):
    half = BLK // 2
    for ref, firsts in zip(pieces, piece_rows(idx_ref)):
        for core, first in enumerate(firsts):
            for n, src in enumerate(sources):
                ref[n, core] = src[n % 2, pl.ds(first, half), :]


def pair_cols(idx_ref, h, quarter):
    _, r, _ = coords(idx_ref)
    col = pl.multiple_of(h * PAIR, PAIR)
    return pl.ds(col, PAIR), pl.ds(pl.multiple_of(r * quarter + col, PAIR), PAIR)


def window_bounds(win_ref, c, stretch, shape, axis):
    block = lax.broadcasted_iota(jnp.int32, shape, axis) // BLK
    lo = jnp.zeros(shape, jnp.int32)
    hi = jnp.zeros(shape, jnp.int32)
    for b in range(4):
        start = win_ref[4 * stretch + b, 0] - (2 * c - 2)
        count = win_ref[4 * stretch + b, 1]
        lo = jnp.where(block == b, start, lo)
        hi = jnp.where(block == b, start + count, hi)
    return lo, hi


def window_of(idx_ref, win_ref, stretch, b):
    c, _, _ = coords(idx_ref)
    return win_ref[4 * stretch + b, 0] - (2 * c - 2), win_ref[4 * stretch + b, 1]


def block_bias(idx_ref, win_ref, len_ref, bias):
    c, r, _ = coords(idx_ref)
    row = lax.broadcasted_iota(jnp.int32, bias.shape[1:], 0)
    for i, stretch in enumerate((r, 1 - r)):
        for b in range(4):
            start, count = window_of(idx_ref, win_ref, stretch, b)
            keep = row < count * BLK
            if len_ref is not None:
                length = jnp.zeros(row.shape, jnp.int32)
                for j in range(WMAX):
                    block = jnp.clip(2 * c - 2 + start + j, 0, len_ref.shape[0] - 1)
                    length = jnp.where(row // BLK == j, len_ref[block], length)
                keep = keep & (row % BLK < length)
            bias[4 * i + b] = jnp.where(keep, 0.0, NEG)


def both_heads(x):
    return jnp.concatenate([head_part(x, 0), head_part(x, 1)], axis=0)


def own_heads(x):
    lane = lax.broadcasted_iota(jnp.int32, (BLK, PAIR), 1)
    return jnp.where(lane < HD, x[:BLK], x[BLK:])


def block_groups(r):
    blocks = [(i, stretch, b) for b in range(4) for i, stretch in enumerate((r, 1 - r))]
    return [blocks[n : n + GROUP] for n in range(0, 8, GROUP)]


def tn(x, y):
    return lax.dot_general(x, y, (((0,), (0,)), ((), ())), preferred_element_type=F32)


def group_places(c):
    side = 2 - 2 * (c & 1)
    return 1, side, 2 - side


def group_bias(idx_ref, win_ref, groups, bias):
    c, r, _ = coords(idx_ref)
    places = group_places(c)
    shape = bias.shape[1:]
    lane = lax.broadcasted_iota(jnp.int32, shape, 1)
    place = jnp.zeros(shape, jnp.int32)
    for n, group in enumerate(groups):
        place = jnp.where(lane // PAIR == n, 2 * places[group], place)
    place = place + (lane % PAIR) // BLK
    for i, stretch in enumerate((r, 1 - r)):
        lo, hi = window_bounds(win_ref, c, stretch, shape, 0)
        bias[i] = jnp.where((place >= lo) & (place < hi), 0.0, NEG)


def pair_stats(x, y):
    m = jnp.maximum(x[0:2], y[0:2])
    wx, wy = jnp.exp(x[0:2] - m), jnp.exp(y[0:2] - m)
    total = wx + wy
    lse, delta = m + jnp.log(total), (wx * x[2:4] + wy * y[2:4]) / total
    return jnp.concatenate([lse, delta, lse, delta], axis=0)


def stats_kernel(groups, idx_ref, win_ref, *refs):
    count = len(groups)
    pieces, refs = refs[: 2 * count], refs[2 * count :]
    video, refs = ((refs[0], refs[1]), (refs[2], refs[3])), refs[4:]
    stat_ref, audio, bias = refs[-3:]
    _, _, a = coords(idx_ref)
    half, quarter = BLK // 2, audio.shape[2]
    group_bias(idx_ref, win_ref, groups, bias)
    for n in range(count):
        for ref, part in ((pieces[2 * n], a), (pieces[2 * n + 1], 1 - a)):
            for core in range(2):
                first = pl.multiple_of(n * PAIR + core * BLK + part * half, half)
                for k in range(2):
                    audio[k, pl.ds(first, half), :] = ref[k, core]

    @pl.loop(0, quarter // PAIR)
    def _(h):
        cols, wide_cols = pair_cols(idx_ref, h, quarter)
        queries, cot = audio[0, :, cols], audio[1, :, cols]
        work = []
        for e in range(2):
            s = [nt(head_part(k_ref[:, wide_cols], e), queries) + bias[i] for i, (k_ref, _) in enumerate(video)]
            work.append((s, [nt(head_part(v_ref[:, wide_cols], e), cot) for _, v_ref in video]))
        lses, deltas = [], []
        for s, dp in work:
            m = jnp.maximum(*[jnp.max(x, axis=0, keepdims=True) for x in s])
            ex = [jnp.exp(x - m) for x in s]
            total = sum(jnp.sum(x, axis=0, keepdims=True) for x in ex)
            lses.append(m + jnp.log(total))
            deltas.append(sum(jnp.sum(x * y, axis=0, keepdims=True) for x, y in zip(ex, dp)) / total)
        rows = jnp.concatenate(lses + deltas + lses + deltas, axis=0)
        if count == 1:
            rows = jnp.concatenate([pair_stats(refs[0][h][:, :PAIR], refs[1][h][:, PAIR:]), rows], axis=1)
        stat_ref[h] = rows


def merge_stats(idx_ref, chips, own_a, own_b, by_a, by_b, by_q2):
    c, _, _ = coords(idx_ref)
    even = (c & 1) == 0
    has_b = jnp.where(even, c >= 2, c + 2 < chips)
    has_q2 = jnp.where(even, c + 2 < chips, c >= 2)

    def part(x, k, there=None):
        x = x[:, k * PAIR : (k + 1) * PAIR]
        return (x[0:2] if there is None else jnp.where(there, x[0:2], NEG)), x[2:4]

    merged = []
    for group in (
        (part(own_a, 0), part(by_a, 1), part(by_b, 1, has_b)),
        (part(own_a, 1), part(by_a, 0), part(by_q2, 1, has_q2)),
        (part(own_b, 1), part(by_b, 0, has_b)),
    ):
        m = functools.reduce(jnp.maximum, [lse for lse, _ in group])
        ws = [jnp.exp(lse - m) for lse, _ in group]
        total = sum(ws)
        merged.append((m + jnp.log(total), sum(wt * d for wt, (_, d) in zip(ws, group)) / total))
    return merged


def va_kernel(idx_ref, win_ref, len_ref, *refs):
    pieces = refs[:6]
    video = ((refs[6], refs[7]), (refs[8], refs[9]))
    outs = ((refs[10], refs[11]), (refs[12], refs[13]))
    kv_grads, audio, bias, grads = refs[14:]
    _, r, _ = coords(idx_ref)
    quarter = audio.shape[2]
    block_bias(idx_ref, win_ref, len_ref, bias)
    gather_audio(idx_ref, pieces, (2, 3), audio)
    scale = jnp.asarray(HD**-0.5, BF)

    @pl.loop(0, quarter // PAIR)
    def _(h):
        cols, wide_cols = pair_cols(idx_ref, h, quarter)
        grads[...] = jnp.zeros(grads.shape, F32)
        for group in block_groups(r):
            work = []
            for i, stretch, b in group:
                start, _ = window_of(idx_ref, win_ref, stretch, b)
                span = pl.ds(pl.multiple_of(start * BLK, BLK), WMAX * BLK)
                rows = slice(b * BLK, (b + 1) * BLK)
                q = both_heads(video[i][0][rows, wide_cols] * scale)
                g = both_heads(video[i][1][rows, wide_cols])
                keys, values = audio[0, span, cols], audio[1, span, cols]
                s = nt(keys, q) + bias[4 * i + b]
                dp = nt(values, g)
                work.append((i, rows, span, q, g, keys, values, s, dp))
            done = []
            for i, rows, span, q, g, keys, values, s, dp in work:
                ex = jnp.exp(s - jnp.max(s, axis=0, keepdims=True))
                inv = 1.0 / jnp.sum(ex, axis=0, keepdims=True)
                delta = jnp.sum(ex * dp, axis=0, keepdims=True) * inv
                p = ex * inv
                pb = p.astype(BF)
                ds = (p * (dp - delta)).astype(BF)
                done.append((i, rows, span, nn(ds, q), nn(pb, g), tn(pb, values), tn(ds, keys)))
            for i, rows, span, dk, dv, out, dq in done:
                grads[0, span, :] += dk
                grads[1, span, :] += dv
                outs[i][0][rows, cols] = own_heads(out).astype(BF)
                outs[i][1][rows, cols] = (own_heads(dq) * HD**-0.5).astype(BF)
        for n in range(2):
            kv_grads[n, :, cols] = grads[n].astype(BF)


def av_kernel(chips, idx_ref, win_ref, *refs):
    pieces = refs[:6]
    video = ((refs[6], refs[7]), (refs[8], refs[9]))
    stats, kv_grads = refs[10:15], refs[15]
    outs = ((refs[16], refs[17]), (refs[18], refs[19]))
    back = refs[20:26]
    audio, bias, grads, rowstat, qo_grads = refs[26:]
    c, r, _ = coords(idx_ref)
    quarter = audio.shape[2]
    block_bias(idx_ref, win_ref, None, bias)
    gather_audio(idx_ref, pieces, (0, 1), audio)

    @pl.loop(0, quarter // PAIR)
    def _(h):
        cols, wide_cols = pair_cols(idx_ref, h, quarter)
        for place, merged in zip(group_places(c), merge_stats(idx_ref, chips, *[ref[h] for ref in stats])):
            for n, x in enumerate(merged):
                wide = [jnp.broadcast_to(x[e : e + 1], (HD, PAIR)) for e in range(2)]
                rowstat[n, pl.ds(place * PAIR, PAIR), :] = jnp.concatenate(wide, axis=0).T
        grads[...] = jnp.zeros(grads.shape, F32)
        for group in block_groups(r):
            work = []
            for i, stretch, b in group:
                start, _ = window_of(idx_ref, win_ref, stretch, b)
                span = pl.ds(pl.multiple_of(start * BLK, BLK), WMAX * BLK)
                rows = slice(b * BLK, (b + 1) * BLK)
                keys = both_heads(video[i][0][rows, wide_cols])
                values = both_heads(video[i][1][rows, wide_cols])
                q, g = audio[0, span, cols], audio[1, span, cols]
                s = nt(q, keys) + bias[4 * i + b]
                dp = nt(g, values)
                work.append((i, rows, span, keys, values, q, g, s, dp))
            done = []
            for i, rows, span, keys, values, q, g, s, dp in work:
                p = jnp.exp(s - rowstat[0, span, :])
                pb = p.astype(BF)
                ds = (p * (dp - rowstat[1, span, :])).astype(BF)
                done.append((i, rows, span, nn(ds, keys), nn(pb, values), tn(ds, q), tn(pb, g)))
            for i, rows, span, dq, out, dk, dv in done:
                grads[0, span, :] += dq
                grads[1, span, :] += out
                outs[i][0][rows, cols] = own_heads(dk).astype(BF)
                outs[i][1][rows, cols] = own_heads(dv).astype(BF)
        qo_grads[0, :, cols] = (grads[0] * HD**-0.5).astype(BF)
        qo_grads[1, :, cols] = grads[1].astype(BF)

    scatter_audio(idx_ref, (kv_grads, kv_grads, qo_grads, qo_grads), back)


def sum_kernel(idx_ref, len_ref, keep, by_aud, by_a, by_ax, by_b, by_bx, after, mine, other):
    c, r, a = coords(idx_ref)
    half, quarter = keep.shape[2], keep.shape[3]
    row = lax.broadcasted_iota(jnp.int32, (half, quarter), 0) + a * half
    for slot, out in ((r, mine), (1 - r, other)):
        valid = row < len_ref[2 * c + slot]
        for part, parts in ((a, (keep, by_a, by_b)), (1 - a, (by_aud, by_ax, by_bx))):
            for n in range(4):
                x = sum(ref[n, slot].astype(F32) for ref in parts)
                if n == 3:
                    x = jnp.where(valid, x, 0.0)
                out[n, part] = x.astype(BF)


def join_audio_kernel(idx_ref, mine, other, *outs):
    _, r, _ = coords(idx_ref)
    quarter = mine.shape[3]
    for n, out in enumerate(outs):
        for part in range(2):
            for core, ref in ((r, mine), (1 - r, other)):
                col = pl.multiple_of((2 * part + core) * quarter, 128)
                out[:, pl.ds(col, quarter)] = ref[n, part]


def join_video_kernel(idx_ref, *refs):
    _, r, _ = coords(idx_ref)
    quarter = refs[0].shape[1]
    for own, far, out in zip(refs[:4], refs[4:8], refs[8:12]):
        for core, src in ((r, own), (1 - r, far)):
            out[:, pl.ds(pl.multiple_of(core * quarter, PAIR), quarter)] = src[...]
    refs[12][0] = 0


def cost(flops, transcendentals, nbytes):
    return pl.CostEstimate(flops=flops, transcendentals=transcendentals, bytes_accessed=nbytes)


def make_body(mesh):
    nv = mesh.shape["vid"]
    chips = nv // 2
    everyone = [(v, a) for v in range(nv) for a in range(2)]

    def perm(move):
        pairs = []
        for v, a in everyone:
            w, b = move(v, a)
            if 0 <= w < nv:
                pairs.append((2 * v + a, 2 * w + b))
        return pairs

    def diagonal(v):
        return 2 * ((((v >> 1) + 1) ^ 1) - 1) + (v & 1)

    moves = {
        "core": perm(lambda v, a: (v ^ 1, a)),
        "aud": perm(lambda v, a: (v, 1 - a)),
        "A": perm(lambda v, a: (v ^ 2, a)),
        "Ax": perm(lambda v, a: (v ^ 2, 1 - a)),
        "B": perm(lambda v, a: (diagonal(v), a)),
        "Bx": perm(lambda v, a: (diagonal(v), 1 - a)),
        "Q2": perm(lambda v, a: (v + 4 if v & 2 else v - 4, a)),
    }

    def move(x, name):
        return lax.ppermute(x, ("vid", "aud"), moves[name])

    def step(q_v, k_v, v_v, g_v, q_a, k_a, v_a, g_a, window, audio_len):
        rows, width = q_v.shape
        quarter = width // 2
        half = q_a.shape[0]
        steps = quarter // PAIR
        idx = jnp.reshape(2 * lax.axis_index("vid") + lax.axis_index("aud"), (1,)).astype(jnp.int32)
        shape = jax.ShapeDtypeStruct

        smem = pl.BlockSpec(memory_space=pltpu.SMEM)
        win_spec = pl.BlockSpec((8, 2), lambda g, i: (i[0] >> 2, 0), memory_space=pltpu.SMEM)
        len_spec = smem
        whole = pl.BlockSpec(memory_space=pltpu.VMEM)
        hbm = pl.BlockSpec(memory_space=pltpu.HBM)

        def call(kernel, ins, outs, args, grid=(1,), scratch=(), est=None):
            return pl.pallas_call(
                kernel,
                grid_spec=pltpu.PrefetchScalarGridSpec(
                    num_scalar_prefetch=1,
                    grid=grid,
                    in_specs=ins,
                    out_specs=[s for s, _ in outs],
                    scratch_shapes=list(scratch),
                ),
                out_shape=[o for _, o in outs],
                cost_estimate=est,
                compiler_params=pltpu.CompilerParams(vmem_limit_bytes=24 << 20),
            )(idx, *args)

        audio = (q_a, g_a, k_a, v_a)
        audio_other = [move(x, "core") for x in audio]
        piece = shape((4, 2, half, quarter), BF)
        stack = shape((4, half, 2 * width), BF)
        (mine,) = call(
            load_kernel,
            [hbm] * 4,
            [(whole, stack)],
            [pltpu.with_memory_space_constraint(x, pltpu.HBM) for x in audio],
            scratch=(pltpu.SemaphoreType.DMA((4,)),),
            grid=(),
            est=cost(0, 0, 800000),
        )
        keep, send = call(
            pack_kernel,
            [smem] + [whole] * 5,
            [(whole, piece)] * 2,
            (audio_len, mine, *audio_other),
            grid=(),
            est=cost(0, 0, 1600000),
        )
        pieces = [keep, move(send, "aud"), move(keep, "A"), move(send, "Ax")]
        pieces += [move(keep, "B"), move(send, "Bx")]
        k_f, v_f, q_f, g_f = [move(x, "core") for x in (k_v, v_v, q_v, g_v)]

        audio_scratch = pltpu.VMEM((2, KEYS, quarter), BF)
        grad_scratch = pltpu.VMEM((2, KEYS, PAIR), F32)
        bias_scratch = pltpu.VMEM((8, WMAX * BLK, PAIR), F32)
        pairs = 2 * steps * 2 * rows * KEYS

        stat = shape((steps, 8, 2 * PAIR), F32)

        def find_stats(groups, before):
            lanes = len(groups) * PAIR
            (found,) = call(
                lambda *refs: stats_kernel(groups, *refs),
                [win_spec] + [whole] * (2 * len(groups) + 4 + len(before)),
                [(whole, stat)],
                (window, *[pieces[2 * g + n] for g in groups for n in range(2)], k_v, v_v, k_f, v_f, *before),
                scratch=(pltpu.VMEM((2, lanes, quarter), BF), pltpu.VMEM((2, rows, lanes), F32)),
                est=cost(4 * HD * pairs * lanes // KEYS, pairs * lanes // KEYS, 2000000),
            )
            return found

        stats_a = find_stats((0, 1), ())
        by_a = move(stats_a, "A")
        stats_b = find_stats((2,), (stats_a, by_a))
        by_b, by_q2 = move(stats_b, "B"), move(stats_b, "Q2")

        full, part = shape((rows, width), BF), shape((rows, quarter), BF)
        out_own, dq_own, out_far, dq_far, kv_grads = call(
            va_kernel,
            [win_spec, len_spec] + [whole] * 10,
            [(whole, part)] * 4 + [(whole, shape((2, KEYS, quarter), BF))],
            (window, audio_len, *pieces, q_v, g_v, q_f, g_f),
            scratch=(audio_scratch, bias_scratch, grad_scratch),
            est=cost(10 * HD * pairs, pairs, 5000000),
        )
        dk_own, dv_own, dk_far, dv_far, *back = call(
            lambda *refs: av_kernel(chips, *refs),
            [win_spec] + [whole] * 16,
            [(whole, part)] * 4 + [(whole, piece)] * 6,
            (window, *pieces, k_v, v_v, k_f, v_f, stats_a, stats_b, by_a, by_b, by_q2, kv_grads),
            scratch=(audio_scratch, bias_scratch, grad_scratch, grad_scratch, audio_scratch),
            est=cost(12 * HD * pairs, pairs, 5000000),
        )
        parts = [back[0]] + [move(x, name) for x, name in zip(back[1:], ("aud", "A", "Ax", "B", "Bx"))]

        fars = [move(x, "core") for x in (out_far, dq_far, dk_far, dv_far)]
        out_video, dq_video, dk_video, dv_video, joined = call(
            join_video_kernel,
            [whole] * 8,
            [(whole, full)] * 4 + [(smem, shape((1,), jnp.int32))],
            (out_own, dq_own, dk_own, dv_own, *fars),
            est=cost(0, 0, 1600000),
        )
        mine, other = call(
            sum_kernel, [smem] + [whole] * 6 + [smem], [(whole, piece)] * 2, (audio_len, *parts, joined), grid=(),
            est=cost(1000000, 0, 1600000),
        )
        other = move(other, "core")
        dk_audio, dv_audio, dq_audio, out_audio = call(
            join_audio_kernel,
            [whole] * 2,
            [(whole, shape((half, 2 * width), BF))] * 4,
            (mine, other),
            grid=(),
            est=cost(0, 0, 800000),
        )
        return (out_video, out_audio, dq_video, dk_video, dv_video, dq_audio, dk_audio, dv_audio)

    return step


def solution(mesh):
    video, audio = P("vid", "aud"), P(("vid", "aud"), None)
    return jax.shard_map(
        make_body(mesh),
        mesh=mesh,
        in_specs=(video,) * 4 + (audio,) * 4 + (P(), P()),
        out_specs=(video, audio, video, video, video, audio, audio, audio),
        check_vma=False,
    )
```

```python
import functools

import jax
import jax.numpy as jnp
from jax import lax
from jax.experimental import pallas as pl
from jax.experimental.pallas import tpu as pltpu
from jax.sharding import PartitionSpec as P


HD = 64
BLK = 64
WMAX = 3
PAIR = 2 * HD
NEG = -1e30
BF = jnp.bfloat16
F32 = jnp.float32


NPOS = 6
KEYS = NPOS * BLK
GROUP = 8


def nt(x, y):
    return lax.dot_general(x, y, (((1,), (1,)), ((), ())), preferred_element_type=F32)


def nn(x, y):
    return lax.dot_general(x, y, (((1,), (0,)), ((), ())), preferred_element_type=F32)


def coords():
    vid, aud = lax.axis_index("vid"), lax.axis_index("aud")
    return vid >> 1, vid & 1, aud


def head_part(x, e):
    lane = lax.broadcasted_iota(jnp.int32, x.shape, 1)
    return jnp.where((lane < HD) if e == 0 else (lane >= HD), x, jnp.zeros_like(x))


def load_kernel(*refs):
    srcs, dst, sems = refs[:4], refs[4], refs[5]
    copies = [pltpu.make_async_copy(src, dst.at[n], sems.at[n]) for n, src in enumerate(srcs)]
    for copy in copies:
        copy.start()
    for copy in copies:
        copy.wait()


def pack_kernel(len_ref, mine, *refs):
    other, (keep, send, mask) = refs[:4], refs[4:]
    c, r, a = coords()
    half, quarter = keep.shape[2], keep.shape[3]
    row = lax.broadcasted_iota(jnp.int32, (half, quarter), 0) + a * half
    for slot, arrays in ((r, [mine.at[n] for n in range(4)]), (1 - r, other)):
        valid = row < len_ref[2 * c + slot]
        mask[slot] = jnp.where(valid, 1.0, 0.0)
        for n, ref in enumerate(arrays):

            def part(which, core):
                col = pl.multiple_of((2 * which + core) * quarter, 128)
                x = ref[:, pl.ds(col, quarter)]
                if n == 0:
                    x = x * jnp.asarray(HD**-0.5, BF)
                if n == 1:
                    x = jnp.where(valid, x, jnp.zeros_like(x))
                return x

            keep[n, slot] = part(a, r)
            send[n, slot] = part(1 - a, r)


def piece_rows():
    c, _, a = coords()
    half = BLK // 2
    side = 2 - 2 * (c & 1)
    starts = []
    for place, part in ((1, a), (1, 1 - a), (side, a), (side, 1 - a), (2 - side, a), (2 - side, 1 - a)):
        first = place * 2 * BLK + part * half
        starts.append([pl.multiple_of(first + core * BLK, half) for core in range(2)])
    return starts


def gather_audio(pieces, arrays, dst):
    half = BLK // 2
    for ref, firsts in zip(pieces, piece_rows()):
        for core, first in enumerate(firsts):
            for n, k in enumerate(arrays):
                dst[n, pl.ds(first, half), :] = ref[k, core]


def scatter_audio(sources, pieces):
    half = BLK // 2
    for ref, firsts in zip(pieces, piece_rows()):
        for core, first in enumerate(firsts):
            for n, src in enumerate(sources):
                ref[n, core] = src[n % 2, pl.ds(first, half), :]


def pair_cols(h, quarter):
    _, r, _ = coords()
    col = pl.multiple_of(h * PAIR, PAIR)
    return pl.ds(col, PAIR), pl.ds(pl.multiple_of(r * quarter + col, PAIR), PAIR)


def window_bounds(win_ref, c, stretch, shape, axis):
    block = lax.broadcasted_iota(jnp.int32, shape, axis) // BLK
    lo = jnp.zeros(shape, jnp.int32)
    hi = jnp.zeros(shape, jnp.int32)
    for b in range(4):
        start = win_ref[0, 8 * c + 4 * stretch + b] - (2 * c - 2)
        count = win_ref[1, 8 * c + 4 * stretch + b]
        lo = jnp.where(block == b, start, lo)
        hi = jnp.where(block == b, start + count, hi)
    return lo, hi


def window_of(win_ref, stretch, b):
    c, _, _ = coords()
    block = 8 * c + 4 * stretch + b
    return win_ref[0, block] - (2 * c - 2), win_ref[1, block]


def block_bias(win_ref, len_ref, bias):
    c, r, _ = coords()
    row = lax.broadcasted_iota(jnp.int32, bias.shape[1:], 0)
    for i, stretch in enumerate((r, 1 - r)):
        for b in range(4):
            start, count = window_of(win_ref, stretch, b)
            keep = row < count * BLK
            if len_ref is not None:
                length = jnp.zeros(row.shape, jnp.int32)
                for j in range(WMAX):
                    block = jnp.clip(2 * c - 2 + start + j, 0, len_ref.shape[0] - 1)
                    length = jnp.where(row // BLK == j, len_ref[block], length)
                keep = keep & (row % BLK < length)
            bias[4 * i + b] = jnp.where(keep, 0.0, NEG)


def both_heads(x):
    return jnp.concatenate([head_part(x, 0), head_part(x, 1)], axis=0)


def own_heads(x):
    lane = lax.broadcasted_iota(jnp.int32, (BLK, PAIR), 1)
    return jnp.where(lane < HD, x[:BLK], x[BLK:])


def block_groups(r):
    blocks = [(i, stretch, b) for b in range(4) for i, stretch in enumerate((r, 1 - r))]
    return [blocks[n : n + GROUP] for n in range(0, 8, GROUP)]


def tn(x, y):
    return lax.dot_general(x, y, (((0,), (0,)), ((), ())), preferred_element_type=F32)


def group_places(c):
    side = 2 - 2 * (c & 1)
    return 1, side, 2 - side


def group_bias(win_ref, groups, bias):
    c, r, _ = coords()
    places = group_places(c)
    shape = bias.shape[1:]
    lane = lax.broadcasted_iota(jnp.int32, shape, 1)
    place = jnp.zeros(shape, jnp.int32)
    for n, group in enumerate(groups):
        place = jnp.where(lane // PAIR == n, 2 * places[group], place)
    place = place + (lane % PAIR) // BLK
    for i, stretch in enumerate((r, 1 - r)):
        lo, hi = window_bounds(win_ref, c, stretch, shape, 0)
        bias[i] = jnp.where((place >= lo) & (place < hi), 0.0, NEG)


def pair_stats(x, y):
    m = jnp.maximum(x[0:2], y[0:2])
    wx, wy = jnp.exp(x[0:2] - m), jnp.exp(y[0:2] - m)
    total = wx + wy
    lse, delta = m + jnp.log(total), (wx * x[2:4] + wy * y[2:4]) / total
    return jnp.concatenate([lse, delta, lse, delta], axis=0)


def stats_kernel(groups, win_ref, *refs):
    count = len(groups)
    pieces, refs = refs[: 2 * count], refs[2 * count :]
    video, refs = ((refs[0], refs[1]), (refs[2], refs[3])), refs[4:]
    stat_ref, audio, bias = refs[-3:]
    _, _, a = coords()
    half, quarter = BLK // 2, audio.shape[2]
    group_bias(win_ref, groups, bias)
    for n in range(count):
        for ref, part in ((pieces[2 * n], a), (pieces[2 * n + 1], 1 - a)):
            for core in range(2):
                first = pl.multiple_of(n * PAIR + core * BLK + part * half, half)
                for k in range(2):
                    audio[k, pl.ds(first, half), :] = ref[k, core]

    @pl.loop(0, quarter // PAIR, unroll=True)
    def _(h):
        cols, wide_cols = pair_cols(h, quarter)
        queries, cot = audio[0, :, cols], audio[1, :, cols]
        work = []
        for e in range(2):
            s = [nt(head_part(k_ref[:, wide_cols], e), queries) + bias[i] for i, (k_ref, _) in enumerate(video)]
            work.append((s, [nt(head_part(v_ref[:, wide_cols], e), cot) for _, v_ref in video]))
        lses, deltas = [], []
        for s, dp in work:
            m = jnp.maximum(*[jnp.max(x, axis=0, keepdims=True) for x in s])
            ex = [jnp.exp(x - m) for x in s]
            total = sum(jnp.sum(x, axis=0, keepdims=True) for x in ex)
            lses.append(m + jnp.log(total))
            deltas.append(sum(jnp.sum(x * y, axis=0, keepdims=True) for x, y in zip(ex, dp)) / total)
        rows = jnp.concatenate(lses + deltas + lses + deltas, axis=0)
        if count == 1:
            rows = jnp.concatenate([pair_stats(refs[0][h][:, :PAIR], refs[1][h][:, PAIR:]), rows], axis=1)
        stat_ref[h] = rows


def merge_stats(chips, own_a, own_b, by_a, by_b, by_q2):
    c, _, _ = coords()
    even = (c & 1) == 0
    has_b = jnp.where(even, c >= 2, c + 2 < chips)
    has_q2 = jnp.where(even, c + 2 < chips, c >= 2)

    def part(x, k, there=None):
        x = x[:, k * PAIR : (k + 1) * PAIR]
        return (x[0:2] if there is None else jnp.where(there, x[0:2], NEG)), x[2:4]

    merged = []
    for group in (
        (part(own_a, 0), part(by_a, 1), part(by_b, 1, has_b)),
        (part(own_a, 1), part(by_a, 0), part(by_q2, 1, has_q2)),
        (part(own_b, 1), part(by_b, 0, has_b)),
    ):
        m = functools.reduce(jnp.maximum, [lse for lse, _ in group])
        ws = [jnp.exp(lse - m) for lse, _ in group]
        total = sum(ws)
        merged.append((m + jnp.log(total), sum(wt * d for wt, (_, d) in zip(ws, group)) / total))
    return merged


def va_kernel(win_ref, len_ref, *refs):
    pieces = refs[:6]
    video = ((refs[6], refs[7]), (refs[8], refs[9]))
    outs = ((refs[10], refs[11]), (refs[12], refs[13]))
    kv_grads, audio, bias, grads = refs[14:]
    _, r, _ = coords()
    quarter = audio.shape[2]
    block_bias(win_ref, len_ref, bias)
    gather_audio(pieces, (2, 3), audio)
    scale = jnp.asarray(HD**-0.5, BF)

    @pl.loop(0, quarter // PAIR)
    def _(h):
        cols, wide_cols = pair_cols(h, quarter)
        grads[...] = jnp.zeros(grads.shape, F32)
        for group in block_groups(r):
            work = []
            for i, stretch, b in group:
                start, _ = window_of(win_ref, stretch, b)
                span = pl.ds(pl.multiple_of(start * BLK, BLK), WMAX * BLK)
                rows = slice(b * BLK, (b + 1) * BLK)
                q = both_heads(video[i][0][rows, wide_cols] * scale)
                g = both_heads(video[i][1][rows, wide_cols])
                keys, values = audio[0, span, cols], audio[1, span, cols]
                s = nt(keys, q) + bias[4 * i + b]
                dp = nt(values, g)
                work.append((i, rows, span, q, g, keys, values, s, dp))
            done = []
            for i, rows, span, q, g, keys, values, s, dp in work:
                ex = jnp.exp(s - jnp.max(s, axis=0, keepdims=True))
                inv = 1.0 / jnp.sum(ex, axis=0, keepdims=True)
                delta = jnp.sum(ex * dp, axis=0, keepdims=True) * inv
                p = ex * inv
                pb = p.astype(BF)
                ds = (p * (dp - delta)).astype(BF)
                done.append((i, rows, span, nn(ds, q), nn(pb, g), tn(pb, values), tn(ds, keys)))
            for i, rows, span, dk, dv, out, dq in done:
                grads[0, span, :] += dk
                grads[1, span, :] += dv
                outs[i][0][rows, cols] = own_heads(out).astype(BF)
                outs[i][1][rows, cols] = (own_heads(dq) * HD**-0.5).astype(BF)
        for n in range(2):
            kv_grads[n, :, cols] = grads[n].astype(BF)


def av_kernel(chips, win_ref, *refs):
    pieces = refs[:6]
    video = ((refs[6], refs[7]), (refs[8], refs[9]))
    stats, kv_grads = refs[10:15], refs[15]
    outs = ((refs[16], refs[17]), (refs[18], refs[19]))
    back = refs[20:26]
    audio, bias, grads, rowstat, qo_grads = refs[26:]
    c, r, _ = coords()
    quarter = audio.shape[2]
    block_bias(win_ref, None, bias)
    gather_audio(pieces, (0, 1), audio)

    @pl.loop(0, quarter // PAIR)
    def _(h):
        cols, wide_cols = pair_cols(h, quarter)
        for place, merged in zip(group_places(c), merge_stats(chips, *[ref[h] for ref in stats])):
            for n, x in enumerate(merged):
                wide = [jnp.broadcast_to(x[e : e + 1], (HD, PAIR)) for e in range(2)]
                rowstat[n, pl.ds(place * PAIR, PAIR), :] = jnp.concatenate(wide, axis=0).T
        grads[...] = jnp.zeros(grads.shape, F32)
        for group in block_groups(r):
            work = []
            for i, stretch, b in group:
                start, _ = window_of(win_ref, stretch, b)
                span = pl.ds(pl.multiple_of(start * BLK, BLK), WMAX * BLK)
                rows = slice(b * BLK, (b + 1) * BLK)
                keys = both_heads(video[i][0][rows, wide_cols])
                values = both_heads(video[i][1][rows, wide_cols])
                q, g = audio[0, span, cols], audio[1, span, cols]
                s = nt(q, keys) + bias[4 * i + b]
                dp = nt(g, values)
                work.append((i, rows, span, keys, values, q, g, s, dp))
            done = []
            for i, rows, span, keys, values, q, g, s, dp in work:
                p = jnp.exp(s - rowstat[0, span, :])
                pb = p.astype(BF)
                ds = (p * (dp - rowstat[1, span, :])).astype(BF)
                done.append((i, rows, span, nn(ds, keys), nn(pb, values), tn(ds, q), tn(pb, g)))
            for i, rows, span, dq, out, dk, dv in done:
                grads[0, span, :] += dq
                grads[1, span, :] += out
                outs[i][0][rows, cols] = own_heads(dk).astype(BF)
                outs[i][1][rows, cols] = own_heads(dv).astype(BF)
        qo_grads[0, :, cols] = (grads[0] * HD**-0.5).astype(BF)
        qo_grads[1, :, cols] = grads[1].astype(BF)

    scatter_audio((kv_grads, kv_grads, qo_grads, qo_grads), back)


def sum_kernel(mask, keep, by_aud, by_a, by_ax, by_b, by_bx, after, mine, other):
    _, r, a = coords()
    for slot, out in ((r, mine), (1 - r, other)):
        for part, parts in ((a, (keep, by_a, by_b)), (1 - a, (by_aud, by_ax, by_bx))):
            for n in range(4):
                x = sum(ref[n, slot].astype(F32) for ref in parts)
                if n == 3:
                    x = jnp.where(mask[slot] > 0.0, x, 0.0)
                out[n, part] = x.astype(BF)


def join_audio_kernel(mine, other, *outs):
    _, r, _ = coords()
    quarter = mine.shape[3]
    for n, out in enumerate(outs):
        for part in range(2):
            for core, ref in ((r, mine), (1 - r, other)):
                col = pl.multiple_of((2 * part + core) * quarter, 128)
                out[:, pl.ds(col, quarter)] = ref[n, part]


def join_video_kernel(*refs):
    _, r, _ = coords()
    quarter = refs[0].shape[1]
    for own, far, out in zip(refs[:4], refs[4:8], refs[8:12]):
        for core, src in ((r, own), (1 - r, far)):
            out[:, pl.ds(pl.multiple_of(core * quarter, PAIR), quarter)] = src[...]
    refs[12][...] = jnp.zeros(refs[12].shape, F32)


def cost(flops, transcendentals, nbytes):
    return pl.CostEstimate(flops=flops, transcendentals=transcendentals, bytes_accessed=nbytes)


def make_body(mesh):
    nv = mesh.shape["vid"]
    chips = nv // 2
    everyone = [(v, a) for v in range(nv) for a in range(2)]

    def perm(move):
        pairs = []
        for v, a in everyone:
            w, b = move(v, a)
            if 0 <= w < nv:
                pairs.append((2 * v + a, 2 * w + b))
        return pairs

    def diagonal(v):
        return 2 * ((((v >> 1) + 1) ^ 1) - 1) + (v & 1)

    moves = {
        "core": perm(lambda v, a: (v ^ 1, a)),
        "aud": perm(lambda v, a: (v, 1 - a)),
        "A": perm(lambda v, a: (v ^ 2, a)),
        "Ax": perm(lambda v, a: (v ^ 2, 1 - a)),
        "B": perm(lambda v, a: (diagonal(v), a)),
        "Bx": perm(lambda v, a: (diagonal(v), 1 - a)),
        "Q2": perm(lambda v, a: (v + 4 if v & 2 else v - 4, a)),
    }

    def move(x, name):
        return lax.ppermute(x, ("vid", "aud"), moves[name])

    def step(q_v, k_v, v_v, g_v, q_a, k_a, v_a, g_a, window, audio_len):
        rows, width = q_v.shape
        quarter = width // 2
        half = q_a.shape[0]
        steps = quarter // PAIR
        window = window.T
        shape = jax.ShapeDtypeStruct

        smem = pl.BlockSpec(memory_space=pltpu.SMEM)
        whole = pl.BlockSpec(memory_space=pltpu.VMEM)
        hbm = pl.BlockSpec(memory_space=pltpu.HBM)

        def call(kernel, name, ins, outs, args, scratch=(), est=None):
            params = dict(
                name=name,
                out_shape=[o for _, o in outs],
                cost_estimate=est,
                compiler_params=pltpu.CompilerParams(vmem_limit_bytes=24 << 20),
            )
            outs = [s for s, _ in outs]
            return pl.pallas_call(kernel, in_specs=ins, out_specs=outs, scratch_shapes=list(scratch), **params)(*args)

        audio = (q_a, g_a, k_a, v_a)
        audio_other = [move(x, "core") for x in audio]
        piece = shape((4, 2, half, quarter), BF)
        stack = shape((4, half, 2 * width), BF)
        (mine,) = call(
            load_kernel,
            "load",
            [hbm] * 4,
            [(whole, stack)],
            [pltpu.with_memory_space_constraint(x, pltpu.HBM) for x in audio],
            scratch=(pltpu.SemaphoreType.DMA((4,)),),
            est=cost(0, 0, 800000),
        )
        keep, send, mask = call(
            pack_kernel,
            "pack",
            [smem] + [whole] * 5,
            [(whole, piece)] * 2 + [(whole, shape((2, half, quarter), F32))],
            (audio_len, mine, *audio_other),
            est=cost(0, 0, 1600000),
        )
        pieces = [keep, move(send, "aud"), move(keep, "A"), move(send, "Ax")]
        pieces += [move(keep, "B"), move(send, "Bx")]
        k_f, v_f, q_f, g_f = [move(x, "core") for x in (k_v, v_v, q_v, g_v)]

        audio_scratch = pltpu.VMEM((2, KEYS, quarter), BF)
        grad_scratch = pltpu.VMEM((2, KEYS, PAIR), F32)
        bias_scratch = pltpu.VMEM((8, WMAX * BLK, PAIR), F32)
        pairs = 2 * steps * 2 * rows * KEYS

        stat = shape((steps, 8, 2 * PAIR), F32)

        def find_stats(groups, name, before):
            lanes = len(groups) * PAIR
            (found,) = call(
                lambda *refs: stats_kernel(groups, *refs),
                name,
                [smem] + [whole] * (2 * len(groups) + 4 + len(before)),
                [(whole, stat)],
                (window, *[pieces[2 * g + n] for g in groups for n in range(2)], k_v, v_v, k_f, v_f, *before),
                scratch=(pltpu.VMEM((2, lanes, quarter), BF), pltpu.VMEM((2, rows, lanes), F32)),
                est=cost(4 * HD * pairs * lanes // KEYS, pairs * lanes // KEYS, 2000000),
            )
            return found

        stats_a = find_stats((0, 1), "stats_a", ())
        by_a = move(stats_a, "A")
        stats_b = find_stats((2,), "stats_b", (stats_a, by_a))
        by_b, by_q2 = move(stats_b, "B"), move(stats_b, "Q2")

        full, part = shape((rows, width), BF), shape((rows, quarter), BF)
        out_own, dq_own, out_far, dq_far, kv_grads = call(
            va_kernel,
            "va",
            [smem, smem] + [whole] * 10,
            [(whole, part)] * 4 + [(whole, shape((2, KEYS, quarter), BF))],
            (window, audio_len, *pieces, *[pltpu.with_memory_space_constraint(x, pltpu.VMEM) for x in (q_v, g_v, q_f, g_f)]),
            scratch=(audio_scratch, bias_scratch, grad_scratch),
            est=cost(10 * HD * pairs, pairs, 5000000),
        )
        dk_own, dv_own, dk_far, dv_far, *back = call(
            lambda *refs: av_kernel(chips, *refs),
            "av",
            [smem] + [whole] * 16,
            [(whole, part)] * 4 + [(whole, piece)] * 6,
            (window, *pieces, k_v, v_v, k_f, v_f, stats_a, stats_b, by_a, by_b, by_q2, kv_grads),
            scratch=(audio_scratch, bias_scratch, grad_scratch, grad_scratch, audio_scratch),
            est=cost(12 * HD * pairs, pairs, 5000000),
        )
        parts = [back[0]] + [move(x, name) for x, name in zip(back[1:], ("aud", "A", "Ax", "B", "Bx"))]

        fars = [move(x, "core") for x in (out_far, dq_far, dk_far, dv_far)]
        out_video, dq_video, dk_video, dv_video, joined = call(
            join_video_kernel,
            "join_video",
            [whole] * 8,
            [(whole, full)] * 4 + [(whole, shape((8, PAIR), F32))],
            (out_own, dq_own, dk_own, dv_own, *fars),
            est=cost(0, 0, 1600000),
        )
        mine, other = call(
            sum_kernel, "sum_audio", [whole] * 8, [(whole, piece)] * 2, (mask, *parts, joined),
            est=cost(1000000, 0, 1600000),
        )
        other = move(other, "core")
        dk_audio, dv_audio, dq_audio, out_audio = call(
            join_audio_kernel,
            "join_audio",
            [whole] * 2,
            [(whole, shape((half, 2 * width), BF))] * 4,
            (mine, other),
            est=cost(0, 0, 800000),
        )
        return (out_video, out_audio, dq_video, dk_video, dv_video, dq_audio, dk_audio, dv_audio)

    return step


def solution(mesh):
    video, audio = P("vid", "aud"), P(("vid", "aud"), None)
    return jax.shard_map(
        make_body(mesh),
        mesh=mesh,
        in_specs=(video,) * 4 + (audio,) * 4 + (P(), P()),
        out_specs=(video, audio, video, video, video, audio, audio, audio),
        check_vma=False,
    )
```

```python
import functools

import jax
import jax.numpy as jnp
from jax import lax
from jax.experimental import pallas as pl
from jax.experimental.pallas import tpu as pltpu
from jax.sharding import PartitionSpec as P


HD = 64
BLK = 64
WMAX = 3
PAIR = 2 * HD
NEG = -1e30
BF = jnp.bfloat16
F32 = jnp.float32


NPOS = 6
KEYS = NPOS * BLK
GROUP = 8


def nt(x, y):
    return lax.dot_general(x, y, (((1,), (1,)), ((), ())), preferred_element_type=F32)


def nn(x, y):
    return lax.dot_general(x, y, (((1,), (0,)), ((), ())), preferred_element_type=F32)


def coords():
    vid, aud = lax.axis_index("vid"), lax.axis_index("aud")
    return vid >> 1, vid & 1, aud


def head_part(x, e):
    lane = lax.broadcasted_iota(jnp.int32, x.shape, 1)
    return jnp.where((lane < HD) if e == 0 else (lane >= HD), x, jnp.zeros_like(x))


def load_kernel(*refs):
    srcs, dst, sems = refs[:4], refs[4], refs[5]
    copies = [pltpu.make_async_copy(src, dst.at[n], sems.at[n]) for n, src in enumerate(srcs)]
    for copy in copies:
        copy.start()
    for copy in copies:
        copy.wait()


def pack_kernel(len_ref, mine, *refs):
    other, (keep, send, mask) = refs[:4], refs[4:]
    c, r, a = coords()
    half, quarter = keep.shape[2], keep.shape[3]
    row = lax.broadcasted_iota(jnp.int32, (half, quarter), 0) + a * half
    for slot, arrays in ((r, [mine.at[n] for n in range(4)]), (1 - r, other)):
        valid = row < len_ref[2 * c + slot]
        mask[slot] = jnp.where(valid, 1.0, 0.0)
        for n, ref in enumerate(arrays):

            def part(which, core):
                col = pl.multiple_of((2 * which + core) * quarter, 128)
                x = ref[:, pl.ds(col, quarter)]
                if n == 0:
                    x = x * jnp.asarray(HD**-0.5, BF)
                if n == 1:
                    x = jnp.where(valid, x, jnp.zeros_like(x))
                return x

            keep[n, slot] = part(a, r)
            send[n, slot] = part(1 - a, r)


def piece_rows():
    c, _, a = coords()
    half = BLK // 2
    side = 2 - 2 * (c & 1)
    starts = []
    for place, part in ((1, a), (1, 1 - a), (side, a), (side, 1 - a), (2 - side, a), (2 - side, 1 - a)):
        first = place * 2 * BLK + part * half
        starts.append([pl.multiple_of(first + core * BLK, half) for core in range(2)])
    return starts


def gather_audio(pieces, arrays, dst):
    half = BLK // 2
    for ref, firsts in zip(pieces, piece_rows()):
        for core, first in enumerate(firsts):
            for n, k in enumerate(arrays):
                dst[n, pl.ds(first, half), :] = ref[k, core]


def scatter_audio(sources, pieces):
    half = BLK // 2
    for ref, firsts in zip(pieces, piece_rows()):
        for core, first in enumerate(firsts):
            for n, src in enumerate(sources):
                ref[n, core] = src[n % 2, pl.ds(first, half), :]


def pair_cols(h, quarter):
    _, r, _ = coords()
    col = pl.multiple_of(h * PAIR, PAIR)
    return pl.ds(col, PAIR), pl.ds(pl.multiple_of(r * quarter + col, PAIR), PAIR)


def window_bounds(win_ref, c, stretch, shape, axis):
    block = lax.broadcasted_iota(jnp.int32, shape, axis) // BLK
    lo = jnp.zeros(shape, jnp.int32)
    hi = jnp.zeros(shape, jnp.int32)
    for b in range(4):
        start = win_ref[0, 8 * c + 4 * stretch + b] - (2 * c - 2)
        count = win_ref[1, 8 * c + 4 * stretch + b]
        lo = jnp.where(block == b, start, lo)
        hi = jnp.where(block == b, start + count, hi)
    return lo, hi


def window_of(win_ref, stretch, b):
    c, _, _ = coords()
    block = 8 * c + 4 * stretch + b
    return win_ref[0, block] - (2 * c - 2), win_ref[1, block]


def block_bias(win_ref, len_ref, bias):
    c, r, _ = coords()
    row = lax.broadcasted_iota(jnp.int32, bias.shape[1:], 0)
    for i, stretch in enumerate((r, 1 - r)):
        for b in range(4):
            start, count = window_of(win_ref, stretch, b)
            keep = row < count * BLK
            if len_ref is not None:
                length = jnp.zeros(row.shape, jnp.int32)
                for j in range(WMAX):
                    block = jnp.clip(2 * c - 2 + start + j, 0, len_ref.shape[0] - 1)
                    length = jnp.where(row // BLK == j, len_ref[block], length)
                keep = keep & (row % BLK < length)
            bias[4 * i + b] = jnp.where(keep, 0.0, NEG)


def both_heads(x):
    return jnp.concatenate([head_part(x, 0), head_part(x, 1)], axis=0)


def own_heads(x):
    lane = lax.broadcasted_iota(jnp.int32, (BLK, PAIR), 1)
    return jnp.where(lane < HD, x[:BLK], x[BLK:])


def block_groups(r):
    blocks = [(i, stretch, b) for b in range(4) for i, stretch in enumerate((r, 1 - r))]
    return [blocks[n : n + GROUP] for n in range(0, 8, GROUP)]


def tn(x, y):
    return lax.dot_general(x, y, (((0,), (0,)), ((), ())), preferred_element_type=F32)


def group_places(c):
    side = 2 - 2 * (c & 1)
    return 1, side, 2 - side


def group_bias(win_ref, groups, bias):
    c, r, _ = coords()
    places = group_places(c)
    shape = bias.shape[1:]
    lane = lax.broadcasted_iota(jnp.int32, shape, 1)
    place = jnp.zeros(shape, jnp.int32)
    for n, group in enumerate(groups):
        place = jnp.where(lane // PAIR == n, 2 * places[group], place)
    place = place + (lane % PAIR) // BLK
    for i, stretch in enumerate((r, 1 - r)):
        lo, hi = window_bounds(win_ref, c, stretch, shape, 0)
        bias[i] = jnp.where((place >= lo) & (place < hi), 0.0, NEG)


def pair_stats(x, y):
    m = jnp.maximum(x[0:2], y[0:2])
    wx, wy = jnp.exp(x[0:2] - m), jnp.exp(y[0:2] - m)
    total = wx + wy
    lse, delta = m + jnp.log(total), (wx * x[2:4] + wy * y[2:4]) / total
    return jnp.concatenate([lse, delta, lse, delta], axis=0)


def stats_kernel(groups, win_ref, *refs):
    count = len(groups)
    pieces, refs = refs[: 2 * count], refs[2 * count :]
    video, refs = ((refs[0], refs[1]), (refs[2], refs[3])), refs[4:]
    stat_ref, audio, bias = refs[-3:]
    _, _, a = coords()
    half, quarter = BLK // 2, audio.shape[2]
    group_bias(win_ref, groups, bias)
    for n in range(count):
        for ref, part in ((pieces[2 * n], a), (pieces[2 * n + 1], 1 - a)):
            for core in range(2):
                first = pl.multiple_of(n * PAIR + core * BLK + part * half, half)
                for k in range(2):
                    audio[k, pl.ds(first, half), :] = ref[k, core]

    @pl.loop(0, quarter // PAIR, unroll=True)
    def _(h):
        cols, wide_cols = pair_cols(h, quarter)
        queries, cot = audio[0, :, cols], audio[1, :, cols]
        work = []
        for e in range(2):
            s = [nt(head_part(k_ref[:, wide_cols], e), queries) + bias[i] for i, (k_ref, _) in enumerate(video)]
            work.append((s, [nt(head_part(v_ref[:, wide_cols], e), cot) for _, v_ref in video]))
        lses, deltas = [], []
        for s, dp in work:
            m = jnp.maximum(*[jnp.max(x, axis=0, keepdims=True) for x in s])
            ex = [jnp.exp(x - m) for x in s]
            total = sum(jnp.sum(x, axis=0, keepdims=True) for x in ex)
            lses.append(m + jnp.log(total))
            deltas.append(sum(jnp.sum(x * y, axis=0, keepdims=True) for x, y in zip(ex, dp)) / total)
        rows = jnp.concatenate(lses + deltas + lses + deltas, axis=0)
        if count == 1:
            rows = jnp.concatenate([pair_stats(refs[0][h][:, :PAIR], refs[1][h][:, PAIR:]), rows], axis=1)
        stat_ref[h] = rows


def merge_stats(chips, own_a, own_b, by_a, by_b, by_q2):
    c, _, _ = coords()
    even = (c & 1) == 0
    has_b = jnp.where(even, c >= 2, c + 2 < chips)
    has_q2 = jnp.where(even, c + 2 < chips, c >= 2)

    def part(x, k, there=None):
        x = x[:, k * PAIR : (k + 1) * PAIR]
        return (x[0:2] if there is None else jnp.where(there, x[0:2], NEG)), x[2:4]

    merged = []
    for group in (
        (part(own_a, 0), part(by_a, 1), part(by_b, 1, has_b)),
        (part(own_a, 1), part(by_a, 0), part(by_q2, 1, has_q2)),
        (part(own_b, 1), part(by_b, 0, has_b)),
    ):
        m = functools.reduce(jnp.maximum, [lse for lse, _ in group])
        ws = [jnp.exp(lse - m) for lse, _ in group]
        total = sum(ws)
        merged.append((m + jnp.log(total), sum(wt * d for wt, (_, d) in zip(ws, group)) / total))
    return merged


def va_kernel(win_ref, len_ref, *refs):
    pieces = refs[:6]
    video = ((refs[6], refs[7]), (refs[8], refs[9]))
    outs = ((refs[10], refs[11]), (refs[12].at[0], refs[12].at[1]))
    kv_grads, audio, bias, grads = refs[13:]
    _, r, _ = coords()
    quarter = audio.shape[2]
    block_bias(win_ref, len_ref, bias)
    gather_audio(pieces, (2, 3), audio)
    scale = jnp.asarray(HD**-0.5, BF)

    @pl.loop(0, quarter // PAIR)
    def _(h):
        cols, wide_cols = pair_cols(h, quarter)
        grads[...] = jnp.zeros(grads.shape, F32)
        for group in block_groups(r):
            work = []
            for i, stretch, b in group:
                start, _ = window_of(win_ref, stretch, b)
                span = pl.ds(pl.multiple_of(start * BLK, BLK), WMAX * BLK)
                rows = slice(b * BLK, (b + 1) * BLK)
                q = both_heads(video[i][0][rows, wide_cols] * scale)
                g = both_heads(video[i][1][rows, wide_cols])
                keys, values = audio[0, span, cols], audio[1, span, cols]
                s = nt(keys, q) + bias[4 * i + b]
                dp = nt(values, g)
                work.append((i, rows, span, q, g, keys, values, s, dp))
            done = []
            for i, rows, span, q, g, keys, values, s, dp in work:
                ex = jnp.exp(s - jnp.max(s, axis=0, keepdims=True))
                inv = 1.0 / jnp.sum(ex, axis=0, keepdims=True)
                delta = jnp.sum(ex * dp, axis=0, keepdims=True) * inv
                p = ex * inv
                pb = p.astype(BF)
                ds = (p * (dp - delta)).astype(BF)
                done.append((i, rows, span, nn(ds, q), nn(pb, g), tn(pb, values), tn(ds, keys)))
            for i, rows, span, dk, dv, out, dq in done:
                grads[0, span, :] += dk
                grads[1, span, :] += dv
                outs[i][0][rows, cols] = own_heads(out).astype(BF)
                outs[i][1][rows, cols] = (own_heads(dq) * HD**-0.5).astype(BF)
        for n in range(2):
            kv_grads[n, :, cols] = grads[n].astype(BF)


def av_kernel(chips, win_ref, *refs):
    pieces = refs[:6]
    video = ((refs[6], refs[7]), (refs[8], refs[9]))
    stats, kv_grads = refs[10:15], refs[15]
    outs = ((refs[16], refs[17]), (refs[18].at[0], refs[18].at[1]))
    back = refs[19:25]
    audio, bias, grads, rowstat, qo_grads = refs[25:]
    c, r, _ = coords()
    quarter = audio.shape[2]
    block_bias(win_ref, None, bias)
    gather_audio(pieces, (0, 1), audio)

    @pl.loop(0, quarter // PAIR)
    def _(h):
        cols, wide_cols = pair_cols(h, quarter)
        for place, merged in zip(group_places(c), merge_stats(chips, *[ref[h] for ref in stats])):
            for n, x in enumerate(merged):
                wide = [jnp.broadcast_to(x[e : e + 1], (HD, PAIR)) for e in range(2)]
                rowstat[n, pl.ds(place * PAIR, PAIR), :] = jnp.concatenate(wide, axis=0).T
        grads[...] = jnp.zeros(grads.shape, F32)
        for group in block_groups(r):
            work = []
            for i, stretch, b in group:
                start, _ = window_of(win_ref, stretch, b)
                span = pl.ds(pl.multiple_of(start * BLK, BLK), WMAX * BLK)
                rows = slice(b * BLK, (b + 1) * BLK)
                keys = both_heads(video[i][0][rows, wide_cols])
                values = both_heads(video[i][1][rows, wide_cols])
                q, g = audio[0, span, cols], audio[1, span, cols]
                s = nt(q, keys) + bias[4 * i + b]
                dp = nt(g, values)
                work.append((i, rows, span, keys, values, q, g, s, dp))
            done = []
            for i, rows, span, keys, values, q, g, s, dp in work:
                p = jnp.exp(s - rowstat[0, span, :])
                pb = p.astype(BF)
                ds = (p * (dp - rowstat[1, span, :])).astype(BF)
                done.append((i, rows, span, nn(ds, keys), nn(pb, values), tn(ds, q), tn(pb, g)))
            for i, rows, span, dq, out, dk, dv in done:
                grads[0, span, :] += dq
                grads[1, span, :] += out
                outs[i][0][rows, cols] = own_heads(dk).astype(BF)
                outs[i][1][rows, cols] = own_heads(dv).astype(BF)
        qo_grads[0, :, cols] = (grads[0] * HD**-0.5).astype(BF)
        qo_grads[1, :, cols] = grads[1].astype(BF)

    scatter_audio((kv_grads, kv_grads, qo_grads, qo_grads), back)


def sum_kernel(mask, keep, by_aud, by_a, by_ax, by_b, by_bx, after, mine, other):
    _, r, a = coords()
    for slot, out in ((r, mine), (1 - r, other)):
        for part, parts in ((a, (keep, by_a, by_b)), (1 - a, (by_aud, by_ax, by_bx))):
            for n in range(4):
                x = sum(ref[n, slot].astype(F32) for ref in parts)
                if n == 3:
                    x = jnp.where(mask[slot] > 0.0, x, 0.0)
                out[n, part] = x.astype(BF)


def join_audio_kernel(mine, other, *outs):
    _, r, _ = coords()
    quarter = mine.shape[3]
    for n, out in enumerate(outs):
        for part in range(2):
            for core, ref in ((r, mine), (1 - r, other)):
                col = pl.multiple_of((2 * part + core) * quarter, 128)
                out[:, pl.ds(col, quarter)] = ref[n, part]


def join_video_kernel(*refs):
    _, r, _ = coords()
    quarter = refs[0].shape[1]
    fars = [ref.at[n] for ref in refs[4:6] for n in range(2)]
    for own, far, out in zip(refs[:4], fars, refs[6:10]):
        for core, src in ((r, own), (1 - r, far)):
            out[:, pl.ds(pl.multiple_of(core * quarter, PAIR), quarter)] = src[...]
    refs[10][...] = jnp.zeros(refs[10].shape, F32)


def cost(flops, transcendentals, nbytes):
    return pl.CostEstimate(flops=flops, transcendentals=transcendentals, bytes_accessed=nbytes)


def make_body(mesh):
    nv = mesh.shape["vid"]
    chips = nv // 2
    everyone = [(v, a) for v in range(nv) for a in range(2)]

    def perm(move):
        pairs = []
        for v, a in everyone:
            w, b = move(v, a)
            if 0 <= w < nv:
                pairs.append((2 * v + a, 2 * w + b))
        return pairs

    def diagonal(v):
        return 2 * ((((v >> 1) + 1) ^ 1) - 1) + (v & 1)

    moves = {
        "core": perm(lambda v, a: (v ^ 1, a)),
        "aud": perm(lambda v, a: (v, 1 - a)),
        "A": perm(lambda v, a: (v ^ 2, a)),
        "Ax": perm(lambda v, a: (v ^ 2, 1 - a)),
        "B": perm(lambda v, a: (diagonal(v), a)),
        "Bx": perm(lambda v, a: (diagonal(v), 1 - a)),
        "Q2": perm(lambda v, a: (v + 4 if v & 2 else v - 4, a)),
    }

    def move(x, name):
        return lax.ppermute(x, ("vid", "aud"), moves[name])

    def step(q_v, k_v, v_v, g_v, q_a, k_a, v_a, g_a, window, audio_len):
        rows, width = q_v.shape
        quarter = width // 2
        half = q_a.shape[0]
        steps = quarter // PAIR
        window = window.T
        shape = jax.ShapeDtypeStruct

        smem = pl.BlockSpec(memory_space=pltpu.SMEM)
        whole = pl.BlockSpec(memory_space=pltpu.VMEM)
        hbm = pl.BlockSpec(memory_space=pltpu.HBM)

        def call(kernel, name, ins, outs, args, scratch=(), est=None):
            params = dict(
                name=name,
                out_shape=[o for _, o in outs],
                cost_estimate=est,
                compiler_params=pltpu.CompilerParams(vmem_limit_bytes=24 << 20),
            )
            outs = [s for s, _ in outs]
            return pl.pallas_call(kernel, in_specs=ins, out_specs=outs, scratch_shapes=list(scratch), **params)(*args)

        audio = (q_a, g_a, k_a, v_a)
        audio_other = [move(x, "core") for x in audio]
        piece = shape((4, 2, half, quarter), BF)
        stack = shape((4, half, 2 * width), BF)
        (mine,) = call(
            load_kernel,
            "load",
            [hbm] * 4,
            [(whole, stack)],
            [pltpu.with_memory_space_constraint(x, pltpu.HBM) for x in audio],
            scratch=(pltpu.SemaphoreType.DMA((4,)),),
            est=cost(0, 0, 800000),
        )
        keep, send, mask = call(
            pack_kernel,
            "pack",
            [smem] + [whole] * 5,
            [(whole, piece)] * 2 + [(whole, shape((2, half, quarter), F32))],
            (audio_len, mine, *audio_other),
            est=cost(0, 0, 1600000),
        )
        pieces = [keep, move(send, "aud"), move(keep, "A"), move(send, "Ax")]
        pieces += [move(keep, "B"), move(send, "Bx")]
        k_f, v_f, q_f, g_f = [move(x, "core") for x in (k_v, v_v, q_v, g_v)]

        audio_scratch = pltpu.VMEM((2, KEYS, quarter), BF)
        grad_scratch = pltpu.VMEM((2, KEYS, PAIR), F32)
        bias_scratch = pltpu.VMEM((8, WMAX * BLK, PAIR), F32)
        pairs = 2 * steps * 2 * rows * KEYS

        stat = shape((steps, 8, 2 * PAIR), F32)

        def find_stats(groups, name, before):
            lanes = len(groups) * PAIR
            (found,) = call(
                lambda *refs: stats_kernel(groups, *refs),
                name,
                [smem] + [whole] * (2 * len(groups) + 4 + len(before)),
                [(whole, stat)],
                (window, *[pieces[2 * g + n] for g in groups for n in range(2)], k_v, v_v, k_f, v_f, *before),
                scratch=(pltpu.VMEM((2, lanes, quarter), BF), pltpu.VMEM((2, rows, lanes), F32)),
                est=cost(4 * HD * pairs * lanes // KEYS, pairs * lanes // KEYS, 2000000),
            )
            return found

        stats_a = find_stats((0, 1), "stats_a", ())
        by_a = move(stats_a, "A")
        stats_b = find_stats((2,), "stats_b", (stats_a, by_a))
        by_b, by_q2 = move(stats_b, "B"), move(stats_b, "Q2")

        far = shape((2, rows, quarter), BF)
        full, part = shape((rows, width), BF), shape((rows, quarter), BF)
        out_own, dq_own, va_far, kv_grads = call(
            va_kernel,
            "va",
            [smem, smem] + [whole] * 10,
            [(whole, part)] * 2 + [(whole, far)] + [(whole, shape((2, KEYS, quarter), BF))],
            (window, audio_len, *pieces, *[pltpu.with_memory_space_constraint(x, pltpu.VMEM) for x in (q_v, g_v, q_f, g_f)]),
            scratch=(audio_scratch, bias_scratch, grad_scratch),
            est=cost(10 * HD * pairs, pairs, 5000000),
        )
        dk_own, dv_own, av_far, *back = call(
            lambda *refs: av_kernel(chips, *refs),
            "av",
            [smem] + [whole] * 16,
            [(whole, part)] * 2 + [(whole, far)] + [(whole, piece)] * 6,
            (window, *pieces, k_v, v_v, k_f, v_f, stats_a, stats_b, by_a, by_b, by_q2, kv_grads),
            scratch=(audio_scratch, bias_scratch, grad_scratch, grad_scratch, audio_scratch),
            est=cost(12 * HD * pairs, pairs, 5000000),
        )
        parts = [back[0]] + [move(x, name) for x, name in zip(back[1:], ("aud", "A", "Ax", "B", "Bx"))]

        fars = [move(x, "core") for x in (va_far, av_far)]
        out_video, dq_video, dk_video, dv_video, joined = call(
            join_video_kernel,
            "join_video",
            [whole] * 6,
            [(whole, full)] * 4 + [(whole, shape((8, PAIR), F32))],
            (out_own, dq_own, dk_own, dv_own, *fars),
            est=cost(0, 0, 1600000),
        )
        mine, other = call(
            sum_kernel, "sum_audio", [whole] * 8, [(whole, piece)] * 2, (mask, *parts, joined),
            est=cost(1000000, 0, 1600000),
        )
        other = move(other, "core")
        dk_audio, dv_audio, dq_audio, out_audio = call(
            join_audio_kernel,
            "join_audio",
            [whole] * 2,
            [(whole, shape((half, 2 * width), BF))] * 4,
            (mine, other),
            est=cost(0, 0, 800000),
        )
        return (out_video, out_audio, dq_video, dk_video, dv_video, dq_audio, dk_audio, dv_audio)

    return step


def solution(mesh):
    video, audio = P("vid", "aud"), P(("vid", "aud"), None)
    return jax.shard_map(
        make_body(mesh),
        mesh=mesh,
        in_specs=(video,) * 4 + (audio,) * 4 + (P(), P()),
        out_specs=(video, audio, video, video, video, audio, audio, audio),
        check_vma=False,
    )
```
